32 devices in a mesh: groups: 2 (over x), gz: 8 (over z, y), gy: 2 (over core).
Axes of the slice: x: 2, y: 2, z: 4, core: 2. Of those that a mesh axis runs over, the one named last changes fastest.
Arguments:
- momentum: float32 [3, 64, 64, 1024], P(None, ('groups', 'gz'), 'gy'), parts along dimension 1, may hold values from -4 to 4
- template: float32 [64, 64, 1024], P(('groups', 'gz'), 'gy'), parts along dimension 0, may hold values from -6 to 6
- target: float32 [64, 64, 1024], P(('groups', 'gz'), 'gy'), parts along dimension 0, may hold values from -6 to 6
Outputs:
- momentum_out: float32 [3, 64, 64, 1024], P(None, ('groups', 'gz'), 'gy'), parts along dimension 1
- deformed: float32 [64, 64, 1024], P(('groups', 'gz'), 'gy'), parts along dimension 0
- gradient: float32 [3, 64, 64, 1024], P(None, ('groups', 'gz'), 'gy'), parts along dimension 1
The draws below stay inside these ranges and needn't reach their ends.
There are 2 independent parts, one for each index of `groups`. The reference program is written for one: setup_inputs(seed, part) draws one part's arguments, and reference() takes and returns one part's arrays. A program takes and returns all parts, laid end to end along the dimension named above; each array names one. Nothing has to cross between parts.
All inputs are finite; a program needn't handle non-finite values.
Results may differ from the reference program's by a relative error of at most 0.00002.
Values sent between devices are 32-bit elements; how exact they have to be, the bound alone decides.
No kernel may reach another device: no remote copies, remote signals or barrier semaphores. Data moves between devices by JAX's collectives and lax.ppermute only.
A program may use at most 64 MiB of HBM per device.

```python
import jax
import jax.numpy as jnp
from jax import lax

NX = 1024
STEPS = 2
NZ = 32
NY = 64


def block_scale(key, extent, pieces, low, high):
    def one(position, blocks):
        heights = jax.random.uniform(jax.random.fold_in(jax.random.fold_in(key, 6), position), (blocks,), jnp.float32, low / len(pieces), high / len(pieces))
        return jnp.repeat(jnp.exp(heights), extent[position] // blocks).reshape((-1,) + (1,) * (len(extent) - position - 1))

    loudness = one(*pieces[0])
    for cut in pieces[1:]:
        loudness = loudness * one(*cut)
    return loudness


def centred(stream_key, dims, spread, bound, shards=(), held_as=jnp.bfloat16):
    gain = block_scale(stream_key, dims, shards, -0.22, 0.18) if shards else 1.0
    values = jax.random.normal(stream_key, dims, jnp.float32) * spread * gain
    return jnp.minimum(jnp.maximum(values, -bound), bound).astype(held_as)


def setup_inputs(seed: int = 0, part: int = 0) -> dict:
    seeds = jax.random.split(jax.random.key(seed), 4)
    part_keys = jax.random.split(jax.random.fold_in(seeds[3], part), 4)
    return {
        "momentum": centred(part_keys[0], (3, NZ, NY, NX), 1.0, 4.0, ((1, 8), (2, 2)), jnp.float32),
        "template": centred(part_keys[1], (NZ, NY, NX), 1.0, 6.0, ((0, 8), (1, 2)), jnp.float32),
        "target": centred(part_keys[2], (NZ, NY, NX), 1.0, 6.0, ((0, 8), (1, 2)), jnp.float32),
    }


TAPS = (0.05, 0.1, 0.2, 0.3, 0.2, 0.1, 0.05)
STEP_SIZE = 0.25


def taps_sum(padded, axis, length):
    total = jnp.zeros(padded.shape[:axis] + (length,) + padded.shape[axis + 1:], jnp.float32)
    for k in range(7):
        total = total + TAPS[k] * lax.slice_in_dim(padded, k, k + length, axis=axis)
    return total


def pad_axis(field, axis, width):
    widths = [(0, 0)] * field.ndim
    widths[axis] = (width, width)
    return jnp.pad(field, widths)


def smooth(field):
    for axis in (3, 2, 1):
        field = taps_sum(pad_axis(field, axis, 3), axis, field.shape[axis])
    return field


def pad_one(field):
    return jnp.pad(field, ((0, 0), (1, 1), (1, 1), (1, 1)))


def window(padded, axis, offset):
    out = padded
    for ax in (1, 2, 3):
        start = 1 + (offset if ax == axis else 0)
        out = lax.slice_in_dim(out, start, start + padded.shape[ax] - 2, axis=ax)
    return out


def advance(state_pad, velo_pad):
    state = window(state_pad, 0, 0)
    velo = window(velo_pad, 0, 0)
    advect = jnp.zeros_like(state)
    divergence = jnp.zeros_like(state[0])
    stretch = []
    for comp in range(3):
        axis = 3 - comp
        lower = window(state_pad, axis, -1)
        upper = window(state_pad, axis, 1)
        speed = velo[comp][None]
        advect = advect + jnp.maximum(speed, 0.0) * (state - lower) + jnp.minimum(speed, 0.0) * (upper - state)
        slope = 0.5 * (window(velo_pad, axis, 1) - window(velo_pad, axis, -1))
        divergence = divergence + slope[comp]
        stretch.append(state[0] * slope[0] + state[1] * slope[1] + state[2] * slope[2])
    moment = state[:3] - STEP_SIZE * (advect[:3] + jnp.stack(stretch) + state[:3] * divergence[None])
    image = state[3:] - STEP_SIZE * advect[3:]
    return jnp.concatenate([moment, image], axis=0)


def source(state, image_pad, target):
    residual_img = state[3] - target
    forces = []
    for comp in range(3):
        axis = 3 - comp
        slope = 0.5 * (window(image_pad, axis, 1) - window(image_pad, axis, -1))[0]
        forces.append(state[comp] - residual_img * slope)
    return jnp.stack(forces)


def reference(momentum, template, target):
    state = jnp.concatenate([momentum, template[None]], axis=0)
    for step in range(STEPS):
        velo = smooth(state[:3])
        state = advance(pad_one(state), pad_one(velo))
    image_pad = pad_one(state[3:])
    gradient = smooth(source(state, image_pad, target))
    return state[:3], state[3], gradient
```

```python
import functools

import jax
import jax.numpy as jnp
from jax import lax
from jax.experimental import pallas as pl
from jax.experimental.pallas import tpu as pltpu
from jax.sharding import PartitionSpec as P

LANES = 128
SUB = 8

UNIT = 0.05
SCALE = UNIT * UNIT * UNIT
STEP_SIZE = 0.25

AXES = ("gz", "gy")
VMEM = pl.BlockSpec(memory_space=pltpu.VMEM)
SMEM = pl.BlockSpec(memory_space=pltpu.SMEM)


def place(depth, half):
    return 4 * (depth // 2) + 2 * half + depth % 2


def swap_pairs(count):
    swapped = {1: 2, 2: 1}
    return [(i, 4 * (i // 4) + swapped.get(i % 4, i % 4)) for i in range(count)]


def up_pairs(count):
    return [(place(d, h), place(d + 1, h)) for h in range(2) for d in range(count // 2 - 1)]


def down_pairs(count):
    return [(b, a) for a, b in up_pairs(count)]


def tiled(cells):
    lead, (rows, width) = cells.shape[:-2], cells.shape[-2:]
    cells = cells.reshape(lead + (rows // SUB, SUB, width // LANES, LANES))
    cells = jnp.swapaxes(cells, -2, -3)
    return cells.reshape(lead + (rows * width // LANES, LANES))


def untiled(cells, rows):
    lead, (total, lanes) = cells.shape[:-2], cells.shape[-2:]
    cols = total // rows
    cells = cells.reshape(lead + (rows // SUB, cols, SUB, LANES))
    cells = jnp.swapaxes(cells, -2, -3)
    return cells.reshape(lead + (rows, cols * LANES))


class Line:
    def __init__(self, cols):
        self.cols = cols
        self.lane = lax.broadcasted_iota(jnp.int32, (cols, LANES), 1)
        self.sub = lax.broadcasted_iota(jnp.int32, (cols, LANES), 0)

    def after(self, row):
        return jnp.where(self.sub < self.cols - 1, pltpu.roll(row, self.cols - 1, 0), 0.0)

    def before(self, row):
        return jnp.where(self.sub > 0, pltpu.roll(row, 1, 0), 0.0)

    def ahead(self, row, nxt, k):
        return pltpu.roll(jnp.where(self.lane >= k, row, nxt), LANES - k, 1)

    def behind(self, row, prv, k):
        return pltpu.roll(jnp.where(self.lane < LANES - k, row, prv), k, 1)

    def near(self, row):
        return self.ahead(row, self.after(row), 1), self.behind(row, self.before(row), 1)

    def smooth(self, row):
        nxt, prv = self.after(row), self.before(row)
        one, two, three = (
            self.ahead(row, nxt, k) + self.behind(row, prv, k) for k in (1, 2, 3)
        )
        return 2.0 * (two + 2.0 * one + 3.0 * row) + three


def smooth_rows(line, load, store, count):
    last = line.smooth(load(0))
    pairs = last
    sums = {-2: None, -1: last}
    for r in range(1, count):
        here = line.smooth(load(r))
        nxt = last + here
        sums[r - 1] = pairs + nxt
        last, pairs = here, nxt
        done = r - 3
        if done >= 0:
            out = 3.0 * sums[done] + sums[done + 2]
            store(done, out if sums[done - 2] is None else out + sums[done - 2])
            del sums[done - 2]


def smooth_planes(planes):
    pairs = [a + b for a, b in zip(planes, planes[1:])]
    sums = [a + b for a, b in zip(pairs, pairs[1:])]
    return [
        SCALE * (3.0 * mid + (low + high)) for low, mid, high in zip(sums, sums[2:], sums[4:])
    ]


def spot(row, cols):
    return (row // SUB) * SUB * cols + row % SUB


def mirrored(row, rows, cols, flip):
    a, b = spot(row, cols), spot(rows - 1 - row, cols)
    return a + flip * (b - a)


def pack_kernel(extra, rows, flip_ref, m_ref, i_ref, t_ref, halo_ref, mo_ref, io_ref, to_ref):
    cols = mo_ref.shape[-2]
    planes = i_ref.shape[0]
    flip = flip_ref[0]
    halo_rows = halo_ref.shape[2] // cols
    sign = (1 - 2 * flip).astype(jnp.float32)

    def copy(src, halo, dst, count, factor):
        for r in range(count):
            if r < rows:
                at = mirrored(r, rows, cols, flip)
                row = src[pl.ds(at, cols, stride=SUB), :]
            else:
                at = mirrored(r - rows, halo_rows, cols, flip)
                row = halo[pl.ds(at, cols, stride=SUB), :]
            dst[r] = row if factor is None else row * factor

    def body(z, carry):
        for comp in range(3):
            copy(
                m_ref.at[comp, z], halo_ref.at[comp, z], mo_ref.at[comp, z], rows + extra[0],
                sign if comp == 1 else None,
            )
        copy(i_ref.at[z], halo_ref.at[3, z], io_ref.at[z], rows + extra[0], None)
        copy(t_ref.at[z], halo_ref.at[4, z], to_ref.at[z], rows + extra[1], None)
        return carry

    lax.fori_loop(0, planes, body, 0)


def velocity(line, edge_ref, lo_ref, own_ref, hi_ref, s_ref, v_ref, count):
    planes = own_ref.shape[1]

    for part, ref in enumerate((lo_ref, own_ref, hi_ref)):

        def body(n, carry, part=part, ref=ref):
            comp, z = n // planes, n % planes
            out = s_ref.at[comp, part * planes + z]

            def store(r, row):
                out[r] = row

            smooth_rows(line, lambda r: ref[comp, z, r], store, count)
            return carry

        lax.fori_loop(0, 3 * planes, body, 0)

    below, above = edge_ref[0], edge_ref[1]

    def rows(r, carry):
        for comp in range(3):
            out = smooth_planes([s_ref[comp, z, r] for z in range(3 * planes)][planes - 4 : 2 * planes + 4])
            out[0] = out[0] * below
            out[-1] = out[-1] * above
            for z, plane in enumerate(out):
                v_ref[comp, z, r] = plane
        return carry

    lax.fori_loop(0, count - 3, rows, 0)


def change(line, speed, f, around):
    total = None
    for (rise, fall), (upper, lower) in zip(speed, around):
        up = rise * (f - lower if lower is not None else f)
        down = fall * (upper - f)
        total = up + down if total is None else total + (up + down)
    return total


def stacked(lo_ref, own_ref, hi_ref):
    planes, low = own_ref.shape[0], lo_ref.shape[0]

    def load(z, r):
        if z < 0:
            return lo_ref[low + z, r]
        if z >= planes:
            return hi_ref[z - planes, r]
        return own_ref[z, r]

    return load


def advance(line, v_ref, momentum, image, z, r, first):
    velo = [v_ref[c, z + 1, r] for c in range(3)]
    speed = [(jnp.maximum(v, 0.0), jnp.minimum(v, 0.0)) for v in velo]

    def around(load):
        mid = load(z, r)
        return mid, [
            line.near(mid),
            (load(z, r + 1), None if first else load(z, r - 1)),
            (load(z + 1, r), load(z - 1, r)),
        ]

    new_image = None
    if image is not None:
        mid, sides = around(image)
        new_image = mid - STEP_SIZE * change(line, speed, mid, sides)
    if momentum is None:
        return None, new_image

    slopes = []
    for comp in range(3):
        ahead, behind = line.near(velo[comp])
        slopes.append(
            (
                ahead - behind,
                v_ref[comp, z + 1, r + 1] - (0.0 if first else v_ref[comp, z + 1, r - 1]),
                v_ref[comp, z + 2, r] - v_ref[comp, z, r],
            )
        )
    divergence = slopes[0][0] + slopes[1][1] + slopes[2][2]
    fields = [around(load) for load in momentum]
    mids = [mid for mid, _ in fields]
    new = []
    for comp in range(3):
        mid, sides = fields[comp]
        stretch = mid * divergence
        for other in range(3):
            stretch = stretch + mids[other] * slopes[other][comp]
        moved = change(line, speed, mid, sides)
        new.append(mid - (STEP_SIZE * moved + (0.5 * STEP_SIZE) * stretch))
    return new, new_image


def over_rows(body, start, stop):
    if start == 0:
        body(0, True)
        start = 1

    def step(r, carry):
        body(r, False)
        return carry

    lax.fori_loop(start, stop, step, 0)


def first_kernel(edge_ref, mlo_ref, m_ref, mhi_ref, ilo_ref, i_ref, ihi_ref, mo_ref, io_ref, s_ref, v_ref):
    line = Line(m_ref.shape[-2])
    planes, count = m_ref.shape[1:3]
    velocity(line, edge_ref, mlo_ref, m_ref, mhi_ref, s_ref, v_ref, count)
    momentum = [stacked(mlo_ref.at[c], m_ref.at[c], mhi_ref.at[c]) for c in range(3)]
    image = stacked(ilo_ref, i_ref, ihi_ref)

    def body(r, first):
        for z in range(planes):
            new, img = advance(line, v_ref, momentum, image, z, r, first)
            for c in range(3):
                mo_ref[c, z, r] = new[c]
            io_ref[z, r] = img

    over_rows(body, 0, count - 4)


def second_kernel(
    rows, edge_ref, flip_ref, mlo_ref, m_ref, mhi_ref, ilo_ref, i_ref, ihi_ref, t_ref,
    mout_ref, iout_ref, so_ref, s_ref, v_ref, m2_ref, i2_ref, q_ref,
):
    line = Line(m_ref.shape[-2])
    cols = line.cols
    planes, count = m_ref.shape[1:3]
    velocity(line, edge_ref, mlo_ref, m_ref, mhi_ref, s_ref, v_ref, count)
    momentum = [stacked(mlo_ref.at[c], m_ref.at[c], mhi_ref.at[c]) for c in range(3)]
    image = stacked(ilo_ref, i_ref, ihi_ref)
    flip = flip_ref[0]
    sign = (1 - 2 * flip).astype(jnp.float32)

    def native(r):
        r = jnp.int32(r)
        r = r + flip * (rows - 1 - 2 * r)
        return (r // SUB) * (SUB * cols) + r % SUB

    def step(kept, r, first):
        at = native(r) if kept else None
        for z in range(planes):
            new, img = advance(line, v_ref, momentum, image, z, r, first)
            for c in range(3):
                m2_ref[c, z, r] = new[c]
                if kept:
                    mout_ref[c, z, pl.ds(at, cols, stride=SUB), :] = new[c] * sign if c == 1 else new[c]
            i2_ref[z + 1, r] = img
            if kept:
                iout_ref[z, pl.ds(at, cols, stride=SUB), :] = img
        for z in (-1, planes):
            i2_ref[z + 1, r] = advance(line, v_ref, None, image, z, r, first)[1]

    over_rows(functools.partial(step, True), 0, rows)
    over_rows(functools.partial(step, False), rows, count - 4)
    for z in range(planes):
        i2_ref[z + 1, count - 4] = advance(line, v_ref, None, image, z, count - 4, False)[1]

    def force(r, first):
        for z in range(planes):
            img = i2_ref[z + 1, r]
            half = 0.5 * (img - t_ref[z, r])
            ahead, behind = line.near(img)
            slopes = (
                ahead - behind,
                i2_ref[z + 1, r + 1] - (0.0 if first else i2_ref[z + 1, r - 1]),
                i2_ref[z + 2, r] - i2_ref[z, r],
            )
            for c in range(3):
                q_ref[c, z, r] = m2_ref[c, z, r] - half * slopes[c]

    over_rows(force, 0, count - 4)

    def body(n, carry):
        comp, z = n // planes, n % planes

        def store(r, row):
            so_ref[comp, z, r] = row

        smooth_rows(line, lambda r: q_ref[comp, z, r], store, count - 4)
        return carry

    lax.fori_loop(0, 3 * planes, body, 0)


def last_kernel(flip_ref, lo_ref, s_ref, hi_ref, out_ref):
    planes, rows, cols = s_ref.shape[1:4]
    flip = flip_ref[0]
    sign = (1 - 2 * flip).astype(jnp.float32)

    def body(r, carry):
        at = r + flip * (rows - 1 - 2 * r)
        at = (at // SUB) * (SUB * cols) + at % SUB
        for c in range(3):
            stack = [lo_ref[c, z, r] for z in range(3)]
            stack += [s_ref[c, z, r] for z in range(planes)]
            stack += [hi_ref[c, z, r] for z in range(3)]
            for z, plane in enumerate(smooth_planes(stack)):
                out_ref[c, z, pl.ds(at, cols, stride=SUB), :] = plane * sign if c == 1 else plane
        return carry

    lax.fori_loop(0, rows, body, 0)


def call(kernel, specs, outs, scratch=(), flops=0):
    return pl.pallas_call(
        kernel,
        in_specs=specs,
        out_specs=[VMEM] * len(outs),
        out_shape=[jax.ShapeDtypeStruct(o, jnp.float32) for o in outs],
        scratch_shapes=[pltpu.VMEM(s, jnp.float32) for s in scratch],
    )


def on_device(momentum, template, target):
    planes, rows, width = template.shape
    cols = width // LANES
    halves = lax.axis_size("gy")
    count = lax.axis_size("gz") * halves
    flat = lax.axis_index("gz") * halves + lax.axis_index("gy")
    depth, half = 2 * (flat // 4) + flat % 2, (flat // 2) % 2
    edge = jnp.stack([depth > 0, depth < count // 2 - 1]).astype(jnp.float32)
    flip = half.reshape(1)
    flip_here = lax.axis_index("gy").reshape(1)

    mom, img, tgt = tiled(momentum), tiled(template), tiled(target)
    near = 2 * SUB
    edge_rows = near * cols

    def border(cells):
        return jnp.where(
            lax.axis_index("gy") == 0, cells[..., -edge_rows:, :], cells[..., :edge_rows, :]
        )

    halo = lax.ppermute(
        jnp.concatenate([border(mom), border(img)[None], border(tgt)[None]]),
        "gy",
        [(0, 1), (1, 0)],
    )
    extra = 3 * 4 - 1
    reach = rows + extra
    tail = (cols, LANES)
    m0, i0, t0 = call(
        functools.partial(pack_kernel, (extra, 3), rows),
        [SMEM, VMEM, VMEM, VMEM, VMEM],
        [(3, planes, reach) + tail, (planes, reach) + tail, (planes, rows + 3) + tail],
    )(flip_here, mom, img, tgt, halo)

    swap = swap_pairs(count)
    up, down = up_pairs(count), down_pairs(count)

    def send(cells, pairs):
        return lax.ppermute(cells, AXES, pairs)

    m0 = send(m0, swap)
    i0 = send(i0, swap)
    t0 = send(t0, swap)

    def scratch(size):
        return [(3, 3 * planes, size - 3) + tail, (3, planes + 2, size - 3) + tail]

    size = reach
    m1, i1 = call(
        first_kernel,
        [SMEM] + [VMEM] * 6,
        [(3, planes, size - 4) + tail, (planes, size - 4) + tail],
        scratch(size),
    )(
        edge,
        send(m0, up), m0, send(m0, down),
        send(i0[-1:], up), i0, send(i0[:1], down),
    )

    size = reach - 4
    m2, i2, sq = call(
        functools.partial(second_kernel, rows),
        [SMEM, SMEM] + [VMEM] * 7,
        [(3, planes, rows * cols, LANES), (planes, rows * cols, LANES), (3, planes, rows) + tail],
        scratch(size)
        + [
            (3, planes, size - 4) + tail,
            (planes + 2, size - 3) + tail,
            (3, planes, size - 4) + tail,
        ],
    )(
        edge, flip,
        send(m1, up), m1, send(m1, down),
        send(i1[-2:], up), i1, send(i1[:2], down),
        t0,
    )
    m2 = send(m2, swap)
    i2 = send(i2, swap)

    (grad,) = call(last_kernel, [SMEM] + [VMEM] * 3, [(3, planes, rows * cols, LANES)])(
        flip, send(sq[:, -3:], up), sq, send(sq[:, :3], down)
    )
    grad = send(grad, swap)
    return untiled(m2, rows), untiled(i2, rows), untiled(grad, rows)


def solution(mesh):
    return jax.shard_map(
        on_device,
        mesh=mesh,
        in_specs=(
            P(None, ("groups", "gz"), "gy", None),
            P(("groups", "gz"), "gy", None),
            P(("groups", "gz"), "gy", None),
        ),
        out_specs=(
            P(None, ("groups", "gz"), "gy", None),
            P(("groups", "gz"), "gy", None),
            P(None, ("groups", "gz"), "gy", None),
        ),
        check_vma=False,
    )
```

```python
import functools

import jax
import jax.numpy as jnp
from jax import lax
from jax.experimental import pallas as pl
from jax.experimental.pallas import tpu as pltpu
from jax.sharding import PartitionSpec as P

LANES = 128
SUB = 8

UNIT = 0.05
SCALE = UNIT * UNIT * UNIT
STEP_SIZE = 0.25

AXES = ("gz", "gy")
VMEM = pl.BlockSpec(memory_space=pltpu.VMEM)
SMEM = pl.BlockSpec(memory_space=pltpu.SMEM)


def place(depth, half):
    return 4 * (depth // 2) + 2 * half + depth % 2


def swap_pairs(count):
    swapped = {1: 2, 2: 1}
    return [(i, 4 * (i // 4) + swapped.get(i % 4, i % 4)) for i in range(count)]


def up_pairs(count):
    return [(place(d, h), place(d + 1, h)) for h in range(2) for d in range(count // 2 - 1)]


def down_pairs(count):
    return [(b, a) for a, b in up_pairs(count)]


def tiled(cells):
    lead, (rows, width) = cells.shape[:-2], cells.shape[-2:]
    cells = cells.reshape(lead + (rows // SUB, SUB, width // LANES, LANES))
    cells = jnp.swapaxes(cells, -2, -3)
    return cells.reshape(lead + (rows * width // LANES, LANES))


def untiled(cells, rows):
    lead, (total, lanes) = cells.shape[:-2], cells.shape[-2:]
    cols = total // rows
    cells = cells.reshape(lead + (rows // SUB, cols, SUB, LANES))
    cells = jnp.swapaxes(cells, -2, -3)
    return cells.reshape(lead + (rows, cols * LANES))


class Line:
    def __init__(self, cols):
        self.cols = cols
        self.lane = lax.broadcasted_iota(jnp.int32, (cols, LANES), 1)
        self.sub = lax.broadcasted_iota(jnp.int32, (cols, LANES), 0)

    def after(self, row):
        return jnp.where(self.sub < self.cols - 1, pltpu.roll(row, self.cols - 1, 0), 0.0)

    def before(self, row):
        return jnp.where(self.sub > 0, pltpu.roll(row, 1, 0), 0.0)

    def ahead(self, row, nxt, k):
        return pltpu.roll(jnp.where(self.lane >= k, row, nxt), LANES - k, 1)

    def behind(self, row, prv, k):
        return pltpu.roll(jnp.where(self.lane < LANES - k, row, prv), k, 1)

    def near(self, row):
        return self.ahead(row, self.after(row), 1), self.behind(row, self.before(row), 1)

    def smooth(self, row):
        first, last = self.sub == 0, self.sub == self.cols - 1
        one = pltpu.roll(row, LANES - 1, 1)
        one = jnp.where(
            self.lane == LANES - 1, jnp.where(last, 0.0, pltpu.roll(one, self.cols - 1, 0)), one
        )
        pair = row + one
        prev = pltpu.roll(pair, 1, 1)
        prev = jnp.where(self.lane == 0, jnp.where(first, row, pltpu.roll(prev, 1, 0)), prev)
        mid = prev + pair
        high = pltpu.roll(mid, LANES - 2, 1)
        high = jnp.where(
            self.lane >= LANES - 2, jnp.where(last, one, pltpu.roll(high, self.cols - 1, 0)), high
        )
        low = pltpu.roll(mid, 2, 1)
        low = jnp.where(
            self.lane < 2, jnp.where(first, prev - row, pltpu.roll(low, 1, 0)), low
        )
        return 3.0 * mid + (low + high)


def smooth_rows(line, load, store, count, top):
    last = line.smooth(load(0))
    pairs = last if top else None
    sums = {-2: None, -1: last if top else None}
    for r in range(1, count):
        here = line.smooth(load(r))
        nxt = last + here
        sums[r - 1] = None if pairs is None else pairs + nxt
        last, pairs = here, nxt
        done = r - 3
        if done >= (0 if top else 3):
            out = 3.0 * sums[done] + sums[done + 2]
            store(done, out if sums[done - 2] is None else out + sums[done - 2])


def smooth_planes(planes):
    pairs = [a + b for a, b in zip(planes, planes[1:])]
    sums = [a + b for a, b in zip(pairs, pairs[1:])]
    return [
        SCALE * (3.0 * mid + (low + high)) for low, mid, high in zip(sums, sums[2:], sums[4:])
    ]


def spot(row, cols):
    return (row // SUB) * SUB * cols + row % SUB


def mirrored(row, rows, cols, flip):
    a, b = spot(row, cols), spot(rows - 1 - row, cols)
    return a + flip * (b - a)


def pack_kernel(first, stop, rows, with_target, flip_ref, m_ref, i_ref, *refs):
    if with_target:
        t_ref, halo_ref, out_ref, tout_ref = refs
    else:
        (out_ref,) = refs
        t_ref = halo_ref = None
    cols = out_ref.shape[-2]
    planes = i_ref.shape[0]
    flip = flip_ref[0]
    sign = (1 - 2 * flip).astype(jnp.float32)

    def copy(src, halo, dst, start, end, factor):
        for r in range(start, end):
            if r < rows:
                row = src[pl.ds(mirrored(r, rows, cols, flip), cols, stride=SUB), :]
            else:
                at = mirrored(r - rows, halo.shape[0] // cols, cols, flip)
                row = halo[pl.ds(at, cols, stride=SUB), :]
            dst[r - start] = row if factor is None else row * factor

    def halo_at(n, z):
        return None if halo_ref is None else halo_ref.at[n, z]

    def body(z, carry):
        for comp in range(3):
            copy(
                m_ref.at[comp, z], halo_at(comp, z), out_ref.at[2 + comp * planes + z], first, stop,
                sign if comp == 1 else None,
            )
        spare = jnp.where(z < 2, 3 * planes + 2 + z, z - (planes - 2))
        copy(i_ref.at[z], halo_at(3, z), out_ref.at[spare], first, stop, None)
        if with_target:
            copy(t_ref.at[z], halo_at(4, z), tout_ref.at[z], 0, rows + 3, None)
        return carry

    lax.fori_loop(0, planes, body, 0)


def unpack_kernel(counts, parts, flip_ref, *refs):
    ins, outs = refs[: len(counts)], refs[len(counts) :]
    rows = sum(counts)
    flip = flip_ref[0]
    sign = (1 - 2 * flip).astype(jnp.float32)
    cols = ins[0].shape[-2]

    for out, (offset, components) in zip(outs, parts):
        planes = out.shape[-3]
        for comp in range(components):
            dst = out.at[comp] if len(out.shape) == 4 else out

            def body(z, carry, comp=comp, dst=dst, offset=offset, planes=planes):
                done = 0
                for ref, count in zip(ins, counts):
                    for r in range(count):
                        row = ref[offset + comp * planes + z, r]
                        at = mirrored(done + r, rows, cols, flip)
                        dst[z, pl.ds(at, cols, stride=SUB), :] = row * sign if comp == 1 else row
                    done += count
                return carry

            lax.fori_loop(0, planes, body, 0)


def fetch(parts, buf, sems, at):
    copies, row = [], 0
    for ref, start in parts:
        count = ref.shape[1] - start
        copies.append(
            pltpu.make_async_copy(
                ref.at[:, pl.ds(start, count)], buf.at[:, pl.ds(row, count)], sems.at[at + len(copies)]
            )
        )
        row += count
    for copy in copies:
        copy.start()
    return copies


def wait(copies):
    for copy in copies:
        copy.wait()


def velocity(line, edge_ref, blocks, s_ref, v_ref, top):
    count = s_ref.shape[2]
    planes = v_ref.shape[1] - 2
    start = 0 if top else 3

    for part in (1, 0, 2):
        copies, ref, offset = blocks[part]
        wait(copies)

        def body(n, carry, part=part, ref=ref, offset=offset):
            out = s_ref.at[part * 3 * planes + n]

            def store(r, row):
                out[r] = row

            smooth_rows(line, lambda r: ref[offset + n, r], store, s_ref.shape[1], top)
            return carry

        lax.fori_loop(0, 3 * planes, body, 0)

    below, above = edge_ref[0], edge_ref[1]

    def rows(r, carry):
        for comp in range(3):
            stack = [s_ref[part * 3 * planes + comp * planes + z, r] for part in range(3) for z in range(planes)]
            out = smooth_planes(stack[planes - 4 : 2 * planes + 4])
            out[0] = out[0] * below
            out[-1] = out[-1] * above
            for z, plane in enumerate(out):
                v_ref[comp, z, r] = plane
        return carry

    lax.fori_loop(start, s_ref.shape[1] - 3, rows, 0)


def change(line, speed, f, around):
    total = None
    for (rise, fall), (upper, lower) in zip(speed, around):
        up = rise * (f - lower if lower is not None else f)
        down = fall * (upper - f)
        total = up + down if total is None else total + (up + down)
    return total


def advance(line, v_ref, momentum, image, z, r, first):
    velo = [v_ref[c, z + 1, r] for c in range(3)]
    speed = [(jnp.maximum(v, 0.0), jnp.minimum(v, 0.0)) for v in velo]

    def around(load):
        mid = load(z, r)
        return mid, [
            line.near(mid),
            (load(z, r + 1), None if first else load(z, r - 1)),
            (load(z + 1, r), load(z - 1, r)),
        ]

    new_image = None
    if image is not None:
        mid, sides = around(image)
        new_image = mid - STEP_SIZE * change(line, speed, mid, sides)
    if momentum is None:
        return None, new_image

    slopes = []
    for comp in range(3):
        ahead, behind = line.near(velo[comp])
        slopes.append(
            (
                ahead - behind,
                v_ref[comp, z + 1, r + 1] - (0.0 if first else v_ref[comp, z + 1, r - 1]),
                v_ref[comp, z + 2, r] - v_ref[comp, z, r],
            )
        )
    divergence = slopes[0][0] + slopes[1][1] + slopes[2][2]
    fields = [around(load) for load in momentum]
    mids = [mid for mid, _ in fields]
    new = []
    for comp in range(3):
        mid, sides = fields[comp]
        stretch = mid * divergence
        for other in range(3):
            stretch = stretch + mids[other] * slopes[other][comp]
        moved = change(line, speed, mid, sides)
        new.append(mid - (STEP_SIZE * moved + (0.5 * STEP_SIZE) * stretch))
    return new, new_image


def over_rows(body, start, stop, top):
    if top and start == 0:
        body(0, True)
        start = 1

    def step(r, carry):
        body(r, False)
        return carry

    lax.fori_loop(start, stop, step, 0)


def momentum_at(own, lo, hi, offsets, planes):
    def at(comp):
        def load(z, r):
            if z < 0:
                return lo[offsets[0] + comp * planes + planes + z, r]
            if z >= planes:
                return hi[offsets[2] + comp * planes + z - planes, r]
            return own[offsets[1] + comp * planes + z, r]

        return load

    return [at(comp) for comp in range(3)]


def first_kernel(chunks, planes, edge_ref, *refs):
    top = chunks == 1
    ins, (up_ref, down_ref), scratch = refs[: 3 * chunks], refs[3 * chunks :][:2], refs[3 * chunks + 2 :]
    own, lo, hi, s_ref, v_ref, sems = scratch
    overlap = 8
    copies = []
    for n, buf in enumerate((own, lo, hi)):
        parts = [(ref, 0) for ref in ins[n * chunks : (n + 1) * chunks]]
        if not top:
            parts[0] = (parts[0][0], parts[0][0].shape[1] - overlap)
        copies.append(fetch(parts, buf, sems, n * chunks))
    line = Line(own.shape[-2])
    velocity(line, edge_ref, [(copies[1], lo, 1), (copies[0], own, 2), (copies[2], hi, 0)], s_ref, v_ref, top)
    momentum = momentum_at(own, lo, hi, (1, 2, 0), planes)

    def image(z, r):
        if z < 0:
            return lo[0, r]
        if z >= planes:
            return hi[3 * planes, r]
        return own[3 * planes + 2 + z, r] if z < 2 else own[z - (planes - 2), r]

    start = 0 if top else 4

    def body(r, first):
        for z in range(planes):
            new, img = advance(line, v_ref, momentum, image, z, r, first)
            for c in range(3):
                up_ref[2 + c * planes + z, r - start] = new[c]
                down_ref[c * planes + z, r - start] = new[c]
            if z < 2:
                down_ref[3 * planes + z, r - start] = img
            else:
                up_ref[z - (planes - 2), r - start] = img

    over_rows(body, start, own.shape[1] - 4, top)


def second_kernel(chunks, planes, rows, edge_ref, t_ref, *refs):
    top = chunks == 1
    start, stop, t_start, given = rows
    ins, refs = refs[: 4 * chunks], refs[4 * chunks :]
    if top:
        (out_ref, squp_ref, sqdown_ref, tail_ref), scratch = refs[:4], refs[4:]
        before_ref = None
    else:
        before_ref = refs[0]
        (out_ref, squp_ref, sqdown_ref), scratch = refs[1:4], refs[4:]
    own, down, lo, hi, s_ref, v_ref, i2_ref, q_ref, t_buf, sems = scratch
    overlap = 8
    copies = []
    for n, buf in enumerate((own, down, lo, hi)):
        parts = [(ref, 0) for ref in ins[n * chunks : (n + 1) * chunks]]
        if not top:
            parts[0] = (parts[0][0], parts[0][0].shape[1] - overlap)
        if n == 1:
            parts = [(ref.at[pl.ds(3 * planes, 2)], at) for ref, at in parts]
        copies.append(fetch(parts, buf, sems, n * chunks))
    last = 4 * chunks
    t_copy = pltpu.make_async_copy(t_ref.at[:, pl.ds(t_start, t_buf.shape[1])], t_buf, sems.at[last])
    t_copy.start()
    lead = 0 if top else 6
    if not top:
        q_copy = pltpu.make_async_copy(before_ref, q_ref.at[:, pl.ds(0, lead)], sems.at[last + 1])
        q_copy.start()
    line = Line(own.shape[-2])
    velocity(line, edge_ref, [(copies[2], lo, 2), (copies[0], own, 2), (copies[3], hi, 0)], s_ref, v_ref, top)
    momentum = momentum_at(own, lo, hi, (2, 2, 0), planes)
    wait(copies[1])

    def image(z, r):
        if z < 0:
            return lo[2 + z, r]
        if z >= planes:
            return hi[3 * planes + z - planes, r]
        return down[z, r] if z < 2 else own[z - (planes - 2), r]

    def step(keep, r, first):
        for z in range(planes):
            new, img = advance(line, v_ref, momentum, image, z, r, first)
            for c in range(3):
                q_ref[c * planes + z, r - start + lead] = new[c]
                if keep:
                    out_ref[c * planes + z, r - start] = new[c]
            i2_ref[z + 1, r] = img
            if keep:
                out_ref[3 * planes + z, r - start] = img
        for z in (-1, planes):
            i2_ref[z + 1, r] = advance(line, v_ref, None, image, z, r, first)[1]

    if not top:
        for z in range(planes):
            i2_ref[z + 1, start - 1] = advance(line, v_ref, None, image, z, start - 1, False)[1]
    over_rows(functools.partial(step, True), start, start + given, top)
    if start + given < stop:
        over_rows(functools.partial(step, False), start + given, stop, top)
    for z in range(planes):
        i2_ref[z + 1, stop] = advance(line, v_ref, None, image, z, stop, False)[1]
    t_copy.wait()
    if not top:
        q_copy.wait()

    def force(r, first):
        for z in range(planes):
            img = i2_ref[z + 1, r]
            half = 0.5 * (img - t_buf[z, r - start])
            ahead, behind = line.near(img)
            slopes = (
                ahead - behind,
                i2_ref[z + 1, r + 1] - (0.0 if first else i2_ref[z + 1, r - 1]),
                i2_ref[z + 2, r] - i2_ref[z, r],
            )
            for c in range(3):
                at = c * planes + z
                q_ref[at, r - start + lead] = q_ref[at, r - start + lead] - half * slopes[c]

    over_rows(force, start, stop, top)
    size = q_ref.shape[1]
    if top:
        for n in range(3 * planes):
            for r in range(6):
                tail_ref[n, r] = q_ref[n, size - 6 + r]

    for z in range(planes):

        def body(c, carry, z=z):
            n = c * planes + z

            def store(r, row):
                r = r if top else r - 3
                if z > 0:
                    squp_ref[c * (planes - 1) + z - 1, r] = row
                if z < planes - 1:
                    sqdown_ref[c * (planes - 1) + z, r] = row

            smooth_rows(line, lambda r: q_ref[n, r], store, size, top)
            return carry

        lax.fori_loop(0, 3, body, 0)


def last_kernel(planes, up_ref, down_ref, lo_ref, hi_ref, out_ref):
    near = planes - 1

    def body(r, carry):
        for c in range(3):
            stack = [lo_ref[c * near + near - 3 + z, r] for z in range(3)]
            stack += [down_ref[c * near + z, r] for z in range(near)]
            stack += [up_ref[c * near + near - 1, r]]
            stack += [hi_ref[c * near + z, r] for z in range(3)]
            for z, plane in enumerate(smooth_planes(stack)):
                out_ref[c * planes + z, r] = plane
        return carry

    lax.fori_loop(0, up_ref.shape[1], body, 0)


ANY = pl.BlockSpec(memory_space=pl.ANY)


def call(kernel, specs, outs, scratch=(), copies=0, cost=0.0, name=None):
    return pl.pallas_call(
        kernel,
        name=name,
        in_specs=specs,
        out_specs=[VMEM] * len(outs),
        out_shape=[jax.ShapeDtypeStruct(o, jnp.float32) for o in outs],
        scratch_shapes=[pltpu.VMEM(s, jnp.float32) for s in scratch]
        + ([pltpu.SemaphoreType.DMA((copies,))] if copies else []),
        cost_estimate=pl.CostEstimate(flops=0, transcendentals=0, bytes_accessed=int(cost * 3.3e6)),
    )


def on_device(momentum, template, target):
    planes, rows, width = template.shape
    cols = width // LANES
    halves = lax.axis_size("gy")
    count = lax.axis_size("gz") * halves
    flat = lax.axis_index("gz") * halves + lax.axis_index("gy")
    depth = 2 * (flat // 4) + flat % 2
    edge = jnp.stack([depth > 0, depth < count // 2 - 1]).astype(jnp.float32)
    flip = lax.axis_index("gy").reshape(1)
    swap, up, down = swap_pairs(count), up_pairs(count), down_pairs(count)
    tail = (cols, LANES)
    all_planes = 4 * planes
    mplanes = 3 * planes

    def send(cells, pairs):
        return lax.ppermute(cells, AXES, pairs)

    mom, img, tgt = tiled(momentum), tiled(template), tiled(target)
    near = 2 * SUB
    edge_rows = near * cols

    def border(cells):
        return jnp.where(
            lax.axis_index("gy") == 0, cells[..., -edge_rows:, :], cells[..., :edge_rows, :]
        )

    reach = 4 + 4 + 3
    total = [rows + reach, rows + reach - 4, rows + reach - 8, rows]
    cut = [3 * rows // 4]
    cut += [cut[0] - 4, cut[0] - 8, cut[0] - 11]

    halo = lax.ppermute(
        jnp.concatenate([border(mom), border(img)[None], border(tgt)[None]]), "gy", [(0, 1), (1, 0)]
    )
    (a0,) = call(
        functools.partial(pack_kernel, 0, cut[0], rows, False),
        [SMEM, VMEM, VMEM],
        [(all_planes, cut[0]) + tail],
        cost=2.5, name="pack_a",
    )(flip, mom, img)
    a0 = send(a0, swap)
    b0, t0 = call(
        functools.partial(pack_kernel, cut[0], total[0], rows, True),
        [SMEM] + [VMEM] * 4,
        [(all_planes, total[0] - cut[0]) + tail, (planes, total[2]) + tail],
        cost=3, name="pack_b",
    )(flip, mom, img, tgt, halo)
    b0 = send(b0, swap)
    t0 = send(t0, swap)

    def exchange(chunk):
        return (
            chunk,
            send(chunk[1 : 2 + mplanes], up),
            send(chunk[2 : 3 + mplanes], down),
        )

    z_a, z_b = exchange(a0), exchange(b0)

    def first(chunks, parts, size):
        give = size - 4 - (0 if chunks == 1 else 4)
        return call(
            functools.partial(first_kernel, chunks, planes),
            [SMEM] + [ANY] * (3 * chunks),
            [(mplanes + 2, give) + tail] * 2,
            [(all_planes, size) + tail] + [(mplanes + 1, size) + tail] * 2
            + [(3 * mplanes, size) + tail, (3, planes + 2, size) + tail],
            copies=3 * chunks, cost=9, name=f"first_{chunks}",
        )(edge, *parts)

    up_a, down_a = first(1, z_a, cut[0])
    lo_a, hi_a = send(up_a, up), send(down_a, down)
    up_b, down_b = first(
        2, [part for pair in zip(z_a, z_b) for part in pair], total[0] - cut[0] + 8
    )
    lo_b, hi_b = send(up_b, up), send(down_b, down)

    def second(chunks, parts, size, given, sq_rows, t_start, before):
        start = 0 if chunks == 1 else 4
        stop = size - 4
        lead = 0 if chunks == 1 else 6
        outs = [(all_planes, given) + tail] + [(3 * (planes - 1), sq_rows) + tail] * 2
        if chunks == 1:
            outs.append((mplanes, 6) + tail)
        return call(
            functools.partial(second_kernel, chunks, planes, (start, stop, t_start, given)),
            [SMEM, ANY] + [ANY] * (4 * chunks + len(before)),
            outs,
            [(mplanes + 2, size) + tail, (2, size) + tail, (mplanes + 2, size) + tail, (mplanes + 2, size) + tail]
            + [(3 * mplanes, size) + tail, (3, planes + 2, size) + tail]
            + [(planes + 2, size) + tail, (mplanes, lead + stop - start) + tail, (planes, stop - start) + tail],
            copies=4 * chunks + 2, cost=11, name=f"second_{chunks}",
        )(edge, t0, *parts, *before)

    out_a, squp_a, sqdown_a, q_tail = second(
        1, (up_a, down_a, lo_a, hi_a), cut[1], cut[2], cut[3], 0, ()
    )
    out_a = send(out_a, swap)
    sqlo_a, sqhi_a = send(squp_a, up), send(sqdown_a, down)
    out_b, squp_b, sqdown_b = second(
        2, (up_a, up_b, down_a, down_b, lo_a, lo_b, hi_a, hi_b), total[1] - cut[1] + 8,
        rows - cut[2], rows - cut[3], cut[2], (q_tail,),
    )
    out_b = send(out_b, swap)
    sqlo_b, sqhi_b = send(squp_b, up), send(sqdown_b, down)

    def last(parts, name):
        return call(
            functools.partial(last_kernel, planes), [VMEM] * 4, [(mplanes, parts[0].shape[1]) + tail],
            cost=2, name=name,
        )(*parts)[0]

    g_a = send(last((squp_a, sqdown_a, sqlo_a, sqhi_a), "last_a"), swap)
    g_b = send(last((squp_b, sqdown_b, sqlo_b, sqhi_b), "last_b"), swap)

    native = (rows * cols, LANES)
    m2, i2 = call(
        functools.partial(unpack_kernel, (cut[2], rows - cut[2]), ((0, 3), (mplanes, 1))),
        [SMEM, VMEM, VMEM], [(3, planes) + native, (planes,) + native], cost=2, name="unpack_m",
    )(flip, out_a, out_b)
    (grad,) = call(
        functools.partial(unpack_kernel, (cut[3], rows - cut[3]), ((0, 3),)),
        [SMEM, VMEM, VMEM], [(3, planes) + native], cost=2, name="unpack_g",
    )(flip, g_a, g_b)
    return untiled(m2, rows), untiled(i2, rows), untiled(grad, rows)


def solution(mesh):
    return jax.shard_map(
        on_device,
        mesh=mesh,
        in_specs=(
            P(None, ("groups", "gz"), "gy", None),
            P(("groups", "gz"), "gy", None),
            P(("groups", "gz"), "gy", None),
        ),
        out_specs=(
            P(None, ("groups", "gz"), "gy", None),
            P(("groups", "gz"), "gy", None),
            P(None, ("groups", "gz"), "gy", None),
        ),
        check_vma=False,
    )
```

```python
import functools

import jax
import jax.numpy as jnp
from jax import lax
from jax.experimental import pallas as pl
from jax.experimental.pallas import tpu as pltpu
from jax.sharding import PartitionSpec as P

LANES = 128
SUB = 8

UNIT = 0.05
SCALE = UNIT * UNIT * UNIT
STEP_SIZE = 0.25
UNROLL = (4, 2, 1)

AXES = ("gz", "gy")
VMEM = pl.BlockSpec(memory_space=pltpu.VMEM)
SMEM = pl.BlockSpec(memory_space=pltpu.SMEM)


def place(depth, half):
    return 4 * (depth // 2) + 2 * half + depth % 2


def swap_pairs(count):
    swapped = {1: 2, 2: 1}
    return [(i, 4 * (i // 4) + swapped.get(i % 4, i % 4)) for i in range(count)]


def up_pairs(count):
    return [(place(d, h), place(d + 1, h)) for h in range(2) for d in range(count // 2 - 1)]


def down_pairs(count):
    return [(b, a) for a, b in up_pairs(count)]


def tiled(cells):
    lead, (rows, width) = cells.shape[:-2], cells.shape[-2:]
    cells = cells.reshape(lead + (rows // SUB, SUB, width // LANES, LANES))
    cells = jnp.swapaxes(cells, -2, -3)
    return cells.reshape(lead + (rows * width // LANES, LANES))


def untiled(cells, rows):
    lead, (total, lanes) = cells.shape[:-2], cells.shape[-2:]
    cols = total // rows
    cells = cells.reshape(lead + (rows // SUB, cols, SUB, LANES))
    cells = jnp.swapaxes(cells, -2, -3)
    return cells.reshape(lead + (rows, cols * LANES))


class Line:
    def __init__(self, cols):
        self.cols = cols
        lane = lax.broadcasted_iota(jnp.int32, (cols, LANES), 1)
        sub = lax.broadcasted_iota(jnp.int32, (cols, LANES), 0)
        self.first, self.last = sub == 0, sub == cols - 1
        self.at_start, self.near_start = lane == 0, lane < 2
        self.at_end, self.near_end = lane == LANES - 1, lane >= LANES - 2

    def beside(self, row):
        ahead = pltpu.roll(row, LANES - 1, 1)
        ahead = jnp.where(
            self.at_end, jnp.where(self.last, 0.0, pltpu.roll(ahead, self.cols - 1, 0)), ahead
        )
        behind = pltpu.roll(row, 1, 1)
        behind = jnp.where(
            self.at_start, jnp.where(self.first, 0.0, pltpu.roll(behind, 1, 0)), behind
        )
        return ahead, behind

    def smooth(self, row):
        ahead, behind = self.beside(row)
        mid = (ahead + behind) + (row + row)
        high = pltpu.roll(mid, LANES - 2, 1)
        high = jnp.where(
            self.near_end, jnp.where(self.last, ahead, pltpu.roll(high, self.cols - 1, 0)), high
        )
        low = pltpu.roll(mid, 2, 1)
        low = jnp.where(
            self.near_start, jnp.where(self.first, behind, pltpu.roll(low, 1, 0)), low
        )
        return 3.0 * mid + (low + high)


def smooth_rows(line, load, store, count, top):
    last = line.smooth(load(0))
    pairs = last if top else None
    sums = {-2: None, -1: last if top else None}
    for r in range(1, count):
        here = line.smooth(load(r))
        nxt = last + here
        sums[r - 1] = None if pairs is None else pairs + nxt
        last, pairs = here, nxt
        done = r - 3
        if done >= (0 if top else 3):
            out = 3.0 * sums[done] + sums[done + 2]
            store(done, out if sums[done - 2] is None else out + sums[done - 2])


def smooth_planes(planes, scale=SCALE):
    pairs = [a + b for a, b in zip(planes, planes[1:])]
    sums = [a + b for a, b in zip(pairs, pairs[1:])]
    out = [3.0 * mid + (low + high) for low, mid, high in zip(sums, sums[2:], sums[4:])]
    return out if scale == 1.0 else [scale * row for row in out]


def spot(row, cols):
    return (row // SUB) * SUB * cols + row % SUB


def mirrored(row, rows, cols, flip):
    a, b = spot(row, cols), spot(rows - 1 - row, cols)
    return a + flip * (b - a)


def pack_kernel(first, stop, rows, with_target, flip_ref, m_ref, i_ref, *refs):
    if with_target:
        t_ref, halo_ref, out_ref, tout_ref = refs
    else:
        (out_ref,) = refs
        t_ref = halo_ref = None
    cols = out_ref.shape[-2]
    planes = i_ref.shape[0]
    flip = flip_ref[0]
    sign = (1 - 2 * flip).astype(jnp.float32)

    def copy(src, halo, dst, start, end, factor):
        for r in range(start, end):
            if r < rows:
                row = src[pl.ds(mirrored(r, rows, cols, flip), cols, stride=SUB), :]
            else:
                at = mirrored(r - rows, halo.shape[0] // cols, cols, flip)
                row = halo[pl.ds(at, cols, stride=SUB), :]
            dst[r - start] = row if factor is None else row * factor

    def halo_at(n, z):
        return None if halo_ref is None else halo_ref.at[n, z]

    def body(z, carry):
        for comp in range(3):
            copy(
                m_ref.at[comp, z], halo_at(comp, z), out_ref.at[2 + comp * planes + z], first, stop,
                sign if comp == 1 else None,
            )
        spare = jnp.where(z < 2, 3 * planes + 2 + z, z - (planes - 2))
        copy(i_ref.at[z], halo_at(3, z), out_ref.at[spare], first, stop, None)
        if with_target:
            copy(t_ref.at[z], halo_at(4, z), tout_ref.at[z], 0, rows + 3, None)
        return carry

    lax.fori_loop(0, planes, body, 0)


def unpack_kernel(counts, parts, flip_ref, *refs):
    ins, outs = refs[: len(counts)], refs[len(counts) :]
    rows = sum(counts)
    flip = flip_ref[0]
    sign = (1 - 2 * flip).astype(jnp.float32)
    cols = ins[0].shape[-2]

    for out, (offset, components) in zip(outs, parts):
        planes = out.shape[-3]
        for comp in range(components):
            dst = out.at[comp] if len(out.shape) == 4 else out

            def body(z, carry, comp=comp, dst=dst, offset=offset, planes=planes):
                done = 0
                for ref, count in zip(ins, counts):
                    for r in range(count):
                        row = ref[offset + comp * planes + z, r]
                        at = mirrored(done + r, rows, cols, flip)
                        dst[z, pl.ds(at, cols, stride=SUB), :] = row * sign if comp == 1 else row
                    done += count
                return carry

            lax.fori_loop(0, planes, body, 0)


def fetch(parts, buf, sems, at):
    copies, row = [], 0
    for ref, start in parts:
        count = ref.shape[1] - start
        copies.append(
            pltpu.make_async_copy(
                ref.at[:, pl.ds(start, count)], buf.at[:, pl.ds(row, count)], sems.at[at + len(copies)]
            )
        )
        row += count
    for copy in copies:
        copy.start()
    return copies


def wait(copies):
    for copy in copies:
        copy.wait()


def velocity(line, edge_ref, blocks, s_ref, v_ref, top):
    planes = v_ref.shape[1] - 2
    count = blocks[0][1].shape[1]
    for copies, _, _ in blocks:
        wait(copies)
    zero = jnp.zeros(v_ref.shape[-2:], jnp.float32)

    for comp in range(3):
        def rows(r, carry, comp=comp):
            last, pairs = carry
            stack = [ref[offset + comp * planes + z, r] for _, ref, offset in blocks for z in range(planes)]
            here = smooth_planes(stack[planes - 4 : 2 * planes + 4], 1.0)
            nxt = [a + b for a, b in zip(last, here)]
            for z in range(planes + 2):
                s_ref[comp, z, r + 1] = pairs[z] + nxt[z]
            return here, nxt

        empty = [zero] * (planes + 2)
        lax.fori_loop(0, count, rows, (empty, empty), unroll=UNROLL[0])
        if top:
            for z in range(planes + 2):
                s_ref[comp, z, 0] = zero

    scales = [SCALE * edge_ref[0]] + [SCALE] * planes + [SCALE * edge_ref[1]]

    def finish(r, carry):
        for comp in range(3):
            for z in range(planes + 2):
                row = 3.0 * s_ref[comp, z, r + 2] + (s_ref[comp, z, r] + s_ref[comp, z, r + 4])
                v_ref[comp, z, r] = scales[z] * line.smooth(row)
        return carry

    lax.fori_loop(0 if top else 3, count - 3, finish, 0, unroll=UNROLL[1])


def change(speed, f, around):
    total = None
    for (rise, fall), (upper, lower) in zip(speed, around):
        up = rise * (f - lower if lower is not None else f)
        down = fall * (upper - f)
        total = up + down if total is None else total + (up + down)
    return total


def advance(line, v_ref, momentum, image, z, r, first):
    velo = [v_ref[c, z + 1, r] for c in range(3)]
    speed = [(jnp.maximum(v, 0.0), jnp.minimum(v, 0.0)) for v in velo]

    def around(load):
        mid = load(z, r)
        return mid, [
            line.beside(mid),
            (load(z, r + 1), None if first else load(z, r - 1)),
            (load(z + 1, r), load(z - 1, r)),
        ]

    new_image = None
    if image is not None:
        mid, sides = around(image)
        new_image = mid - STEP_SIZE * change(speed, mid, sides)
    if momentum is None:
        return None, new_image

    slopes = []
    for comp in range(3):
        ahead, behind = line.beside(velo[comp])
        slopes.append(
            (
                ahead - behind,
                v_ref[comp, z + 1, r + 1] - (0.0 if first else v_ref[comp, z + 1, r - 1]),
                v_ref[comp, z + 2, r] - v_ref[comp, z, r],
            )
        )
    divergence = slopes[0][0] + slopes[1][1] + slopes[2][2]
    fields = [around(load) for load in momentum]
    mids = [mid for mid, _ in fields]
    new = []
    for comp in range(3):
        mid, sides = fields[comp]
        stretch = mid * divergence
        for other in range(3):
            stretch = stretch + mids[other] * slopes[other][comp]
        moved = change(speed, mid, sides)
        new.append(mid - (STEP_SIZE * moved + (0.5 * STEP_SIZE) * stretch))
    return new, new_image


def over_rows(body, start, stop, top):
    if top and start == 0:
        body(0, True)
        start = 1

    def step(r, carry):
        body(r, False)
        return carry

    lax.fori_loop(start, stop, step, 0, unroll=UNROLL[2])


def momentum_at(own, lo, hi, offsets, planes):
    def at(comp):
        def load(z, r):
            if z < 0:
                return lo[offsets[0] + comp * planes + planes + z, r]
            if z >= planes:
                return hi[offsets[2] + comp * planes + z - planes, r]
            return own[offsets[1] + comp * planes + z, r]

        return load

    return [at(comp) for comp in range(3)]


def first_kernel(chunks, planes, edge_ref, *refs):
    top = chunks == 1
    ins, (up_ref, down_ref), scratch = refs[: 3 * chunks], refs[3 * chunks :][:2], refs[3 * chunks + 2 :]
    own, lo, hi, s_ref, v_ref, sems = scratch
    overlap = 8
    copies = []
    for n, buf in enumerate((own, lo, hi)):
        parts = [(ref, 0) for ref in ins[n * chunks : (n + 1) * chunks]]
        if not top:
            parts[0] = (parts[0][0], parts[0][0].shape[1] - overlap)
        copies.append(fetch(parts, buf, sems, n * chunks))
    line = Line(own.shape[-2])
    velocity(line, edge_ref, [(copies[1], lo, 1), (copies[0], own, 2), (copies[2], hi, 0)], s_ref, v_ref, top)
    momentum = momentum_at(own, lo, hi, (1, 2, 0), planes)

    def image(z, r):
        if z < 0:
            return lo[0, r]
        if z >= planes:
            return hi[3 * planes, r]
        return own[3 * planes + 2 + z, r] if z < 2 else own[z - (planes - 2), r]

    start = 0 if top else 4

    def body(r, first):
        for z in range(planes):
            new, img = advance(line, v_ref, momentum, image, z, r, first)
            for c in range(3):
                up_ref[2 + c * planes + z, r - start] = new[c]
                down_ref[c * planes + z, r - start] = new[c]
            if z < 2:
                down_ref[3 * planes + z, r - start] = img
            else:
                up_ref[z - (planes - 2), r - start] = img

    over_rows(body, start, own.shape[1] - 4, top)


def second_kernel(chunks, planes, rows, edge_ref, t_ref, *refs):
    top = chunks == 1
    start, stop, t_start, given = rows
    ins, refs = refs[: 4 * chunks], refs[4 * chunks :]
    if top:
        (out_ref, squp_ref, sqdown_ref, tail_ref), scratch = refs[:4], refs[4:]
        before_ref = None
    else:
        before_ref = refs[0]
        (out_ref, squp_ref, sqdown_ref), scratch = refs[1:4], refs[4:]
    own, down, lo, hi, s_ref, v_ref, i2_ref, q_ref, t_buf, sems = scratch
    overlap = 8
    copies = []
    for n, buf in enumerate((own, down, lo, hi)):
        parts = [(ref, 0) for ref in ins[n * chunks : (n + 1) * chunks]]
        if not top:
            parts[0] = (parts[0][0], parts[0][0].shape[1] - overlap)
        if n == 1:
            parts = [(ref.at[pl.ds(3 * planes, 2)], at) for ref, at in parts]
        copies.append(fetch(parts, buf, sems, n * chunks))
    last = 4 * chunks
    t_copy = pltpu.make_async_copy(t_ref.at[:, pl.ds(t_start, t_buf.shape[1])], t_buf, sems.at[last])
    t_copy.start()
    lead = 0 if top else 6
    if not top:
        q_copy = pltpu.make_async_copy(before_ref, q_ref.at[:, pl.ds(0, lead)], sems.at[last + 1])
        q_copy.start()
    line = Line(own.shape[-2])
    velocity(line, edge_ref, [(copies[2], lo, 2), (copies[0], own, 2), (copies[3], hi, 0)], s_ref, v_ref, top)
    momentum = momentum_at(own, lo, hi, (2, 2, 0), planes)
    wait(copies[1])

    def image(z, r):
        if z < 0:
            return lo[2 + z, r]
        if z >= planes:
            return hi[3 * planes + z - planes, r]
        return down[z, r] if z < 2 else own[z - (planes - 2), r]

    def step(keep, r, first):
        for z in range(planes):
            new, img = advance(line, v_ref, momentum, image, z, r, first)
            for c in range(3):
                q_ref[c * planes + z, r - start + lead] = new[c]
                if keep:
                    out_ref[c * planes + z, r - start] = new[c]
            i2_ref[z + 1, r] = img
            if keep:
                out_ref[3 * planes + z, r - start] = img
        for z in (-1, planes):
            i2_ref[z + 1, r] = advance(line, v_ref, None, image, z, r, first)[1]

    if not top:
        for z in range(planes):
            i2_ref[z + 1, start - 1] = advance(line, v_ref, None, image, z, start - 1, False)[1]
    over_rows(functools.partial(step, True), start, start + given, top)
    if start + given < stop:
        over_rows(functools.partial(step, False), start + given, stop, top)
    for z in range(planes):
        i2_ref[z + 1, stop] = advance(line, v_ref, None, image, z, stop, False)[1]
    t_copy.wait()
    if not top:
        q_copy.wait()

    def force(r, first):
        for z in range(planes):
            img = i2_ref[z + 1, r]
            half = 0.5 * (img - t_buf[z, r - start])
            ahead, behind = line.beside(img)
            slopes = (
                ahead - behind,
                i2_ref[z + 1, r + 1] - (0.0 if first else i2_ref[z + 1, r - 1]),
                i2_ref[z + 2, r] - i2_ref[z, r],
            )
            for c in range(3):
                at = c * planes + z
                q_ref[at, r - start + lead] = q_ref[at, r - start + lead] - half * slopes[c]

    over_rows(force, start, stop, top)
    size = q_ref.shape[1]
    if top:
        for n in range(3 * planes):
            for r in range(6):
                tail_ref[n, r] = q_ref[n, size - 6 + r]

    for z in range(planes):

        def body(c, carry, z=z):
            n = c * planes + z

            def store(r, row):
                r = r if top else r - 3
                if z > 0:
                    squp_ref[c * (planes - 1) + z - 1, r] = row
                if z < planes - 1:
                    sqdown_ref[c * (planes - 1) + z, r] = row

            smooth_rows(line, lambda r: q_ref[n, r], store, size, top)
            return carry

        lax.fori_loop(0, 3, body, 0)


def last_kernel(planes, up_ref, down_ref, lo_ref, hi_ref, out_ref):
    near = planes - 1

    def body(r, carry):
        for c in range(3):
            stack = [lo_ref[c * near + near - 3 + z, r] for z in range(3)]
            stack += [down_ref[c * near + z, r] for z in range(near)]
            stack += [up_ref[c * near + near - 1, r]]
            stack += [hi_ref[c * near + z, r] for z in range(3)]
            for z, plane in enumerate(smooth_planes(stack)):
                out_ref[c * planes + z, r] = plane
        return carry

    lax.fori_loop(0, up_ref.shape[1], body, 0)


ANY = pl.BlockSpec(memory_space=pl.ANY)


def call(kernel, specs, outs, scratch=(), copies=0, cost=0.0):
    return pl.pallas_call(
        kernel,
        in_specs=specs,
        out_specs=[VMEM] * len(outs),
        out_shape=[jax.ShapeDtypeStruct(o, jnp.float32) for o in outs],
        scratch_shapes=[pltpu.VMEM(s, jnp.float32) for s in scratch]
        + ([pltpu.SemaphoreType.DMA((copies,))] if copies else []),
        cost_estimate=pl.CostEstimate(flops=0, transcendentals=0, bytes_accessed=int(cost * 3.3e6)),
    )


def shoot(momentum, template, target):
    planes, rows, width = template.shape
    cols = width // LANES
    halves = lax.axis_size("gy")
    count = lax.axis_size("gz") * halves
    flat = lax.axis_index("gz") * halves + lax.axis_index("gy")
    depth = 2 * (flat // 4) + flat % 2
    edge = jnp.stack([depth > 0, depth < count // 2 - 1]).astype(jnp.float32)
    flip = lax.axis_index("gy").reshape(1)
    swap, up, down = swap_pairs(count), up_pairs(count), down_pairs(count)
    tail = (cols, LANES)
    all_planes = 4 * planes
    mplanes = 3 * planes

    def send(cells, pairs):
        return lax.ppermute(cells, AXES, pairs)

    mom, img, tgt = tiled(momentum), tiled(template), tiled(target)
    near = 2 * SUB
    edge_rows = near * cols

    def border(cells):
        return jnp.where(
            lax.axis_index("gy") == 0, cells[..., -edge_rows:, :], cells[..., :edge_rows, :]
        )

    reach = 4 + 4 + 3
    total = [rows + reach, rows + reach - 4, rows + reach - 8, rows]
    cut = [3 * rows // 4]
    cut += [cut[0] - 4, cut[0] - 8, cut[0] - 11]

    halo = lax.ppermute(
        jnp.concatenate([border(mom), border(img)[None], border(tgt)[None]]), "gy", [(0, 1), (1, 0)]
    )
    (a0,) = call(
        functools.partial(pack_kernel, 0, cut[0], rows, False),
        [SMEM, VMEM, VMEM],
        [(all_planes, cut[0]) + tail],
        cost=2.5,
    )(flip, mom, img)
    a0 = send(a0, swap)
    b0, t0 = call(
        functools.partial(pack_kernel, cut[0], total[0], rows, True),
        [SMEM] + [VMEM] * 4,
        [(all_planes, total[0] - cut[0]) + tail, (planes, total[2]) + tail],
        cost=3,
    )(flip, mom, img, tgt, halo)
    b0 = send(b0, swap)
    t0 = send(t0, swap)

    def exchange(chunk):
        return (chunk, send(chunk[1 : 2 + mplanes], up), send(chunk[2 : 3 + mplanes], down))

    z_a, z_b = exchange(a0), exchange(b0)

    def first(chunks, parts, size):
        give = size - 4 - (0 if chunks == 1 else 4)
        return call(
            functools.partial(first_kernel, chunks, planes),
            [SMEM] + [ANY] * (3 * chunks),
            [(mplanes + 2, give) + tail] * 2,
            [(all_planes, size) + tail] + [(mplanes + 1, size) + tail] * 2
            + [(3, planes + 2, size + 1) + tail, (3, planes + 2, size) + tail],
            copies=3 * chunks, cost=9,
        )(edge, *parts)

    up_a, down_a = first(1, z_a, cut[0])
    lo_a, hi_a = send(up_a, up), send(down_a, down)
    up_b, down_b = first(
        2, [part for pair in zip(z_a, z_b) for part in pair], total[0] - cut[0] + 8
    )
    lo_b, hi_b = send(up_b, up), send(down_b, down)

    def second(chunks, parts, size, given, sq_rows, t_start, before):
        start = 0 if chunks == 1 else 4
        stop = size - 4
        lead = 0 if chunks == 1 else 6
        outs = [(all_planes, given) + tail] + [(3 * (planes - 1), sq_rows) + tail] * 2
        if chunks == 1:
            outs.append((mplanes, 6) + tail)
        return call(
            functools.partial(second_kernel, chunks, planes, (start, stop, t_start, given)),
            [SMEM, ANY] + [ANY] * (4 * chunks + len(before)),
            outs,
            [(mplanes + 2, size) + tail, (2, size) + tail, (mplanes + 2, size) + tail, (mplanes + 2, size) + tail]
            + [(3, planes + 2, size + 1) + tail, (3, planes + 2, size) + tail]
            + [(planes + 2, size) + tail, (mplanes, lead + stop - start) + tail, (planes, stop - start) + tail],
            copies=4 * chunks + 2, cost=11,
        )(edge, t0, *parts, *before)

    out_a, squp_a, sqdown_a, q_tail = second(
        1, (up_a, down_a, lo_a, hi_a), cut[1], cut[2], cut[3], 0, ()
    )
    out_a = send(out_a, swap)
    sqlo_a, sqhi_a = send(squp_a, up), send(sqdown_a, down)
    out_b, squp_b, sqdown_b = second(
        2, (up_a, up_b, down_a, down_b, lo_a, lo_b, hi_a, hi_b), total[1] - cut[1] + 8,
        rows - cut[2], rows - cut[3], cut[2], (q_tail,),
    )
    out_b = send(out_b, swap)
    sqlo_b, sqhi_b = send(squp_b, up), send(sqdown_b, down)

    def last(parts):
        return call(
            functools.partial(last_kernel, planes), [VMEM] * 4, [(mplanes, parts[0].shape[1]) + tail],
            cost=2,
        )(*parts)[0]

    g_a = send(last((squp_a, sqdown_a, sqlo_a, sqhi_a)), swap)
    g_b = send(last((squp_b, sqdown_b, sqlo_b, sqhi_b)), swap)

    native = (rows * cols, LANES)
    m2, i2 = call(
        functools.partial(unpack_kernel, (cut[2], rows - cut[2]), ((0, 3), (mplanes, 1))),
        [SMEM, VMEM, VMEM], [(3, planes) + native, (planes,) + native], cost=2,
    )(flip, out_a, out_b)
    (grad,) = call(
        functools.partial(unpack_kernel, (cut[3], rows - cut[3]), ((0, 3),)),
        [SMEM, VMEM, VMEM], [(3, planes) + native], cost=2,
    )(flip, g_a, g_b)
    return untiled(m2, rows), untiled(i2, rows), untiled(grad, rows)


def solution(mesh):
    return jax.shard_map(
        shoot,
        mesh=mesh,
        in_specs=(
            P(None, ("groups", "gz"), "gy", None),
            P(("groups", "gz"), "gy", None),
            P(("groups", "gz"), "gy", None),
        ),
        out_specs=(
            P(None, ("groups", "gz"), "gy", None),
            P(("groups", "gz"), "gy", None),
            P(None, ("groups", "gz"), "gy", None),
        ),
        check_vma=False,
    )
```

```python
import functools
import math

import jax
import jax.numpy as jnp
from jax import lax
from jax.experimental import pallas as pl
from jax.experimental.pallas import tpu as pltpu
from jax.sharding import PartitionSpec as P

LANES = 128
SUB = 8

UNIT = 0.05
SCALE = UNIT * UNIT * UNIT
STEP_SIZE = 0.25
UNROLL = (4, 2, 1)

AXES = ("gz", "gy")
VMEM = pl.BlockSpec(memory_space=pltpu.VMEM)
SMEM = pl.BlockSpec(memory_space=pltpu.SMEM)


def place(depth, half):
    return 4 * (depth // 2) + 2 * half + depth % 2


def swap_pairs(count):
    swapped = {1: 2, 2: 1}
    return [(i, 4 * (i // 4) + swapped.get(i % 4, i % 4)) for i in range(count)]


def up_pairs(count):
    return [(place(d, h), place(d + 1, h)) for h in range(2) for d in range(count // 2 - 1)]


def down_pairs(count):
    return [(b, a) for a, b in up_pairs(count)]


def tiled(cells):
    lead, (rows, width) = cells.shape[:-2], cells.shape[-2:]
    cells = cells.reshape(lead + (rows // SUB, SUB, width // LANES, LANES))
    cells = jnp.swapaxes(cells, -2, -3)
    return cells.reshape(lead + (rows * width // LANES, LANES))


def untiled(cells, rows):
    lead, (total, lanes) = cells.shape[:-2], cells.shape[-2:]
    cols = total // rows
    cells = cells.reshape(lead + (rows // SUB, cols, SUB, LANES))
    cells = jnp.swapaxes(cells, -2, -3)
    return cells.reshape(lead + (rows, cols * LANES))


class Line:
    def __init__(self, cols):
        self.cols = cols
        lane = lax.broadcasted_iota(jnp.int32, (cols, LANES), 1)
        sub = lax.broadcasted_iota(jnp.int32, (cols, LANES), 0)
        self.first, self.last = sub == 0, sub == cols - 1
        self.at_start, self.near_start = lane == 0, lane < 2
        self.at_end, self.near_end = lane == LANES - 1, lane >= LANES - 2

    def beside(self, row):
        ahead = pltpu.roll(row, LANES - 1, 1)
        ahead = jnp.where(
            self.at_end, jnp.where(self.last, 0.0, pltpu.roll(ahead, self.cols - 1, 0)), ahead
        )
        behind = pltpu.roll(row, 1, 1)
        behind = jnp.where(
            self.at_start, jnp.where(self.first, 0.0, pltpu.roll(behind, 1, 0)), behind
        )
        return ahead, behind

    def smooth(self, row):
        ahead, behind = self.beside(row)
        mid = (ahead + behind) + (row + row)
        high = pltpu.roll(mid, LANES - 2, 1)
        high = jnp.where(
            self.near_end, jnp.where(self.last, ahead, pltpu.roll(high, self.cols - 1, 0)), high
        )
        low = pltpu.roll(mid, 2, 1)
        low = jnp.where(
            self.near_start, jnp.where(self.first, behind, pltpu.roll(low, 1, 0)), low
        )
        return 3.0 * mid + (low + high)


def smooth_rows(line, load, store, count, top):
    last = line.smooth(load(0))
    pairs = last if top else None
    sums = {-2: None, -1: last if top else None}
    for r in range(1, count):
        here = line.smooth(load(r))
        nxt = last + here
        sums[r - 1] = None if pairs is None else pairs + nxt
        last, pairs = here, nxt
        done = r - 3
        if done >= (0 if top else 3):
            out = 3.0 * sums[done] + sums[done + 2]
            store(done, out if sums[done - 2] is None else out + sums[done - 2])


def smooth_planes(planes, scale=SCALE):
    pairs = [a + b for a, b in zip(planes, planes[1:])]
    sums = [a + b for a, b in zip(pairs, pairs[1:])]
    out = [3.0 * mid + (low + high) for low, mid, high in zip(sums, sums[2:], sums[4:])]
    return out if scale == 1.0 else [scale * row for row in out]


def spot(row, cols):
    return (row // SUB) * SUB * cols + row % SUB


def mirrored(row, rows, cols, flip):
    a, b = spot(row, cols), spot(rows - 1 - row, cols)
    return a + flip * (b - a)


def pack_kernel(first, stop, rows, with_target, flip_ref, m_ref, i_ref, *refs):
    if with_target:
        t_ref, halo_ref, out_ref, tout_ref = refs
    else:
        (out_ref,) = refs
        t_ref = halo_ref = None
    cols = out_ref.shape[-2]
    planes = i_ref.shape[0]
    flip = flip_ref[0]
    sign = (1 - 2 * flip).astype(jnp.float32)

    def copy(src, halo, dst, start, end, factor):
        for r in range(start, end):
            if r < rows:
                row = src[pl.ds(mirrored(r, rows, cols, flip), cols, stride=SUB), :]
            else:
                at = mirrored(r - rows, halo.shape[0] // cols, cols, flip)
                row = halo[pl.ds(at, cols, stride=SUB), :]
            dst[r - start] = row if factor is None else row * factor

    def halo_at(n, z):
        return None if halo_ref is None else halo_ref.at[n, z]

    def body(z, carry):
        for comp in range(3):
            copy(
                m_ref.at[comp, z], halo_at(comp, z), out_ref.at[2 + comp * planes + z], first, stop,
                sign if comp == 1 else None,
            )
        spare = jnp.where(z < 2, 3 * planes + 2 + z, z - (planes - 2))
        copy(i_ref.at[z], halo_at(3, z), out_ref.at[spare], first, stop, None)
        if with_target:
            copy(t_ref.at[z], halo_at(4, z), tout_ref.at[z], 0, rows + 3, None)
        return carry

    lax.fori_loop(0, planes, body, 0)


def unpack_kernel(counts, parts, flip_ref, *refs):
    ins, outs = refs[: len(counts)], refs[len(counts) :]
    rows = sum(counts)
    flip = flip_ref[0]
    sign = (1 - 2 * flip).astype(jnp.float32)
    cols = ins[0].shape[-2]

    for out, (offset, components) in zip(outs, parts):
        planes = out.shape[-3]
        for comp in range(components):
            dst = out.at[comp] if len(out.shape) == 4 else out

            def body(z, carry, comp=comp, dst=dst, offset=offset, planes=planes):
                done = 0
                for ref, count in zip(ins, counts):
                    for r in range(count):
                        row = ref[offset + comp * planes + z, r]
                        at = mirrored(done + r, rows, cols, flip)
                        dst[z, pl.ds(at, cols, stride=SUB), :] = row * sign if comp == 1 else row
                    done += count
                return carry

            lax.fori_loop(0, planes, body, 0)


class Both:
    def __init__(self, copies):
        self.copies = copies

    def wait(self):
        for copy in self.copies:
            copy.wait()


class Fetcher:
    def __init__(self, sems):
        self.sems, self.used = sems, 0

    def __call__(self, parts, buf, plane, count, target=None):
        copies, row = [], 0
        target = plane if target is None else target
        for ref, start in parts:
            rows = ref.shape[1] - start
            copy = pltpu.make_async_copy(
                ref.at[pl.ds(plane, count), pl.ds(start, rows)],
                buf.at[pl.ds(target, count), pl.ds(row, rows)],
                self.sems.at[self.used],
            )
            copy.start()
            copies.append(copy)
            self.used += 1
            row += rows
        return Both(copies)


def parts_of(refs, chunks, n, overlap=8):
    refs = refs[n * chunks : (n + 1) * chunks]
    return [(ref, ref.shape[1] - overlap if n + 1 < chunks else 0) for n, ref in enumerate(refs)]


def wait(copies):
    for copy in copies:
        copy.wait()


def velocity(line, edge_ref, blocks, image_copies, s_ref, v_ref, top):
    planes = v_ref.shape[1] - 2
    count = blocks[0][1].shape[1]
    zero = jnp.zeros(v_ref.shape[-2:], jnp.float32)

    for comp in range(3):
        for copies, _, _ in blocks:
            copies[comp].wait()

        def rows(r, carry, comp=comp):
            last, pairs = carry
            stack = [ref[offset + comp * planes + z, r] for _, ref, offset in blocks for z in range(planes)]
            here = smooth_planes(stack[planes - 4 : 2 * planes + 4], 1.0)
            nxt = [a + b for a, b in zip(last, here)]
            for z in range(planes + 2):
                s_ref[comp, z, r + 1] = pairs[z] + nxt[z]
            return here, nxt

        empty = [zero] * (planes + 2)
        lax.fori_loop(0, count, rows, (empty, empty), unroll=UNROLL[0])
        if top:
            for z in range(planes + 2):
                s_ref[comp, z, 0] = zero

    scales = [SCALE * edge_ref[0]] + [SCALE] * planes + [SCALE * edge_ref[1]]

    def finish(r, carry):
        for comp in range(3):
            for z in range(planes + 2):
                row = 3.0 * s_ref[comp, z, r + 2] + (s_ref[comp, z, r] + s_ref[comp, z, r + 4])
                v_ref[comp, z, r] = scales[z] * line.smooth(row)
        return carry

    lax.fori_loop(0 if top else 3, count - 3, finish, 0, unroll=UNROLL[1])
    wait(image_copies)


def change(speed, f, around):
    total = None
    for (rise, fall), (upper, lower) in zip(speed, around):
        up = rise * (f - lower if lower is not None else f)
        down = fall * (upper - f)
        total = up + down if total is None else total + (up + down)
    return total


def advance(line, v_ref, momentum, image, z, r, first):
    velo = [v_ref[c, z + 1, r] for c in range(3)]
    speed = [(jnp.maximum(v, 0.0), jnp.minimum(v, 0.0)) for v in velo]

    def around(load):
        mid = load(z, r)
        return mid, [
            line.beside(mid),
            (load(z, r + 1), None if first else load(z, r - 1)),
            (load(z + 1, r), load(z - 1, r)),
        ]

    new_image = None
    if image is not None:
        mid, sides = around(image)
        new_image = mid - STEP_SIZE * change(speed, mid, sides)
    if momentum is None:
        return None, new_image

    slopes = []
    for comp in range(3):
        ahead, behind = line.beside(velo[comp])
        slopes.append(
            (
                ahead - behind,
                v_ref[comp, z + 1, r + 1] - (0.0 if first else v_ref[comp, z + 1, r - 1]),
                v_ref[comp, z + 2, r] - v_ref[comp, z, r],
            )
        )
    divergence = slopes[0][0] + slopes[1][1] + slopes[2][2]
    fields = [around(load) for load in momentum]
    mids = [mid for mid, _ in fields]
    new = []
    for comp in range(3):
        mid, sides = fields[comp]
        stretch = mid * divergence
        for other in range(3):
            stretch = stretch + mids[other] * slopes[other][comp]
        moved = change(speed, mid, sides)
        new.append(mid - (STEP_SIZE * moved + (0.5 * STEP_SIZE) * stretch))
    return new, new_image


def over_rows(body, start, stop, top):
    if top and start == 0:
        body(0, True)
        start = 1

    def step(r, carry):
        body(r, False)
        return carry

    lax.fori_loop(start, stop, step, 0, unroll=UNROLL[2])


def momentum_at(own, lo, hi, offsets, planes):
    def at(comp):
        def load(z, r):
            if z < 0:
                return lo[offsets[0] + comp * planes + planes + z, r]
            if z >= planes:
                return hi[offsets[2] + comp * planes + z - planes, r]
            return own[offsets[1] + comp * planes + z, r]

        return load

    return [at(comp) for comp in range(3)]


def first_kernel(chunks, planes, edge_ref, *refs):
    top = chunks == 1
    ins, (up_ref, down_ref), scratch = refs[: 3 * chunks], refs[3 * chunks :][:2], refs[3 * chunks + 2 :]
    own, lo, hi, s_ref, v_ref, sems = scratch
    fetch = Fetcher(sems)
    blocks = [(1, lo, 1), (0, own, 2), (2, hi, 0)]
    copies = [[], [], []]
    for comp in range(3):
        for n, (at, buf, offset) in enumerate(blocks):
            copies[n].append(fetch(parts_of(ins, chunks, at), buf, offset + comp * planes, planes))
    image_copies = [
        fetch(parts_of(ins, chunks, at), buf, plane, count)
        for at, buf, plane, count in (
            (0, own, 0, 2), (0, own, 3 * planes + 2, 2), (1, lo, 0, 1), (2, hi, 3 * planes, 1),
        )
    ]
    line = Line(own.shape[-2])

    def image(z, r):
        if z < 0:
            return lo[0, r]
        if z >= planes:
            return hi[3 * planes, r]
        return own[3 * planes + 2 + z, r] if z < 2 else own[z - (planes - 2), r]

    velocity(
        line, edge_ref, [(c, buf, offset) for c, (_, buf, offset) in zip(copies, blocks)],
        image_copies, s_ref, v_ref, top,
    )
    momentum = momentum_at(own, lo, hi, (1, 2, 0), planes)
    start = 0 if top else 4

    def body(r, first):
        for z in range(planes):
            new, img = advance(line, v_ref, momentum, image, z, r, first)
            for c in range(3):
                up_ref[2 + c * planes + z, r - start] = new[c]
                down_ref[c * planes + z, r - start] = new[c]
            if z < 2:
                down_ref[3 * planes + z, r - start] = img
            else:
                up_ref[z - (planes - 2), r - start] = img

    over_rows(body, start, own.shape[1] - 4, top)


def second_kernel(chunks, planes, rows, edge_ref, t_ref, *refs):
    top = chunks == 1
    start, stop, t_start, given = rows
    ins, refs = refs[: 4 * chunks], refs[4 * chunks :]
    if top:
        (out_ref, squp_ref, sqdown_ref, tail_ref), scratch = refs[:4], refs[4:]
        before_ref = None
    else:
        before_ref = refs[0]
        (out_ref, squp_ref, sqdown_ref), scratch = refs[1:4], refs[4:]
    own, down, lo, hi, s_ref, v_ref, i2_ref, q_ref, t_buf, sems = scratch
    fetch = Fetcher(sems)
    blocks = [(2, lo, 2), (0, own, 2), (3, hi, 0)]
    copies = [[], [], []]
    for comp in range(3):
        for n, (at, buf, offset) in enumerate(blocks):
            copies[n].append(fetch(parts_of(ins, chunks, at), buf, offset + comp * planes, planes))
    image_copies = [
        fetch(parts_of(ins, chunks, at), buf, plane, 2, target)
        for at, buf, plane, target in (
            (0, own, 0, 0), (1, down, 3 * planes, 0), (2, lo, 0, 0), (3, hi, 3 * planes, 3 * planes),
        )
    ]
    t_copy = fetch([(t_ref.at[:, pl.ds(t_start, t_buf.shape[1])], 0)], t_buf, 0, planes)
    lead = 0 if top else 6
    if not top:
        q_copy = pltpu.make_async_copy(before_ref, q_ref.at[:, pl.ds(0, lead)], sems.at[fetch.used])
        q_copy.start()
    line = Line(own.shape[-2])

    def image(z, r):
        if z < 0:
            return lo[2 + z, r]
        if z >= planes:
            return hi[3 * planes + z - planes, r]
        return down[z, r] if z < 2 else own[z - (planes - 2), r]

    velocity(
        line, edge_ref, [(c, buf, offset) for c, (_, buf, offset) in zip(copies, blocks)],
        image_copies, s_ref, v_ref, top,
    )
    momentum = momentum_at(own, lo, hi, (2, 2, 0), planes)

    def step(keep, r, first):
        for z in range(planes):
            new, img = advance(line, v_ref, momentum, image, z, r, first)
            for c in range(3):
                q_ref[c * planes + z, r - start + lead] = new[c]
                if keep:
                    out_ref[c * planes + z, r - start] = new[c]
            i2_ref[z + 1, r] = img
            if keep:
                out_ref[3 * planes + z, r - start] = img
        for z in (-1, planes):
            i2_ref[z + 1, r] = advance(line, v_ref, None, image, z, r, first)[1]

    if not top:
        for z in range(planes):
            i2_ref[z + 1, start - 1] = advance(line, v_ref, None, image, z, start - 1, False)[1]
    over_rows(functools.partial(step, True), start, start + given, top)
    if start + given < stop:
        over_rows(functools.partial(step, False), start + given, stop, top)
    for z in range(planes):
        i2_ref[z + 1, stop] = advance(line, v_ref, None, image, z, stop, False)[1]
    t_copy.wait()
    if not top:
        q_copy.wait()

    def force(r, first):
        for z in range(planes):
            img = i2_ref[z + 1, r]
            half = 0.5 * (img - t_buf[z, r - start])
            ahead, behind = line.beside(img)
            slopes = (
                ahead - behind,
                i2_ref[z + 1, r + 1] - (0.0 if first else i2_ref[z + 1, r - 1]),
                i2_ref[z + 2, r] - i2_ref[z, r],
            )
            for c in range(3):
                at = c * planes + z
                q_ref[at, r - start + lead] = q_ref[at, r - start + lead] - half * slopes[c]

    over_rows(force, start, stop, top)
    size = q_ref.shape[1]
    if top:
        for n in range(3 * planes):
            for r in range(6):
                tail_ref[n, r] = q_ref[n, size - 6 + r]

    for z in range(planes):

        def body(c, carry, z=z):
            n = c * planes + z

            def store(r, row):
                r = r if top else r - 3
                if z > 0:
                    squp_ref[c * (planes - 1) + z - 1, r] = row
                if z < planes - 1:
                    sqdown_ref[c * (planes - 1) + z, r] = row

            smooth_rows(line, lambda r: q_ref[n, r], store, size, top)
            return carry

        lax.fori_loop(0, 3, body, 0)


def last_kernel(planes, up_ref, down_ref, lo_ref, hi_ref, out_ref):
    near = planes - 1

    def body(r, carry):
        for c in range(3):
            stack = [lo_ref[c * near + near - 3 + z, r] for z in range(3)]
            stack += [down_ref[c * near + z, r] for z in range(near)]
            stack += [up_ref[c * near + near - 1, r]]
            stack += [hi_ref[c * near + z, r] for z in range(3)]
            for z, plane in enumerate(smooth_planes(stack)):
                out_ref[c * planes + z, r] = plane
        return carry

    lax.fori_loop(0, up_ref.shape[1], body, 0)


ANY = pl.BlockSpec(memory_space=pl.ANY)


def call(kernel, specs, outs, scratch=(), copies=0, cost=0.0, inside=1 << 20):
    sizes = [4 * math.prod(o) for o in outs] * 2 + [4 * math.prod(o) for o in scratch]
    return pl.pallas_call(
        kernel,
        in_specs=specs,
        out_specs=[VMEM] * len(outs),
        out_shape=[jax.ShapeDtypeStruct(o, jnp.float32) for o in outs],
        scratch_shapes=[pltpu.VMEM(s, jnp.float32) for s in scratch]
        + ([pltpu.SemaphoreType.DMA((copies,))] if copies else []),
        compiler_params=pltpu.CompilerParams(vmem_limit_bytes=sum(sizes) + inside + (1 << 20)),
        cost_estimate=pl.CostEstimate(flops=0, transcendentals=0, bytes_accessed=int(cost * 3.3e6)),
    )


def shoot(momentum, template, target):
    planes, rows, width = template.shape
    cols = width // LANES
    halves = lax.axis_size("gy")
    count = lax.axis_size("gz") * halves
    flat = lax.axis_index("gz") * halves + lax.axis_index("gy")
    depth = 2 * (flat // 4) + flat % 2
    edge = jnp.stack([depth > 0, depth < count // 2 - 1]).astype(jnp.float32)
    flip = lax.axis_index("gy").reshape(1)
    swap, up, down = swap_pairs(count), up_pairs(count), down_pairs(count)
    tail = (cols, LANES)
    all_planes = 4 * planes
    mplanes = 3 * planes

    def send(cells, pairs):
        return lax.ppermute(cells, AXES, pairs)

    mom, img, tgt = tiled(momentum), tiled(template), tiled(target)
    near = 2 * SUB
    edge_rows = near * cols

    def border(cells):
        return jnp.where(
            lax.axis_index("gy") == 0, cells[..., -edge_rows:, :], cells[..., :edge_rows, :]
        )

    reach = 4 + 4 + 3
    total = [rows + reach, rows + reach - 4, rows + reach - 8, rows]
    cut = [7 * rows // 8]
    cut += [cut[0] - 4, cut[0] - 8, cut[0] - 11]

    halo = lax.ppermute(
        jnp.concatenate([border(mom), border(img)[None], border(tgt)[None]]), "gy", [(0, 1), (1, 0)]
    )
    (a0,) = call(
        functools.partial(pack_kernel, 0, cut[0], rows, False),
        [SMEM, VMEM, VMEM],
        [(all_planes, cut[0]) + tail],
        cost=2.5, inside=6 << 20,
    )(flip, mom, img)
    a0 = send(a0, swap)
    b0, t0 = call(
        functools.partial(pack_kernel, cut[0], total[0], rows, True),
        [SMEM] + [VMEM] * 4,
        [(all_planes, total[0] - cut[0]) + tail, (planes, total[2]) + tail],
        cost=3, inside=10 << 20,
    )(flip, mom, img, tgt, halo)
    b0 = send(b0, swap)
    t0 = send(t0, swap)

    def exchange(chunk):
        return (chunk, send(chunk[1 : 2 + mplanes], up), send(chunk[2 : 3 + mplanes], down))

    z_a, z_b = exchange(a0), exchange(b0)

    def first(chunks, parts, size):
        give = size - 4 - (0 if chunks == 1 else 4)
        return call(
            functools.partial(first_kernel, chunks, planes),
            [SMEM] + [ANY] * (3 * chunks),
            [(mplanes + 2, give) + tail] * 2,
            [(all_planes, size) + tail] + [(mplanes + 1, size) + tail] * 2
            + [(3, planes + 2, size + 1) + tail, (3, planes + 2, size) + tail],
            copies=13 * chunks, cost=9,
        )(edge, *parts)

    up_a, down_a = first(1, z_a, cut[0])
    lo_a, hi_a = send(up_a, up), send(down_a, down)
    up_b, down_b = first(
        2, [part for pair in zip(z_a, z_b) for part in pair], total[0] - cut[0] + 8
    )
    lo_b, hi_b = send(up_b, up), send(down_b, down)

    def second(chunks, parts, size, given, sq_rows, t_start, before):
        start = 0 if chunks == 1 else 4
        stop = size - 4
        lead = 0 if chunks == 1 else 6
        outs = [(all_planes, given) + tail] + [(3 * (planes - 1), sq_rows) + tail] * 2
        if chunks == 1:
            outs.append((mplanes, 6) + tail)
        return call(
            functools.partial(second_kernel, chunks, planes, (start, stop, t_start, given)),
            [SMEM, ANY] + [ANY] * (4 * chunks + len(before)),
            outs,
            [(mplanes + 2, size) + tail, (2, size) + tail, (mplanes + 2, size) + tail, (mplanes + 2, size) + tail]
            + [(3, planes + 2, size + 1) + tail, (3, planes + 2, size) + tail]
            + [(planes + 2, size) + tail, (mplanes, lead + stop - start) + tail, (planes, stop - start) + tail],
            copies=13 * chunks + 2, cost=11,
        )(edge, t0, *parts, *before)

    out_a, squp_a, sqdown_a, q_tail = second(
        1, (up_a, down_a, lo_a, hi_a), cut[1], cut[2], cut[3], 0, ()
    )
    out_a = send(out_a, swap)
    sqlo_a, sqhi_a = send(squp_a, up), send(sqdown_a, down)
    out_b, squp_b, sqdown_b = second(
        2, (up_a, up_b, down_a, down_b, lo_a, lo_b, hi_a, hi_b), total[1] - cut[1] + 8,
        rows - cut[2], rows - cut[3], cut[2], (q_tail,),
    )
    out_b = send(out_b, swap)
    sqlo_b, sqhi_b = send(squp_b, up), send(sqdown_b, down)

    def last(parts):
        return call(
            functools.partial(last_kernel, planes), [VMEM] * 4, [(mplanes, parts[0].shape[1]) + tail],
            cost=2, inside=6 << 20,
        )(*parts)[0]

    g_a = send(last((squp_a, sqdown_a, sqlo_a, sqhi_a)), swap)
    g_b = send(last((squp_b, sqdown_b, sqlo_b, sqhi_b)), swap)

    native = (rows * cols, LANES)
    m2, i2 = call(
        functools.partial(unpack_kernel, (cut[2], rows - cut[2]), ((0, 3), (mplanes, 1))),
        [SMEM, VMEM, VMEM], [(3, planes) + native, (planes,) + native], cost=2, inside=6 << 20,
    )(flip, out_a, out_b)
    (grad,) = call(
        functools.partial(unpack_kernel, (cut[3], rows - cut[3]), ((0, 3),)),
        [SMEM, VMEM, VMEM], [(3, planes) + native], cost=2, inside=6 << 20,
    )(flip, g_a, g_b)
    return untiled(m2, rows), untiled(i2, rows), untiled(grad, rows)


def solution(mesh):
    return jax.shard_map(
        shoot,
        mesh=mesh,
        in_specs=(
            P(None, ("groups", "gz"), "gy", None),
            P(("groups", "gz"), "gy", None),
            P(("groups", "gz"), "gy", None),
        ),
        out_specs=(
            P(None, ("groups", "gz"), "gy", None),
            P(("groups", "gz"), "gy", None),
            P(None, ("groups", "gz"), "gy", None),
        ),
        check_vma=False,
    )
```

```python
import functools
import math

import jax
import jax.numpy as jnp
from jax import lax
from jax.experimental import pallas as pl
from jax.experimental.pallas import tpu as pltpu
from jax.sharding import PartitionSpec as P

LANES = 128
SUB = 8

UNIT = 0.05
SCALE = UNIT * UNIT * UNIT
STEP_SIZE = 0.25
UNROLL = (4, 2, 1, 4)

AXES = ("gz", "gy")
VMEM = pl.BlockSpec(memory_space=pltpu.VMEM)
SMEM = pl.BlockSpec(memory_space=pltpu.SMEM)


def place(depth, half):
    return 4 * (depth // 2) + 2 * half + depth % 2


def swap_pairs(count):
    swapped = {1: 2, 2: 1}
    return [(i, 4 * (i // 4) + swapped.get(i % 4, i % 4)) for i in range(count)]


def up_pairs(count):
    return [(place(d, h), place(d + 1, h)) for h in range(2) for d in range(count // 2 - 1)]


def down_pairs(count):
    return [(b, a) for a, b in up_pairs(count)]


def tiled(cells):
    lead, (rows, width) = cells.shape[:-2], cells.shape[-2:]
    cells = cells.reshape(lead + (rows // SUB, SUB, width // LANES, LANES))
    cells = jnp.swapaxes(cells, -2, -3)
    return cells.reshape(lead + (rows * width // LANES, LANES))


def untiled(cells, rows):
    lead, (total, lanes) = cells.shape[:-2], cells.shape[-2:]
    cols = total // rows
    cells = cells.reshape(lead + (rows // SUB, cols, SUB, LANES))
    cells = jnp.swapaxes(cells, -2, -3)
    return cells.reshape(lead + (rows, cols * LANES))


class Line:
    def __init__(self, cols):
        self.cols = cols
        lane = lax.broadcasted_iota(jnp.int32, (cols, LANES), 1)
        sub = lax.broadcasted_iota(jnp.int32, (cols, LANES), 0)
        self.first, self.last = sub == 0, sub == cols - 1
        self.at_start, self.near_start = lane == 0, lane < 2
        self.at_end, self.near_end = lane == LANES - 1, lane >= LANES - 2

    def beside(self, row):
        ahead = pltpu.roll(row, LANES - 1, 1)
        ahead = jnp.where(
            self.at_end, jnp.where(self.last, 0.0, pltpu.roll(ahead, self.cols - 1, 0)), ahead
        )
        behind = pltpu.roll(row, 1, 1)
        behind = jnp.where(
            self.at_start, jnp.where(self.first, 0.0, pltpu.roll(behind, 1, 0)), behind
        )
        return ahead, behind

    def smooth(self, row):
        ahead, behind = self.beside(row)
        mid = (ahead + behind) + (row + row)
        high = pltpu.roll(mid, LANES - 2, 1)
        high = jnp.where(
            self.near_end, jnp.where(self.last, ahead, pltpu.roll(high, self.cols - 1, 0)), high
        )
        low = pltpu.roll(mid, 2, 1)
        low = jnp.where(
            self.near_start, jnp.where(self.first, behind, pltpu.roll(low, 1, 0)), low
        )
        return 3.0 * mid + (low + high)


def smooth_rows(line, load, store, count, top):
    last = line.smooth(load(0))
    pairs = last if top else None
    sums = {-2: None, -1: last if top else None}
    for r in range(1, count):
        here = line.smooth(load(r))
        nxt = last + here
        sums[r - 1] = None if pairs is None else pairs + nxt
        last, pairs = here, nxt
        done = r - 3
        if done >= (0 if top else 3):
            out = 3.0 * sums[done] + sums[done + 2]
            store(done, out if sums[done - 2] is None else out + sums[done - 2])


def smooth_planes(planes, scale=SCALE):
    pairs = [a + b for a, b in zip(planes, planes[1:])]
    sums = [a + b for a, b in zip(pairs, pairs[1:])]
    out = [3.0 * mid + (low + high) for low, mid, high in zip(sums, sums[2:], sums[4:])]
    return out if scale == 1.0 else [scale * row for row in out]


def spot(row, cols):
    return (row // SUB) * SUB * cols + row % SUB


def mirrored(row, rows, cols, flip):
    a, b = spot(row, cols), spot(rows - 1 - row, cols)
    return a + flip * (b - a)


def pack_kernel(first, stop, rows, comps, lead, flip_ref, m_ref, *refs):
    i_ref, t_ref, halo_ref, out_ref, tout_ref = {
        1: (None, None, None, *refs, None), 2: (refs[0], None, None, refs[-1], None)
    }.get(len(refs), refs)
    cols = out_ref.shape[-2]
    planes = m_ref.shape[1]
    flip = flip_ref[0]
    sign = (1 - 2 * flip).astype(jnp.float32)

    def copy(src, halo, dst, start, end, factor):
        for r in range(start, end):
            if r < rows:
                row = src[pl.ds(mirrored(r, rows, cols, flip), cols, stride=SUB), :]
            else:
                at = mirrored(r - rows, halo.shape[0] // cols, cols, flip)
                row = halo[pl.ds(at, cols, stride=SUB), :]
            dst[r - start] = row if factor is None else row * factor

    def halo_at(n, z):
        return None if halo_ref is None else halo_ref.at[n, z]

    def body(z, carry):
        for n, comp in enumerate(comps):
            copy(
                m_ref.at[comp, z], halo_at(comp, z), out_ref.at[lead + n * planes + z], first, stop,
                sign if comp == 1 else None,
            )
        if lead:
            spare = jnp.where(z < 2, len(comps) * planes + 2 + z, z - (planes - 2))
            copy(i_ref.at[z], halo_at(3, z), out_ref.at[spare], first, stop, None)
        if t_ref is not None:
            copy(t_ref.at[z], halo_at(4, z), tout_ref.at[z], 0, tout_ref.shape[1], None)
        return carry

    lax.fori_loop(0, planes, body, 0)


def unpack_kernel(counts, parts, flip_ref, *refs):
    ins, outs = refs[: len(counts)], refs[len(counts) :]
    rows = sum(counts)
    flip = flip_ref[0]
    sign = (1 - 2 * flip).astype(jnp.float32)
    cols = ins[0].shape[-2]

    for out, (offset, components) in zip(outs, parts):
        planes = out.shape[-3]
        for comp in range(components):
            dst = out.at[comp] if len(out.shape) == 4 else out

            def body(z, carry, comp=comp, dst=dst, offset=offset, planes=planes):
                done = 0
                for ref, count in zip(ins, counts):
                    for r in range(count):
                        row = ref[offset + comp * planes + z, r]
                        at = mirrored(done + r, rows, cols, flip)
                        dst[z, pl.ds(at, cols, stride=SUB), :] = row * sign if comp == 1 else row
                    done += count
                return carry

            lax.fori_loop(0, planes, body, 0)


class Both:
    def __init__(self, copies):
        self.copies = copies

    def wait(self):
        for copy in self.copies:
            copy.wait()


class Fetcher:
    def __init__(self, sems):
        self.sems, self.used = sems, 0

    def __call__(self, parts, buf, target, count):
        copies, row = [], 0
        for ref, start, plane in parts:
            rows = ref.shape[1] - start
            copy = pltpu.make_async_copy(
                ref.at[pl.ds(plane, count), pl.ds(start, rows)],
                buf.at[pl.ds(target, count), pl.ds(row, rows)],
                self.sems.at[self.used],
            )
            copy.start()
            copies.append(copy)
            self.used += 1
            row += rows
        return Both(copies)


OVERLAP = 8


def parts_of(refs, chunks, n, plane):
    refs = refs[n * chunks : (n + 1) * chunks]
    return [
        (ref, ref.shape[1] - OVERLAP if n + 1 < chunks else 0, plane) for n, ref in enumerate(refs)
    ]


def wait(copies):
    for copy in copies:
        copy.wait()


def velocity(line, edge_ref, blocks, image_copies, s_ref, v_ref, top):
    planes = v_ref.shape[1] - 2
    count = blocks[0][1].shape[1]
    zero = jnp.zeros(v_ref.shape[-2:], jnp.float32)

    for comp in range(3):
        for copies, _, _ in blocks:
            copies[comp].wait()

        def rows(r, carry, comp=comp):
            last, pairs = carry
            stack = [ref[offset + comp * planes + z, r] for _, ref, offset in blocks for z in range(planes)]
            here = smooth_planes(stack[planes - 4 : 2 * planes + 4], 1.0)
            nxt = [a + b for a, b in zip(last, here)]
            for z in range(planes + 2):
                s_ref[comp, z, r + 1] = pairs[z] + nxt[z]
            return here, nxt

        empty = [zero] * (planes + 2)
        lax.fori_loop(0, count, rows, (empty, empty), unroll=UNROLL[0])
        if top:
            for z in range(planes + 2):
                s_ref[comp, z, 0] = zero

    scales = [SCALE * edge_ref[0]] + [SCALE] * planes + [SCALE * edge_ref[1]]

    def finish(r, carry):
        for comp in range(3):
            for z in range(planes + 2):
                row = 3.0 * s_ref[comp, z, r + 2] + (s_ref[comp, z, r] + s_ref[comp, z, r + 4])
                v_ref[comp, z, r] = scales[z] * line.smooth(row)
        return carry

    lax.fori_loop(0 if top else 3, count - 3, finish, 0, unroll=UNROLL[1])
    wait(image_copies)


def change(speed, f, around):
    total = None
    for (rise, fall), (upper, lower) in zip(speed, around):
        up = rise * (f - lower if lower is not None else f)
        down = fall * (upper - f)
        total = up + down if total is None else total + (up + down)
    return total


def advance(line, v_ref, momentum, image, z, r, first):
    velo = [v_ref[c, z + 1, r] for c in range(3)]
    speed = [(jnp.maximum(v, 0.0), jnp.minimum(v, 0.0)) for v in velo]

    def around(load):
        mid = load(z, r)
        return mid, [
            line.beside(mid),
            (load(z, r + 1), None if first else load(z, r - 1)),
            (load(z + 1, r), load(z - 1, r)),
        ]

    new_image = None
    if image is not None:
        mid, sides = around(image)
        new_image = mid - STEP_SIZE * change(speed, mid, sides)
    if momentum is None:
        return None, new_image

    slopes = []
    for comp in range(3):
        ahead, behind = line.beside(velo[comp])
        slopes.append(
            (
                ahead - behind,
                v_ref[comp, z + 1, r + 1] - (0.0 if first else v_ref[comp, z + 1, r - 1]),
                v_ref[comp, z + 2, r] - v_ref[comp, z, r],
            )
        )
    divergence = slopes[0][0] + slopes[1][1] + slopes[2][2]
    fields = [around(load) for load in momentum]
    mids = [mid for mid, _ in fields]
    new = []
    for comp in range(3):
        mid, sides = fields[comp]
        stretch = mid * divergence
        for other in range(3):
            stretch = stretch + mids[other] * slopes[other][comp]
        moved = change(speed, mid, sides)
        new.append(mid - (STEP_SIZE * moved + (0.5 * STEP_SIZE) * stretch))
    return new, new_image


def over_rows(body, start, stop, top, unroll=1):
    if top and start == 0:
        body(0, True)
        start = 1

    def step(r, carry):
        body(r, False)
        return carry

    lax.fori_loop(start, stop, step, 0, unroll=unroll)


def momentum_at(own, lo, hi, offsets, planes):
    def at(comp):
        def load(z, r):
            if z < 0:
                return lo[offsets[0] + comp * planes + planes + z, r]
            if z >= planes:
                return hi[offsets[2] + comp * planes + z - planes, r]
            return own[offsets[1] + comp * planes + z, r]

        return load

    return [at(comp) for comp in range(3)]


def first_kernel(chunks, planes, edge_ref, *refs):
    top = chunks == 1
    each = chunks + 1
    ins, (up_ref, down_ref), scratch = refs[: 3 * each], refs[3 * each :][:2], refs[3 * each + 2 :]
    own, lo, hi, s_ref, v_ref, sems = scratch
    fetch = Fetcher(sems)

    def sources(block, first_chunk, plane):
        refs = ins[block * each : (block + 1) * each]
        which, at = first_chunk
        parts = [(refs[which], 0 if top else refs[which].shape[1] - OVERLAP, at)]
        return parts if top else parts + [(refs[2], 0, plane)]

    blocks = [(1, lo, 1), (0, own, 2), (2, hi, 0)]
    copies = [[], [], []]
    for comp in range(3):
        for n, (at, buf, offset) in enumerate(blocks):
            plane = offset + comp * planes
            first_chunk = (0, comp * planes) if comp < 2 else (1, offset)
            copies[n].append(fetch(sources(at, first_chunk, plane), buf, plane, planes))
    late = 2 * planes
    image_copies = [
        fetch(sources(at, (1, plane if plane == 0 else plane - late), plane), buf, plane, count)
        for at, buf, plane, count in (
            (0, own, 0, 2), (0, own, 3 * planes + 2, 2), (1, lo, 0, 1), (2, hi, 3 * planes, 1),
        )
    ]
    line = Line(own.shape[-2])

    def image(z, r):
        if z < 0:
            return lo[0, r]
        if z >= planes:
            return hi[3 * planes, r]
        return own[3 * planes + 2 + z, r] if z < 2 else own[z - (planes - 2), r]

    velocity(
        line, edge_ref, [(c, buf, offset) for c, (_, buf, offset) in zip(copies, blocks)],
        image_copies, s_ref, v_ref, top,
    )
    momentum = momentum_at(own, lo, hi, (1, 2, 0), planes)
    start = 0 if top else 4

    def body(r, first):
        for z in range(planes):
            new, img = advance(line, v_ref, momentum, image, z, r, first)
            for c in range(3):
                up_ref[2 + c * planes + z, r - start] = new[c]
                down_ref[c * planes + z, r - start] = new[c]
            if z < 2:
                down_ref[3 * planes + z, r - start] = img
            else:
                up_ref[z - (planes - 2), r - start] = img

    over_rows(body, start, own.shape[1] - 4, top)


def second_kernel(chunks, planes, rows, edge_ref, t_ref, *refs):
    top = chunks == 1
    start, stop, t_start, given = rows
    ins, refs = refs[: 4 * chunks], refs[4 * chunks :]
    if top:
        (out_ref, squp_ref, sqdown_ref, tail_ref), scratch = refs[:4], refs[4:]
        before_ref = None
    else:
        before_ref = refs[0]
        (out_ref, squp_ref, sqdown_ref), scratch = refs[1:4], refs[4:]
    own, down, lo, hi, s_ref, v_ref, i2_ref, q_ref, t_buf, sems = scratch
    fetch = Fetcher(sems)
    blocks = [(2, lo, 2), (0, own, 2), (3, hi, 0)]
    copies = [[], [], []]
    for comp in range(3):
        for n, (at, buf, offset) in enumerate(blocks):
            plane = offset + comp * planes
            copies[n].append(fetch(parts_of(ins, chunks, at, plane), buf, plane, planes))
    image_copies = [
        fetch(parts_of(ins, chunks, at, plane), buf, target, 2)
        for at, buf, plane, target in (
            (0, own, 0, 0), (1, down, 3 * planes, 0), (2, lo, 0, 0), (3, hi, 3 * planes, 3 * planes),
        )
    ]
    t_copy = fetch([(t_ref.at[:, pl.ds(t_start, t_buf.shape[1])], 0, 0)], t_buf, 0, planes)
    lead = 0 if top else 6
    if not top:
        q_copy = pltpu.make_async_copy(before_ref, q_ref.at[:, pl.ds(0, lead)], sems.at[fetch.used])
        q_copy.start()
    line = Line(own.shape[-2])

    def image(z, r):
        if z < 0:
            return lo[2 + z, r]
        if z >= planes:
            return hi[3 * planes + z - planes, r]
        return down[z, r] if z < 2 else own[z - (planes - 2), r]

    velocity(
        line, edge_ref, [(c, buf, offset) for c, (_, buf, offset) in zip(copies, blocks)],
        image_copies, s_ref, v_ref, top,
    )
    momentum = momentum_at(own, lo, hi, (2, 2, 0), planes)

    def step(keep, r, first):
        for z in range(planes):
            new, img = advance(line, v_ref, momentum, image, z, r, first)
            for c in range(3):
                q_ref[c * planes + z, r - start + lead] = new[c]
                if keep:
                    out_ref[c * planes + z, r - start] = new[c]
            i2_ref[z + 1, r] = img
            if keep:
                out_ref[3 * planes + z, r - start] = img
        for z in (-1, planes):
            i2_ref[z + 1, r] = advance(line, v_ref, None, image, z, r, first)[1]

    if not top:
        for z in range(planes):
            i2_ref[z + 1, start - 1] = advance(line, v_ref, None, image, z, start - 1, False)[1]
    over_rows(functools.partial(step, True), start, start + given, top)
    if start + given < stop:
        over_rows(functools.partial(step, False), start + given, stop, top)
    for z in range(planes):
        i2_ref[z + 1, stop] = advance(line, v_ref, None, image, z, stop, False)[1]
    t_copy.wait()
    if not top:
        q_copy.wait()

    def force(r, first):
        for z in range(planes):
            img = i2_ref[z + 1, r]
            half = 0.5 * (img - t_buf[z, r - start])
            ahead, behind = line.beside(img)
            slopes = (
                ahead - behind,
                i2_ref[z + 1, r + 1] - (0.0 if first else i2_ref[z + 1, r - 1]),
                i2_ref[z + 2, r] - i2_ref[z, r],
            )
            for c in range(3):
                at = c * planes + z
                q_ref[at, r - start + lead] = q_ref[at, r - start + lead] - half * slopes[c]

    over_rows(force, start, stop, top, UNROLL[3])
    size = q_ref.shape[1]
    if top:
        for n in range(3 * planes):
            for r in range(6):
                tail_ref[n, r] = q_ref[n, size - 6 + r]

    for z in range(planes):

        def body(c, carry, z=z):
            n = c * planes + z

            def store(r, row):
                r = r if top else r - 3
                if z > 0:
                    squp_ref[c * (planes - 1) + z - 1, r] = row
                if z < planes - 1:
                    sqdown_ref[c * (planes - 1) + z, r] = row

            smooth_rows(line, lambda r: q_ref[n, r], store, size, top)
            return carry

        lax.fori_loop(0, 3, body, 0)


def last_kernel(planes, up_ref, down_ref, lo_ref, hi_ref, out_ref):
    near = planes - 1

    def body(r, carry):
        for c in range(3):
            stack = [lo_ref[c * near + near - 3 + z, r] for z in range(3)]
            stack += [down_ref[c * near + z, r] for z in range(near)]
            stack += [up_ref[c * near + near - 1, r]]
            stack += [hi_ref[c * near + z, r] for z in range(3)]
            for z, plane in enumerate(smooth_planes(stack)):
                out_ref[c * planes + z, r] = plane
        return carry

    lax.fori_loop(0, up_ref.shape[1], body, 0)


ANY = pl.BlockSpec(memory_space=pl.ANY)


def call(kernel, specs, outs, scratch=(), copies=0, cost=0.0, inside=1 << 20):
    sizes = [4 * math.prod(o) for o in outs] * 2 + [4 * math.prod(o) for o in scratch]
    return pl.pallas_call(
        kernel,
        in_specs=specs,
        out_specs=[VMEM] * len(outs),
        out_shape=[jax.ShapeDtypeStruct(o, jnp.float32) for o in outs],
        scratch_shapes=[pltpu.VMEM(s, jnp.float32) for s in scratch]
        + ([pltpu.SemaphoreType.DMA((copies,))] if copies else []),
        compiler_params=pltpu.CompilerParams(vmem_limit_bytes=sum(sizes) + inside + (1 << 20)),
        cost_estimate=pl.CostEstimate(flops=0, transcendentals=0, bytes_accessed=int(cost * 3.3e6)),
    )


def shoot(momentum, template, target):
    planes, rows, width = template.shape
    cols = width // LANES
    halves = lax.axis_size("gy")
    count = lax.axis_size("gz") * halves
    flat = lax.axis_index("gz") * halves + lax.axis_index("gy")
    depth = 2 * (flat // 4) + flat % 2
    edge = jnp.stack([depth > 0, depth < count // 2 - 1]).astype(jnp.float32)
    flip = lax.axis_index("gy").reshape(1)
    swap, up, down = swap_pairs(count), up_pairs(count), down_pairs(count)
    tail = (cols, LANES)
    all_planes = 4 * planes
    mplanes = 3 * planes

    def send(cells, pairs):
        return lax.ppermute(cells, AXES, pairs)

    mom, img, tgt = tiled(momentum), tiled(template), tiled(target)
    near = 2 * SUB
    edge_rows = near * cols

    def border(cells):
        return jnp.where(
            lax.axis_index("gy") == 0, cells[..., -edge_rows:, :], cells[..., :edge_rows, :]
        )

    reach = 4 + 4 + 3
    total = [rows + reach, rows + reach - 4, rows + reach - 8, rows]
    cut = [7 * rows // 8]
    cut += [cut[0] - 4, cut[0] - 8, cut[0] - 11]

    halo = lax.ppermute(
        jnp.concatenate([border(mom), border(img)[None], border(tgt)[None]]), "gy", [(0, 1), (1, 0)]
    )

    def pack(comps, lead, start, stop, ins, outs):
        return call(
            functools.partial(pack_kernel, start, stop, rows, comps, lead),
            [SMEM] + [VMEM] * len(ins),
            [(len(comps) * planes + (planes if lead else 0), stop - start) + tail] + outs,
            cost=2, inside=10 << 20,
        )(flip, *ins)

    (a0,) = pack((0, 1), 0, 0, cut[0], (mom,), [])
    a0 = send(a0, swap)
    (a1,) = pack((2,), 2, 0, cut[0], (mom, img), [])
    a1 = send(a1, swap)
    b0, t0 = pack((0, 1, 2), 2, cut[0], total[0], (mom, img, tgt, halo), [(planes, total[2]) + tail])
    b0 = send(b0, swap)
    t0 = send(t0, swap)

    def exchange(chunk):
        size = chunk.shape[0] - 3
        return (chunk, send(chunk[1 : 1 + size], up), send(chunk[2 : 2 + size], down))

    z_a = (a0, send(a0, up), send(a0, down))
    z_a2, z_b = exchange(a1), exchange(b0)

    def first(chunks, parts, size):
        give = size - 4 - (0 if chunks == 1 else 4)
        return call(
            functools.partial(first_kernel, chunks, planes),
            [SMEM] + [ANY] * (3 * chunks + 3),
            [(mplanes + 2, give) + tail] * 2,
            [(all_planes, size) + tail] + [(mplanes + 1, size) + tail] * 2
            + [(3, planes + 2, size + 1) + tail, (3, planes + 2, size) + tail],
            copies=13 * chunks, cost=9,
        )(edge, *parts)

    up_a, down_a = first(1, [part for pair in zip(z_a, z_a2) for part in pair], cut[0])
    lo_a, hi_a = send(up_a, up), send(down_a, down)
    up_b, down_b = first(
        2, [part for pair in zip(z_a, z_a2, z_b) for part in pair], total[0] - cut[0] + OVERLAP
    )
    lo_b, hi_b = send(up_b, up), send(down_b, down)

    def second(chunks, parts, size, given, sq_rows, t_start, before):
        start = 0 if chunks == 1 else 4
        stop = size - 4
        lead = 0 if chunks == 1 else 6
        outs = [(all_planes, given) + tail] + [(3 * (planes - 1), sq_rows) + tail] * 2
        if chunks == 1:
            outs.append((mplanes, 6) + tail)
        return call(
            functools.partial(second_kernel, chunks, planes, (start, stop, t_start, given)),
            [SMEM, ANY] + [ANY] * (4 * chunks + len(before)),
            outs,
            [(mplanes + 2, size) + tail, (2, size) + tail, (mplanes + 2, size) + tail, (mplanes + 2, size) + tail]
            + [(3, planes + 2, size + 1) + tail, (3, planes + 2, size) + tail]
            + [(planes + 2, size) + tail, (mplanes, lead + stop - start) + tail, (planes, stop - start) + tail],
            copies=13 * chunks + 2, cost=11,
        )(edge, t0, *parts, *before)

    out_a, squp_a, sqdown_a, q_tail = second(
        1, (up_a, down_a, lo_a, hi_a), cut[1], cut[2], cut[3], 0, ()
    )
    out_a = send(out_a, swap)
    sqlo_a, sqhi_a = send(squp_a, up), send(sqdown_a, down)
    out_b, squp_b, sqdown_b = second(
        2, (up_a, up_b, down_a, down_b, lo_a, lo_b, hi_a, hi_b), total[1] - cut[1] + OVERLAP,
        rows - cut[2], rows - cut[3], cut[2], (q_tail,),
    )
    out_b = send(out_b, swap)
    sqlo_b, sqhi_b = send(squp_b, up), send(sqdown_b, down)

    def last(parts):
        return call(
            functools.partial(last_kernel, planes), [VMEM] * 4, [(mplanes, parts[0].shape[1]) + tail],
            cost=2, inside=6 << 20,
        )(*parts)[0]

    g_a = send(last((squp_a, sqdown_a, sqlo_a, sqhi_a)), swap)
    g_b = send(last((squp_b, sqdown_b, sqlo_b, sqhi_b)), swap)

    native = (rows * cols, LANES)
    m2, i2 = call(
        functools.partial(unpack_kernel, (cut[2], rows - cut[2]), ((0, 3), (mplanes, 1))),
        [SMEM, VMEM, VMEM], [(3, planes) + native, (planes,) + native], cost=2, inside=6 << 20,
    )(flip, out_a, out_b)
    (grad,) = call(
        functools.partial(unpack_kernel, (cut[3], rows - cut[3]), ((0, 3),)),
        [SMEM, VMEM, VMEM], [(3, planes) + native], cost=2, inside=6 << 20,
    )(flip, g_a, g_b)
    return untiled(m2, rows), untiled(i2, rows), untiled(grad, rows)


def solution(mesh):
    return jax.shard_map(
        shoot,
        mesh=mesh,
        in_specs=(
            P(None, ("groups", "gz"), "gy", None),
            P(("groups", "gz"), "gy", None),
            P(("groups", "gz"), "gy", None),
        ),
        out_specs=(
            P(None, ("groups", "gz"), "gy", None),
            P(("groups", "gz"), "gy", None),
            P(None, ("groups", "gz"), "gy", None),
        ),
        check_vma=False,
    )
```

```python
import functools
import math

import jax
import jax.numpy as jnp
from jax import lax
from jax.experimental import pallas as pl
from jax.experimental.pallas import tpu as pltpu
from jax.sharding import PartitionSpec as P

LANES = 128
SUB = 8

UNIT = 0.05
SCALE = UNIT * UNIT * UNIT
STEP_SIZE = 0.25
UNROLL = (4, 2, 1, 4)

AXES = ("gz", "gy")
VMEM = pl.BlockSpec(memory_space=pltpu.VMEM)
SMEM = pl.BlockSpec(memory_space=pltpu.SMEM)


def place(depth, half):
    return 4 * (depth // 2) + 2 * half + depth % 2


def swap_pairs(count):
    swapped = {1: 2, 2: 1}
    return [(i, 4 * (i // 4) + swapped.get(i % 4, i % 4)) for i in range(count)]


def up_pairs(count):
    return [(place(d, h), place(d + 1, h)) for h in range(2) for d in range(count // 2 - 1)]


def down_pairs(count):
    return [(b, a) for a, b in up_pairs(count)]


def tiled(cells):
    lead, (rows, width) = cells.shape[:-2], cells.shape[-2:]
    cells = cells.reshape(lead + (rows // SUB, SUB, width // LANES, LANES))
    cells = jnp.swapaxes(cells, -2, -3)
    return cells.reshape(lead + (rows * width // LANES, LANES))


def untiled(cells, rows):
    lead, (total, lanes) = cells.shape[:-2], cells.shape[-2:]
    cols = total // rows
    cells = cells.reshape(lead + (rows // SUB, cols, SUB, LANES))
    cells = jnp.swapaxes(cells, -2, -3)
    return cells.reshape(lead + (rows, cols * LANES))


class Line:
    def __init__(self, cols):
        self.cols = cols
        lane = lax.broadcasted_iota(jnp.int32, (cols, LANES), 1)
        sub = lax.broadcasted_iota(jnp.int32, (cols, LANES), 0)
        self.first, self.last = sub == 0, sub == cols - 1
        self.at_start, self.near_start = lane == 0, lane < 2
        self.at_end, self.near_end = lane == LANES - 1, lane >= LANES - 2

    def beside(self, row):
        ahead = pltpu.roll(row, LANES - 1, 1)
        ahead = jnp.where(
            self.at_end, jnp.where(self.last, 0.0, pltpu.roll(ahead, self.cols - 1, 0)), ahead
        )
        behind = pltpu.roll(row, 1, 1)
        behind = jnp.where(
            self.at_start, jnp.where(self.first, 0.0, pltpu.roll(behind, 1, 0)), behind
        )
        return ahead, behind

    def smooth(self, row):
        ahead, behind = self.beside(row)
        mid = (ahead + behind) + (row + row)
        high = pltpu.roll(mid, LANES - 2, 1)
        high = jnp.where(
            self.near_end, jnp.where(self.last, ahead, pltpu.roll(high, self.cols - 1, 0)), high
        )
        low = pltpu.roll(mid, 2, 1)
        low = jnp.where(
            self.near_start, jnp.where(self.first, behind, pltpu.roll(low, 1, 0)), low
        )
        return 3.0 * mid + (low + high)


def smooth_rows(line, load, store, count, top):
    last = line.smooth(load(0))
    pairs = last if top else None
    sums = {-2: None, -1: last if top else None}
    for r in range(1, count):
        here = line.smooth(load(r))
        nxt = last + here
        sums[r - 1] = None if pairs is None else pairs + nxt
        last, pairs = here, nxt
        done = r - 3
        if done >= (0 if top else 3):
            out = 3.0 * sums[done] + sums[done + 2]
            store(done, out if sums[done - 2] is None else out + sums[done - 2])


def smooth_planes(planes, scale=SCALE):
    pairs = [a + b for a, b in zip(planes, planes[1:])]
    sums = [a + b for a, b in zip(pairs, pairs[1:])]
    out = [3.0 * mid + (low + high) for low, mid, high in zip(sums, sums[2:], sums[4:])]
    return out if scale == 1.0 else [scale * row for row in out]


def spot(row, cols):
    return (row // SUB) * SUB * cols + row % SUB


def mirrored(row, rows, cols, flip):
    a, b = spot(row, cols), spot(rows - 1 - row, cols)
    return a + flip * (b - a)


def pack_kernel(first, stop, rows, comps, lead, flip_ref, m_ref, *refs):
    i_ref, t_ref, halo_ref, out_ref, tout_ref = {
        1: (None, None, None, *refs, None), 2: (refs[0], None, None, refs[-1], None)
    }.get(len(refs), refs)
    cols = out_ref.shape[-2]
    planes = m_ref.shape[1]
    flip = flip_ref[0]
    sign = (1 - 2 * flip).astype(jnp.float32)

    def copy(src, halo, dst, start, end, factor):
        for r in range(start, end):
            if r < rows:
                row = src[pl.ds(mirrored(r, rows, cols, flip), cols, stride=SUB), :]
            else:
                at = mirrored(r - rows, halo.shape[0] // cols, cols, flip)
                row = halo[pl.ds(at, cols, stride=SUB), :]
            dst[r - start] = row if factor is None else row * factor

    def halo_at(n, z):
        return None if halo_ref is None else halo_ref.at[n, z]

    def body(z, carry):
        for n, comp in enumerate(comps):
            copy(
                m_ref.at[comp, z], halo_at(comp, z), out_ref.at[lead + n * planes + z], first, stop,
                sign if comp == 1 else None,
            )
        if lead:
            spare = jnp.where(z < 2, len(comps) * planes + 2 + z, z - (planes - 2))
            copy(i_ref.at[z], halo_at(3, z), out_ref.at[spare], first, stop, None)
        if t_ref is not None:
            copy(t_ref.at[z], halo_at(4, z), tout_ref.at[z], 0, tout_ref.shape[1], None)
        return carry

    lax.fori_loop(0, planes, body, 0)


def unpack_kernel(counts, parts, flip_ref, *refs):
    ins, outs = refs[: len(counts)], refs[len(counts) :]
    rows = sum(counts)
    flip = flip_ref[0]
    sign = (1 - 2 * flip).astype(jnp.float32)
    cols = ins[0].shape[-2]

    for out, (offset, components) in zip(outs, parts):
        planes = out.shape[-3]
        for comp in range(components):
            dst = out.at[comp] if len(out.shape) == 4 else out

            def body(z, carry, comp=comp, dst=dst, offset=offset, planes=planes):
                done = 0
                for ref, count in zip(ins, counts):
                    for r in range(count):
                        row = ref[offset + comp * planes + z, r]
                        at = mirrored(done + r, rows, cols, flip)
                        dst[z, pl.ds(at, cols, stride=SUB), :] = row * sign if comp == 1 else row
                    done += count
                return carry

            lax.fori_loop(0, planes, body, 0)


class Both:
    def __init__(self, copies):
        self.copies = copies

    def wait(self):
        for copy in self.copies:
            copy.wait()


class Fetcher:
    def __init__(self, sems):
        self.sems, self.used = sems, 0

    def __call__(self, parts, buf, target, count):
        copies, row = [], 0
        for ref, start, plane in parts:
            rows = ref.shape[1] - start
            copy = pltpu.make_async_copy(
                ref.at[pl.ds(plane, count), pl.ds(start, rows)],
                buf.at[pl.ds(target, count), pl.ds(row, rows)],
                self.sems.at[self.used],
            )
            copy.start()
            copies.append(copy)
            self.used += 1
            row += rows
        return Both(copies)


OVERLAP = 8


def parts_of(refs, chunks, n, plane):
    refs = refs[n * chunks : (n + 1) * chunks]
    return [
        (ref, ref.shape[1] - OVERLAP if n + 1 < chunks else 0, plane) for n, ref in enumerate(refs)
    ]


def wait(copies):
    for copy in copies:
        copy.wait()


def velocity(line, edge_ref, blocks, image_copies, s_ref, v_ref, top):
    planes = v_ref.shape[1] - 2
    count = blocks[0][1].shape[1]
    zero = jnp.zeros(v_ref.shape[-2:], jnp.float32)

    for comp in range(3):
        for copies, _, _ in blocks:
            copies[comp].wait()

        def rows(r, carry, comp=comp):
            last, pairs = carry
            stack = [ref[offset + comp * planes + z, r] for _, ref, offset in blocks for z in range(planes)]
            here = smooth_planes(stack[planes - 4 : 2 * planes + 4], 1.0)
            nxt = [a + b for a, b in zip(last, here)]
            for z in range(planes + 2):
                s_ref[comp, z, r + 1] = pairs[z] + nxt[z]
            return here, nxt

        empty = [zero] * (planes + 2)
        lax.fori_loop(0, count, rows, (empty, empty), unroll=UNROLL[0])
        if top:
            for z in range(planes + 2):
                s_ref[comp, z, 0] = zero

    scales = [SCALE * edge_ref[0]] + [SCALE] * planes + [SCALE * edge_ref[1]]

    def finish(r, carry):
        for comp in range(3):
            for z in range(planes + 2):
                row = 3.0 * s_ref[comp, z, r + 2] + (s_ref[comp, z, r] + s_ref[comp, z, r + 4])
                v_ref[comp, z, r] = scales[z] * line.smooth(row)
        return carry

    lax.fori_loop(0 if top else 3, count - 3, finish, 0, unroll=UNROLL[1])
    wait(image_copies)


def change(speed, f, around):
    total = None
    for (rise, fall), (upper, lower) in zip(speed, around):
        up = rise * (f - lower if lower is not None else f)
        down = fall * (upper - f)
        total = up + down if total is None else total + (up + down)
    return total


def advance(line, v_ref, momentum, image, z, r, first):
    velo = [v_ref[c, z + 1, r] for c in range(3)]
    speed = [(jnp.maximum(v, 0.0), jnp.minimum(v, 0.0)) for v in velo]

    def around(load):
        mid = load(z, r)
        return mid, [
            line.beside(mid),
            (load(z, r + 1), None if first else load(z, r - 1)),
            (load(z + 1, r), load(z - 1, r)),
        ]

    new_image = None
    if image is not None:
        mid, sides = around(image)
        new_image = mid - STEP_SIZE * change(speed, mid, sides)
    if momentum is None:
        return None, new_image

    slopes = []
    for comp in range(3):
        ahead, behind = line.beside(velo[comp])
        slopes.append(
            (
                ahead - behind,
                v_ref[comp, z + 1, r + 1] - (0.0 if first else v_ref[comp, z + 1, r - 1]),
                v_ref[comp, z + 2, r] - v_ref[comp, z, r],
            )
        )
    divergence = slopes[0][0] + slopes[1][1] + slopes[2][2]
    fields = [around(load) for load in momentum]
    mids = [mid for mid, _ in fields]
    new = []
    for comp in range(3):
        mid, sides = fields[comp]
        stretch = mid * divergence
        for other in range(3):
            stretch = stretch + mids[other] * slopes[other][comp]
        moved = change(speed, mid, sides)
        new.append(mid - (STEP_SIZE * moved + (0.5 * STEP_SIZE) * stretch))
    return new, new_image


def over_rows(body, start, stop, top, unroll=1):
    if top and start == 0:
        body(0, True)
        start = 1

    def step(r, carry):
        body(r, False)
        return carry

    lax.fori_loop(start, stop, step, 0, unroll=unroll)


def momentum_at(own, lo, hi, offsets, planes):
    def at(comp):
        def load(z, r):
            if z < 0:
                return lo[offsets[0] + comp * planes + planes + z, r]
            if z >= planes:
                return hi[offsets[2] + comp * planes + z - planes, r]
            return own[offsets[1] + comp * planes + z, r]

        return load

    return [at(comp) for comp in range(3)]


def first_kernel(chunks, planes, edge_ref, *refs):
    top = chunks == 1
    each = chunks + 1
    ins, (up_ref, down_ref), scratch = refs[: 3 * each], refs[3 * each :][:2], refs[3 * each + 2 :]
    own, lo, hi, s_ref, v_ref, sems = scratch
    fetch = Fetcher(sems)

    def sources(block, first_chunk, plane):
        refs = ins[block * each : (block + 1) * each]
        which, at = first_chunk
        parts = [(refs[which], 0 if top else refs[which].shape[1] - OVERLAP, at)]
        return parts if top else parts + [(refs[2], 0, plane)]

    blocks = [(1, lo, 1), (0, own, 2), (2, hi, 0)]
    copies = [[], [], []]
    for comp in range(3):
        for n, (at, buf, offset) in enumerate(blocks):
            plane = offset + comp * planes
            first_chunk = (0, comp * planes) if comp < 2 else (1, offset)
            copies[n].append(fetch(sources(at, first_chunk, plane), buf, plane, planes))
    late = 2 * planes
    image_copies = [
        fetch(sources(at, (1, plane if plane == 0 else plane - late), plane), buf, plane, count)
        for at, buf, plane, count in (
            (0, own, 0, 2), (0, own, 3 * planes + 2, 2), (1, lo, 0, 1), (2, hi, 3 * planes, 1),
        )
    ]
    line = Line(own.shape[-2])

    def image(z, r):
        if z < 0:
            return lo[0, r]
        if z >= planes:
            return hi[3 * planes, r]
        return own[3 * planes + 2 + z, r] if z < 2 else own[z - (planes - 2), r]

    velocity(
        line, edge_ref, [(c, buf, offset) for c, (_, buf, offset) in zip(copies, blocks)],
        image_copies, s_ref, v_ref, top,
    )
    momentum = momentum_at(own, lo, hi, (1, 2, 0), planes)
    start = 0 if top else 4

    def body(r, first):
        for z in range(planes):
            new, img = advance(line, v_ref, momentum, image, z, r, first)
            for c in range(3):
                up_ref[2 + c * planes + z, r - start] = new[c]
                down_ref[c * planes + z, r - start] = new[c]
            if z < 2:
                down_ref[3 * planes + z, r - start] = img
            else:
                up_ref[z - (planes - 2), r - start] = img

    over_rows(body, start, own.shape[1] - 4, top)


def second_kernel(chunks, planes, rows, edge_ref, t_ref, *refs):
    top = chunks == 1
    start, stop, t_start, given = rows
    ins, refs = refs[: 4 * chunks], refs[4 * chunks :]
    if top:
        (out_ref, squp_ref, sqdown_ref, tail_ref), scratch = refs[:4], refs[4:]
        before_ref = None
    else:
        before_ref = refs[0]
        (out_ref, squp_ref, sqdown_ref), scratch = refs[1:4], refs[4:]
    own, down, lo, hi, s_ref, v_ref, i2_ref, q_ref, t_buf, sems = scratch
    fetch = Fetcher(sems)
    blocks = [(2, lo, 2), (0, own, 2), (3, hi, 0)]
    copies = [[], [], []]
    for comp in range(3):
        for n, (at, buf, offset) in enumerate(blocks):
            plane = offset + comp * planes
            copies[n].append(fetch(parts_of(ins, chunks, at, plane), buf, plane, planes))
    image_copies = [
        fetch(parts_of(ins, chunks, at, plane), buf, target, 2)
        for at, buf, plane, target in (
            (0, own, 0, 0), (1, down, 3 * planes, 0), (2, lo, 0, 0), (3, hi, 3 * planes, 3 * planes),
        )
    ]
    t_copy = fetch([(t_ref.at[:, pl.ds(t_start, t_buf.shape[1])], 0, 0)], t_buf, 0, planes)
    lead = 0 if top else 6
    if not top:
        q_copy = pltpu.make_async_copy(before_ref, q_ref.at[:, pl.ds(0, lead)], sems.at[fetch.used])
        q_copy.start()
    line = Line(own.shape[-2])

    def image(z, r):
        if z < 0:
            return lo[2 + z, r]
        if z >= planes:
            return hi[3 * planes + z - planes, r]
        return down[z, r] if z < 2 else own[z - (planes - 2), r]

    velocity(
        line, edge_ref, [(c, buf, offset) for c, (_, buf, offset) in zip(copies, blocks)],
        image_copies, s_ref, v_ref, top,
    )
    momentum = momentum_at(own, lo, hi, (2, 2, 0), planes)

    def step(keep, r, first):
        for z in range(planes):
            new, img = advance(line, v_ref, momentum, image, z, r, first)
            for c in range(3):
                q_ref[c * planes + z, r - start + lead] = new[c]
                if keep:
                    out_ref[c * planes + z, r - start] = new[c]
            i2_ref[z + 1, r] = img
            if keep:
                out_ref[3 * planes + z, r - start] = img
        for z in (-1, planes):
            i2_ref[z + 1, r] = advance(line, v_ref, None, image, z, r, first)[1]

    if not top:
        for z in range(planes):
            i2_ref[z + 1, start - 1] = advance(line, v_ref, None, image, z, start - 1, False)[1]
    over_rows(functools.partial(step, True), start, start + given, top)
    if start + given < stop:
        over_rows(functools.partial(step, False), start + given, stop, top)
    for z in range(planes):
        i2_ref[z + 1, stop] = advance(line, v_ref, None, image, z, stop, False)[1]
    t_copy.wait()
    if not top:
        q_copy.wait()

    def force(r, first):
        for z in range(planes):
            img = i2_ref[z + 1, r]
            half = 0.5 * (img - t_buf[z, r - start])
            ahead, behind = line.beside(img)
            slopes = (
                ahead - behind,
                i2_ref[z + 1, r + 1] - (0.0 if first else i2_ref[z + 1, r - 1]),
                i2_ref[z + 2, r] - i2_ref[z, r],
            )
            for c in range(3):
                at = c * planes + z
                q_ref[at, r - start + lead] = q_ref[at, r - start + lead] - half * slopes[c]

    over_rows(force, start, stop, top, UNROLL[3])
    size = q_ref.shape[1]
    if top:
        for n in range(3 * planes):
            for r in range(6):
                tail_ref[n, r] = q_ref[n, size - 6 + r]

    for z in range(planes):

        def body(c, carry, z=z):
            n = c * planes + z

            def store(r, row):
                r = r if top else r - 3
                if z > 0:
                    squp_ref[c * (planes - 1) + z - 1, r] = row
                if z < planes - 1:
                    sqdown_ref[c * (planes - 1) + z, r] = row

            smooth_rows(line, lambda r: q_ref[n, r], store, size, top)
            return carry

        lax.fori_loop(0, 3, body, 0)


def last_kernel(planes, up_ref, down_ref, lo_ref, hi_ref, out_ref):
    near = planes - 1

    def body(r, carry):
        for c in range(3):
            stack = [lo_ref[c * near + near - 3 + z, r] for z in range(3)]
            stack += [down_ref[c * near + z, r] for z in range(near)]
            stack += [up_ref[c * near + near - 1, r]]
            stack += [hi_ref[c * near + z, r] for z in range(3)]
            for z, plane in enumerate(smooth_planes(stack)):
                out_ref[c * planes + z, r] = plane
        return carry

    lax.fori_loop(0, up_ref.shape[1], body, 0)


ANY = pl.BlockSpec(memory_space=pl.ANY)


def call(kernel, specs, outs, scratch=(), copies=0, cost=0.0, inside=1 << 20):
    sizes = [4 * math.prod(o) for o in outs] * 2 + [4 * math.prod(o) for o in scratch]
    return pl.pallas_call(
        kernel,
        in_specs=specs,
        out_specs=[VMEM] * len(outs),
        out_shape=[jax.ShapeDtypeStruct(o, jnp.float32) for o in outs],
        scratch_shapes=[pltpu.VMEM(s, jnp.float32) for s in scratch]
        + ([pltpu.SemaphoreType.DMA((copies,))] if copies else []),
        compiler_params=pltpu.CompilerParams(vmem_limit_bytes=sum(sizes) + inside + (1 << 20)),
        cost_estimate=pl.CostEstimate(flops=0, transcendentals=0, bytes_accessed=int(cost * 3.3e6)),
    )


def shoot(momentum, template, target):
    planes, rows, width = template.shape
    cols = width // LANES
    halves = lax.axis_size("gy")
    count = lax.axis_size("gz") * halves
    flat = lax.axis_index("gz") * halves + lax.axis_index("gy")
    depth = 2 * (flat // 4) + flat % 2
    edge = jnp.stack([depth > 0, depth < count // 2 - 1]).astype(jnp.float32)
    flip = lax.axis_index("gy").reshape(1)
    swap, up, down = swap_pairs(count), up_pairs(count), down_pairs(count)
    tail = (cols, LANES)
    all_planes = 4 * planes
    mplanes = 3 * planes

    def send(cells, pairs):
        return lax.ppermute(cells, AXES, pairs)

    mom, img, tgt = tiled(momentum), tiled(template), tiled(target)
    near = 2 * SUB
    edge_rows = near * cols

    def border(cells):
        return jnp.where(
            lax.axis_index("gy") == 0, cells[..., -edge_rows:, :], cells[..., :edge_rows, :]
        )

    reach = 4 + 4 + 3
    total = [rows + reach, rows + reach - 4, rows + reach - 8, rows]
    cut = [13 * rows // 16]
    cut += [cut[0] - 4, cut[0] - 8, cut[0] - 11]

    edges = jnp.concatenate([border(mom), border(img)[None], border(tgt)[None]])
    halo = lax.ppermute(edges, "gy", [(0, 1), (1, 0)])

    def pack(comps, lead, start, stop, ins, outs):
        return call(
            functools.partial(pack_kernel, start, stop, rows, comps, lead),
            [SMEM] + [VMEM] * len(ins),
            [(len(comps) * planes + (planes if lead else 0), stop - start) + tail] + outs,
            cost=2, inside=10 << 20,
        )(flip, *ins)

    (a0,) = pack((0, 1), 0, 0, cut[0], (mom,), [])
    a0 = send(a0, swap)
    (a1,) = pack((2,), 2, 0, cut[0], (mom, img), [])
    a1 = send(a1, swap)
    b0, t0 = pack((0, 1, 2), 2, cut[0], total[0], (mom, img, tgt, halo), [(planes, total[2]) + tail])
    b0 = send(b0, swap)
    t0 = send(t0, swap)

    def exchange(chunk):
        size = chunk.shape[0] - 3
        return (chunk, send(chunk[1 : 1 + size], up), send(chunk[2 : 2 + size], down))

    z_a = (a0, send(a0, up), send(a0, down))
    z_a2, z_b = exchange(a1), exchange(b0)

    def first(chunks, parts, size):
        give = size - 4 - (0 if chunks == 1 else 4)
        return call(
            functools.partial(first_kernel, chunks, planes),
            [SMEM] + [ANY] * (3 * chunks + 3),
            [(mplanes + 2, give) + tail] * 2,
            [(all_planes, size) + tail] + [(mplanes + 1, size) + tail] * 2
            + [(3, planes + 2, size + 1) + tail, (3, planes + 2, size) + tail],
            copies=13 * chunks, cost=9,
        )(edge, *parts)

    up_a, down_a = first(1, [part for pair in zip(z_a, z_a2) for part in pair], cut[0])
    lo_a, hi_a = send(up_a, up), send(down_a, down)
    up_b, down_b = first(
        2, [part for pair in zip(z_a, z_a2, z_b) for part in pair], total[0] - cut[0] + OVERLAP
    )
    lo_b, hi_b = send(up_b, up), send(down_b, down)

    def second(chunks, parts, size, given, sq_rows, t_start, before):
        start = 0 if chunks == 1 else 4
        stop = size - 4
        lead = 0 if chunks == 1 else 6
        outs = [(all_planes, given) + tail] + [(3 * (planes - 1), sq_rows) + tail] * 2
        if chunks == 1:
            outs.append((mplanes, 6) + tail)
        return call(
            functools.partial(second_kernel, chunks, planes, (start, stop, t_start, given)),
            [SMEM, ANY] + [ANY] * (4 * chunks + len(before)),
            outs,
            [(mplanes + 2, size) + tail, (2, size) + tail, (mplanes + 2, size) + tail, (mplanes + 2, size) + tail]
            + [(3, planes + 2, size + 1) + tail, (3, planes + 2, size) + tail]
            + [(planes + 2, size) + tail, (mplanes, lead + stop - start) + tail, (planes, stop - start) + tail],
            copies=13 * chunks + 2, cost=11,
        )(edge, t0, *parts, *before)

    out_a, squp_a, sqdown_a, q_tail = second(
        1, (up_a, down_a, lo_a, hi_a), cut[1], cut[2], cut[3], 0, ()
    )
    out_a = send(out_a, swap)
    sqlo_a, sqhi_a = send(squp_a, up), send(sqdown_a, down)
    out_b, squp_b, sqdown_b = second(
        2, (up_a, up_b, down_a, down_b, lo_a, lo_b, hi_a, hi_b), total[1] - cut[1] + OVERLAP,
        rows - cut[2], rows - cut[3], cut[2], (q_tail,),
    )
    out_b = send(out_b, swap)
    sqlo_b, sqhi_b = send(squp_b, up), send(sqdown_b, down)

    def last(parts):
        return call(
            functools.partial(last_kernel, planes), [VMEM] * 4, [(mplanes, parts[0].shape[1]) + tail],
            cost=2, inside=6 << 20,
        )(*parts)[0]

    g_a = send(last((squp_a, sqdown_a, sqlo_a, sqhi_a)), swap)
    g_b = send(last((squp_b, sqdown_b, sqlo_b, sqhi_b)), swap)

    native = (rows * cols, LANES)
    m2, i2 = call(
        functools.partial(unpack_kernel, (cut[2], rows - cut[2]), ((0, 3), (mplanes, 1))),
        [SMEM, VMEM, VMEM], [(3, planes) + native, (planes,) + native], cost=2, inside=6 << 20,
    )(flip, out_a, out_b)
    (grad,) = call(
        functools.partial(unpack_kernel, (cut[3], rows - cut[3]), ((0, 3),)),
        [SMEM, VMEM, VMEM], [(3, planes) + native], cost=2, inside=6 << 20,
    )(flip, g_a, g_b)
    return untiled(m2, rows), untiled(i2, rows), untiled(grad, rows)


def solution(mesh):
    return jax.shard_map(
        shoot,
        mesh=mesh,
        in_specs=(
            P(None, ("groups", "gz"), "gy", None),
            P(("groups", "gz"), "gy", None),
            P(("groups", "gz"), "gy", None),
        ),
        out_specs=(
            P(None, ("groups", "gz"), "gy", None),
            P(("groups", "gz"), "gy", None),
            P(None, ("groups", "gz"), "gy", None),
        ),
        check_vma=False,
    )
```

```python
import functools
import math

import jax
import jax.numpy as jnp
from jax import lax
from jax.experimental import pallas as pl
from jax.experimental.pallas import tpu as pltpu
from jax.sharding import PartitionSpec as P

LANES = 128
SUB = 8

UNIT = 0.05
SCALE = UNIT * UNIT * UNIT
STEP_SIZE = 0.25
UNROLL = (4, 2, 1, 4)

AXES = ("gz", "gy")
VMEM = pl.BlockSpec(memory_space=pltpu.VMEM)
SMEM = pl.BlockSpec(memory_space=pltpu.SMEM)


def place(depth, half):
    return 4 * (depth // 2) + 2 * half + depth % 2


def swap_pairs(count):
    swapped = {1: 2, 2: 1}
    return [(i, 4 * (i // 4) + swapped.get(i % 4, i % 4)) for i in range(count)]


def up_pairs(count):
    return [(place(d, h), place(d + 1, h)) for h in range(2) for d in range(count // 2 - 1)]


def down_pairs(count):
    return [(b, a) for a, b in up_pairs(count)]


def tiled(cells):
    lead, (rows, width) = cells.shape[:-2], cells.shape[-2:]
    cells = cells.reshape(lead + (rows // SUB, SUB, width // LANES, LANES))
    cells = jnp.swapaxes(cells, -2, -3)
    return cells.reshape(lead + (rows * width // LANES, LANES))


def untiled(cells, rows):
    lead, (total, lanes) = cells.shape[:-2], cells.shape[-2:]
    cols = total // rows
    cells = cells.reshape(lead + (rows // SUB, cols, SUB, LANES))
    cells = jnp.swapaxes(cells, -2, -3)
    return cells.reshape(lead + (rows, cols * LANES))


class Line:
    def __init__(self, cols):
        self.cols = cols
        lane = lax.broadcasted_iota(jnp.int32, (cols, LANES), 1)
        sub = lax.broadcasted_iota(jnp.int32, (cols, LANES), 0)
        self.first, self.last = sub == 0, sub == cols - 1
        self.at_start, self.near_start = lane == 0, lane < 2
        self.at_end, self.near_end = lane == LANES - 1, lane >= LANES - 2

    def beside(self, row):
        ahead = pltpu.roll(row, LANES - 1, 1)
        ahead = jnp.where(
            self.at_end, jnp.where(self.last, 0.0, pltpu.roll(ahead, self.cols - 1, 0)), ahead
        )
        behind = pltpu.roll(row, 1, 1)
        behind = jnp.where(
            self.at_start, jnp.where(self.first, 0.0, pltpu.roll(behind, 1, 0)), behind
        )
        return ahead, behind

    def smooth(self, row):
        ahead, behind = self.beside(row)
        mid = (ahead + behind) + (row + row)
        high = pltpu.roll(mid, LANES - 2, 1)
        high = jnp.where(
            self.near_end, jnp.where(self.last, ahead, pltpu.roll(high, self.cols - 1, 0)), high
        )
        low = pltpu.roll(mid, 2, 1)
        low = jnp.where(
            self.near_start, jnp.where(self.first, behind, pltpu.roll(low, 1, 0)), low
        )
        return 3.0 * mid + (low + high)


def smooth_rows(line, load, store, count, top):
    last = line.smooth(load(0))
    pairs = last if top else None
    sums = {-2: None, -1: last if top else None}
    for r in range(1, count):
        here = line.smooth(load(r))
        nxt = last + here
        sums[r - 1] = None if pairs is None else pairs + nxt
        last, pairs = here, nxt
        done = r - 3
        if done >= (0 if top else 3):
            out = 3.0 * sums[done] + sums[done + 2]
            store(done, out if sums[done - 2] is None else out + sums[done - 2])


def smooth_planes(planes, scale=SCALE):
    pairs = [a + b for a, b in zip(planes, planes[1:])]
    sums = [a + b for a, b in zip(pairs, pairs[1:])]
    out = [3.0 * mid + (low + high) for low, mid, high in zip(sums, sums[2:], sums[4:])]
    return out if scale == 1.0 else [scale * row for row in out]


def spot(row, cols):
    return (row // SUB) * SUB * cols + row % SUB


def mirrored(row, rows, cols, flip):
    a, b = spot(row, cols), spot(rows - 1 - row, cols)
    return a + flip * (b - a)


def pack_kernel(first, stop, rows, comps, lead, flip_ref, m_ref, *refs):
    i_ref, t_ref, halo_ref, out_ref, tout_ref = {
        1: (None, None, None, *refs, None), 2: (refs[0], None, None, refs[-1], None)
    }.get(len(refs), refs)
    cols = out_ref.shape[-2]
    planes = m_ref.shape[1]
    flip = flip_ref[0]
    sign = (1 - 2 * flip).astype(jnp.float32)

    def copy(src, halo, dst, start, end, factor):
        for r in range(start, end):
            if r < rows:
                row = src[pl.ds(mirrored(r, rows, cols, flip), cols, stride=SUB), :]
            else:
                at = mirrored(r - rows, halo.shape[0] // cols, cols, flip)
                row = halo[pl.ds(at, cols, stride=SUB), :]
            dst[r - start] = row if factor is None else row * factor

    def halo_at(n, z):
        return None if halo_ref is None else halo_ref.at[n, z]

    def body(z, carry):
        for n, comp in enumerate(comps):
            copy(
                m_ref.at[comp, z], halo_at(comp, z), out_ref.at[lead + n * planes + z], first, stop,
                sign if comp == 1 else None,
            )
        if lead:
            spare = jnp.where(z < 2, len(comps) * planes + 2 + z, z - (planes - 2))
            copy(i_ref.at[z], halo_at(3, z), out_ref.at[spare], first, stop, None)
        if t_ref is not None:
            copy(t_ref.at[z], halo_at(4, z), tout_ref.at[z], 0, tout_ref.shape[1], None)
        return carry

    lax.fori_loop(0, planes, body, 0)


def unpack_kernel(counts, parts, flip_ref, *refs):
    ins, outs = refs[: len(counts)], refs[len(counts) :]
    rows = sum(counts)
    flip = flip_ref[0]
    sign = (1 - 2 * flip).astype(jnp.float32)
    cols = ins[0].shape[-2]

    for out, (offset, components) in zip(outs, parts):
        planes = out.shape[-3]
        for comp in range(components):
            dst = out.at[comp] if len(out.shape) == 4 else out

            def body(z, carry, comp=comp, dst=dst, offset=offset, planes=planes):
                done = 0
                for ref, count in zip(ins, counts):
                    for r in range(count):
                        row = ref[offset + comp * planes + z, r]
                        at = mirrored(done + r, rows, cols, flip)
                        dst[z, pl.ds(at, cols, stride=SUB), :] = row * sign if comp == 1 else row
                    done += count
                return carry

            lax.fori_loop(0, planes, body, 0)


class Both:
    def __init__(self, copies):
        self.copies = copies

    def wait(self):
        for copy in self.copies:
            copy.wait()


class Fetcher:
    def __init__(self, sems):
        self.sems, self.used = sems, 0

    def __call__(self, parts, buf, target, count):
        copies, row = [], 0
        for ref, start, plane in parts:
            rows = ref.shape[1] - start
            copy = pltpu.make_async_copy(
                ref.at[pl.ds(plane, count), pl.ds(start, rows)],
                buf.at[pl.ds(target, count), pl.ds(row, rows)],
                self.sems.at[self.used],
            )
            copy.start()
            copies.append(copy)
            self.used += 1
            row += rows
        return Both(copies)


OVERLAP = 8


def parts_of(refs, chunks, n, plane):
    refs = refs[n * chunks : (n + 1) * chunks]
    return [
        (ref, ref.shape[1] - OVERLAP if n + 1 < chunks else 0, plane) for n, ref in enumerate(refs)
    ]


def wait(copies):
    for copy in copies:
        copy.wait()


def velocity(line, edge_ref, blocks, image_copies, s_ref, v_ref, top):
    planes = v_ref.shape[1] - 2
    count = blocks[0][1].shape[1]
    zero = jnp.zeros(v_ref.shape[-2:], jnp.float32)

    for comp in range(3):
        for copies, _, _ in blocks:
            copies[comp].wait()

        def rows(r, carry, comp=comp):
            last, pairs = carry
            stack = [ref[offset + comp * planes + z, r] for _, ref, offset in blocks for z in range(planes)]
            here = smooth_planes(stack[planes - 4 : 2 * planes + 4], 1.0)
            nxt = [a + b for a, b in zip(last, here)]
            for z in range(planes + 2):
                s_ref[comp, z, r + 1] = pairs[z] + nxt[z]
            return here, nxt

        empty = [zero] * (planes + 2)
        lax.fori_loop(0, count, rows, (empty, empty), unroll=UNROLL[0])
        if top:
            for z in range(planes + 2):
                s_ref[comp, z, 0] = zero

    scales = [SCALE * edge_ref[0]] + [SCALE] * planes + [SCALE * edge_ref[1]]

    def finish(r, carry):
        for comp in range(3):
            for z in range(planes + 2):
                row = 3.0 * s_ref[comp, z, r + 2] + (s_ref[comp, z, r] + s_ref[comp, z, r + 4])
                v_ref[comp, z, r] = scales[z] * line.smooth(row)
        return carry

    lax.fori_loop(0 if top else 3, count - 3, finish, 0, unroll=UNROLL[1])
    wait(image_copies)


def change(speed, f, around):
    total = None
    for (rise, fall), (upper, lower) in zip(speed, around):
        up = rise * (f - lower if lower is not None else f)
        down = fall * (upper - f)
        total = up + down if total is None else total + (up + down)
    return total


def advance(line, v_ref, momentum, image, z, r, first):
    velo = [v_ref[c, z + 1, r] for c in range(3)]
    speed = [(jnp.maximum(v, 0.0), jnp.minimum(v, 0.0)) for v in velo]

    def around(load):
        mid = load(z, r)
        return mid, [
            line.beside(mid),
            (load(z, r + 1), None if first else load(z, r - 1)),
            (load(z + 1, r), load(z - 1, r)),
        ]

    new_image = None
    if image is not None:
        mid, sides = around(image)
        new_image = mid - STEP_SIZE * change(speed, mid, sides)
    if momentum is None:
        return None, new_image

    slopes = []
    for comp in range(3):
        ahead, behind = line.beside(velo[comp])
        slopes.append(
            (
                ahead - behind,
                v_ref[comp, z + 1, r + 1] - (0.0 if first else v_ref[comp, z + 1, r - 1]),
                v_ref[comp, z + 2, r] - v_ref[comp, z, r],
            )
        )
    divergence = slopes[0][0] + slopes[1][1] + slopes[2][2]
    fields = [around(load) for load in momentum]
    mids = [mid for mid, _ in fields]
    new = []
    for comp in range(3):
        mid, sides = fields[comp]
        stretch = mid * divergence
        for other in range(3):
            stretch = stretch + mids[other] * slopes[other][comp]
        moved = change(speed, mid, sides)
        new.append(mid - (STEP_SIZE * moved + (0.5 * STEP_SIZE) * stretch))
    return new, new_image


def over_rows(body, start, stop, top, unroll=1):
    if top and start == 0:
        body(0, True)
        start = 1

    def step(r, carry):
        body(r, False)
        return carry

    lax.fori_loop(start, stop, step, 0, unroll=unroll)


def momentum_at(own, lo, hi, offsets, planes):
    def at(comp):
        def load(z, r):
            if z < 0:
                return lo[offsets[0] + comp * planes + planes + z, r]
            if z >= planes:
                return hi[offsets[2] + comp * planes + z - planes, r]
            return own[offsets[1] + comp * planes + z, r]

        return load

    return [at(comp) for comp in range(3)]


def first_kernel(chunks, planes, edge_ref, *refs):
    top = chunks == 1
    each = chunks + 1
    ins, (up_ref, down_ref), scratch = refs[: 3 * each], refs[3 * each :][:2], refs[3 * each + 2 :]
    own, lo, hi, s_ref, v_ref, sems = scratch
    fetch = Fetcher(sems)

    def sources(block, first_chunk, plane):
        refs = ins[block * each : (block + 1) * each]
        which, at = first_chunk
        parts = [(refs[which], 0 if top else refs[which].shape[1] - OVERLAP, at)]
        return parts if top else parts + [(refs[2], 0, plane)]

    blocks = [(1, lo, 1), (0, own, 2), (2, hi, 0)]
    copies = [[], [], []]
    for comp in range(3):
        for n, (at, buf, offset) in enumerate(blocks):
            plane = offset + comp * planes
            first_chunk = (0, comp * planes) if comp < 2 else (1, offset)
            copies[n].append(fetch(sources(at, first_chunk, plane), buf, plane, planes))
    late = 2 * planes
    image_copies = [
        fetch(sources(at, (1, plane if plane == 0 else plane - late), plane), buf, plane, count)
        for at, buf, plane, count in (
            (0, own, 0, 2), (0, own, 3 * planes + 2, 2), (1, lo, 0, 1), (2, hi, 3 * planes, 1),
        )
    ]
    line = Line(own.shape[-2])

    def image(z, r):
        if z < 0:
            return lo[0, r]
        if z >= planes:
            return hi[3 * planes, r]
        return own[3 * planes + 2 + z, r] if z < 2 else own[z - (planes - 2), r]

    velocity(
        line, edge_ref, [(c, buf, offset) for c, (_, buf, offset) in zip(copies, blocks)],
        image_copies, s_ref, v_ref, top,
    )
    momentum = momentum_at(own, lo, hi, (1, 2, 0), planes)
    start = 0 if top else 4

    def body(r, first):
        for z in range(planes):
            new, img = advance(line, v_ref, momentum, image, z, r, first)
            for c in range(3):
                up_ref[2 + c * planes + z, r - start] = new[c]
                down_ref[c * planes + z, r - start] = new[c]
            if z < 2:
                down_ref[3 * planes + z, r - start] = img
            else:
                up_ref[z - (planes - 2), r - start] = img

    over_rows(body, start, own.shape[1] - 4, top)


def second_kernel(chunks, planes, rows, edge_ref, *refs):
    top = chunks == 1
    start, stop, given = rows
    ins, refs = refs[: 4 * chunks], refs[4 * chunks :]
    out_ref, m2_ref, i2_ref, own, down, lo, hi, s_ref, v_ref, sems = refs
    fetch = Fetcher(sems)
    blocks = [(2, lo, 2), (0, own, 2), (3, hi, 0)]
    copies = [[], [], []]
    for comp in range(3):
        for n, (at, buf, offset) in enumerate(blocks):
            plane = offset + comp * planes
            copies[n].append(fetch(parts_of(ins, chunks, at, plane), buf, plane, planes))
    image_copies = [
        fetch(parts_of(ins, chunks, at, plane), buf, target, 2)
        for at, buf, plane, target in (
            (0, own, 0, 0), (1, down, 3 * planes, 0), (2, lo, 0, 0), (3, hi, 3 * planes, 3 * planes),
        )
    ]
    line = Line(own.shape[-2])

    def image(z, r):
        if z < 0:
            return lo[2 + z, r]
        if z >= planes:
            return hi[3 * planes + z - planes, r]
        return down[z, r] if z < 2 else own[z - (planes - 2), r]

    velocity(
        line, edge_ref, [(c, buf, offset) for c, (_, buf, offset) in zip(copies, blocks)],
        image_copies, s_ref, v_ref, top,
    )
    momentum = momentum_at(own, lo, hi, (2, 2, 0), planes)

    def image_row(zs, r, first=False):
        for z in zs:
            i2_ref[z + 1, r - start + 1] = advance(line, v_ref, None, image, z, r, first)[1]

    def step(keep, r, first):
        for z in range(planes):
            new, img = advance(line, v_ref, momentum, image, z, r, first)
            for c in range(3):
                m2_ref[c * planes + z, r - start] = new[c]
                if keep:
                    out_ref[c * planes + z, r - start] = new[c]
            i2_ref[z + 1, r - start + 1] = img
            if keep:
                out_ref[3 * planes + z, r - start] = img
        image_row((-1, planes), r, first)

    if top:
        for z in range(planes):
            i2_ref[z + 1, 0] = jnp.zeros_like(i2_ref[z + 1, 0])
    else:
        image_row(range(planes), start - 1)
    over_rows(functools.partial(step, True), start, start + given, top)
    if start + given < stop:
        over_rows(functools.partial(step, False), start + given, stop, top)
    image_row(range(planes), stop)


def force_kernel(top, planes, t_start, m2_ref, i2_ref, t_ref, *refs):
    if top:
        squp_ref, sqdown_ref, tail_ref, q_ref = refs
        lead = 0
    else:
        before_ref, squp_ref, sqdown_ref, q_ref = refs
        lead = before_ref.shape[1]
        for n in range(3 * planes):
            for r in range(lead):
                q_ref[n, r] = before_ref[n, r]
    line = Line(m2_ref.shape[-2])

    def force(r, carry):
        for z in range(planes):
            img = i2_ref[z + 1, r + 1]
            half = 0.5 * (img - t_ref[z, t_start + r])
            ahead, behind = line.beside(img)
            slopes = (
                ahead - behind,
                i2_ref[z + 1, r + 2] - i2_ref[z + 1, r],
                i2_ref[z + 2, r + 1] - i2_ref[z, r + 1],
            )
            for c in range(3):
                at = c * planes + z
                q_ref[at, r + lead] = m2_ref[at, r] - half * slopes[c]
        return carry

    lax.fori_loop(0, m2_ref.shape[1], force, 0, unroll=UNROLL[3])
    size = q_ref.shape[1]
    if top:
        for n in range(3 * planes):
            for r in range(6):
                tail_ref[n, r] = q_ref[n, size - 6 + r]

    for z in range(planes):

        def body(c, carry, z=z):
            n = c * planes + z

            def store(r, row):
                r = r if top else r - 3
                if z > 0:
                    squp_ref[c * (planes - 1) + z - 1, r] = row
                if z < planes - 1:
                    sqdown_ref[c * (planes - 1) + z, r] = row

            smooth_rows(line, lambda r: q_ref[n, r], store, size, top)
            return carry

        lax.fori_loop(0, 3, body, 0)


def last_kernel(planes, up_ref, down_ref, lo_ref, hi_ref, out_ref):
    near = planes - 1

    def body(r, carry):
        for c in range(3):
            stack = [lo_ref[c * near + near - 3 + z, r] for z in range(3)]
            stack += [down_ref[c * near + z, r] for z in range(near)]
            stack += [up_ref[c * near + near - 1, r]]
            stack += [hi_ref[c * near + z, r] for z in range(3)]
            for z, plane in enumerate(smooth_planes(stack)):
                out_ref[c * planes + z, r] = plane
        return carry

    lax.fori_loop(0, up_ref.shape[1], body, 0)


ANY = pl.BlockSpec(memory_space=pl.ANY)


def call(kernel, specs, outs, scratch=(), copies=0, cost=0.0, inside=1 << 20):
    sizes = [4 * math.prod(o) for o in outs] * 2 + [4 * math.prod(o) for o in scratch]
    return pl.pallas_call(
        kernel,
        in_specs=specs,
        out_specs=[VMEM] * len(outs),
        out_shape=[jax.ShapeDtypeStruct(o, jnp.float32) for o in outs],
        scratch_shapes=[pltpu.VMEM(s, jnp.float32) for s in scratch]
        + ([pltpu.SemaphoreType.DMA((copies,))] if copies else []),
        compiler_params=pltpu.CompilerParams(vmem_limit_bytes=sum(sizes) + inside + (1 << 20)),
        cost_estimate=pl.CostEstimate(flops=0, transcendentals=0, bytes_accessed=int(cost * 3.3e6)),
    )


def shoot(momentum, template, target):
    planes, rows, width = template.shape
    cols = width // LANES
    halves = lax.axis_size("gy")
    count = lax.axis_size("gz") * halves
    flat = lax.axis_index("gz") * halves + lax.axis_index("gy")
    depth = 2 * (flat // 4) + flat % 2
    edge = jnp.stack([depth > 0, depth < count // 2 - 1]).astype(jnp.float32)
    flip = lax.axis_index("gy").reshape(1)
    swap, up, down = swap_pairs(count), up_pairs(count), down_pairs(count)
    tail = (cols, LANES)
    all_planes = 4 * planes
    mplanes = 3 * planes

    def send(cells, pairs):
        return lax.ppermute(cells, AXES, pairs)

    mom, img, tgt = tiled(momentum), tiled(template), tiled(target)
    near = 2 * SUB
    edge_rows = near * cols

    def border(cells):
        return jnp.where(
            lax.axis_index("gy") == 0, cells[..., -edge_rows:, :], cells[..., :edge_rows, :]
        )

    reach = 4 + 4 + 3
    total = [rows + reach, rows + reach - 4, rows + reach - 8, rows]
    cut = [13 * rows // 16]
    cut += [cut[0] - 4, cut[0] - 8, cut[0] - 11]

    edges = jnp.concatenate([border(mom), border(img)[None], border(tgt)[None]])
    halo = lax.ppermute(edges, "gy", [(0, 1), (1, 0)])

    def pack(comps, lead, start, stop, ins, outs):
        return call(
            functools.partial(pack_kernel, start, stop, rows, comps, lead),
            [SMEM] + [VMEM] * len(ins),
            [(len(comps) * planes + (planes if lead else 0), stop - start) + tail] + outs,
            cost=2, inside=10 << 20,
        )(flip, *ins)

    (a0,) = pack((0, 1), 0, 0, cut[0], (mom,), [])
    a0 = send(a0, swap)
    (a1,) = pack((2,), 2, 0, cut[0], (mom, img), [])
    a1 = send(a1, swap)
    b0, t0 = pack((0, 1, 2), 2, cut[0], total[0], (mom, img, tgt, halo), [(planes, total[2]) + tail])
    b0 = send(b0, swap)
    t0 = send(t0, swap)

    def exchange(chunk):
        size = chunk.shape[0] - 3
        return (chunk, send(chunk[1 : 1 + size], up), send(chunk[2 : 2 + size], down))

    z_a = (a0, send(a0, up), send(a0, down))
    z_a2, z_b = exchange(a1), exchange(b0)

    def first(chunks, parts, size):
        give = size - 4 - (0 if chunks == 1 else 4)
        return call(
            functools.partial(first_kernel, chunks, planes),
            [SMEM] + [ANY] * (3 * chunks + 3),
            [(mplanes + 2, give) + tail] * 2,
            [(all_planes, size) + tail] + [(mplanes + 1, size) + tail] * 2
            + [(3, planes + 2, size + 1) + tail, (3, planes + 2, size) + tail],
            copies=13 * chunks, cost=9,
        )(edge, *parts)

    up_a, down_a = first(1, [part for pair in zip(z_a, z_a2) for part in pair], cut[0])
    lo_a, hi_a = send(up_a, up), send(down_a, down)
    up_b, down_b = first(
        2, [part for pair in zip(z_a, z_a2, z_b) for part in pair], total[0] - cut[0] + OVERLAP
    )
    lo_b, hi_b = send(up_b, up), send(down_b, down)

    def second(chunks, parts, size, given):
        start, stop = (0 if chunks == 1 else 4), size - 4
        return call(
            functools.partial(second_kernel, chunks, planes, (start, stop, given)),
            [SMEM] + [ANY] * (4 * chunks),
            [(all_planes, given) + tail, (mplanes, stop - start) + tail, (planes + 2, stop - start + 2) + tail],
            [(mplanes + 2, size) + tail, (2, size) + tail, (mplanes + 2, size) + tail, (mplanes + 2, size) + tail]
            + [(3, planes + 2, size + 1) + tail, (3, planes + 2, size) + tail],
            copies=13 * chunks, cost=9,
        )(edge, *parts)

    def force(m2, i2, t_start, before, sq_rows):
        outs = [(3 * (planes - 1), sq_rows) + tail] * 2 + ([] if before else [(mplanes, 6) + tail])
        lead = 6 if before else 0
        return call(
            functools.partial(force_kernel, not before, planes, t_start),
            [VMEM] * (3 + len(before)), outs, [(mplanes, lead + m2.shape[1]) + tail],
            cost=3, inside=8 << 20,
        )(m2, i2, t0, *before)

    out_a, m2_a, i2_a = second(1, (up_a, down_a, lo_a, hi_a), cut[1], cut[2])
    out_a = send(out_a, swap)
    squp_a, sqdown_a, q_tail = force(m2_a, i2_a, 0, (), cut[3])
    sqlo_a, sqhi_a = send(squp_a, up), send(sqdown_a, down)
    out_b, m2_b, i2_b = second(
        2, (up_a, up_b, down_a, down_b, lo_a, lo_b, hi_a, hi_b), total[1] - cut[1] + OVERLAP, rows - cut[2]
    )
    out_b = send(out_b, swap)
    squp_b, sqdown_b = force(m2_b, i2_b, cut[2], (q_tail,), rows - cut[3])
    sqlo_b, sqhi_b = send(squp_b, up), send(sqdown_b, down)

    def last(parts):
        return call(
            functools.partial(last_kernel, planes), [VMEM] * 4, [(mplanes, parts[0].shape[1]) + tail],
            cost=2, inside=6 << 20,
        )(*parts)[0]

    g_a = send(last((squp_a, sqdown_a, sqlo_a, sqhi_a)), swap)
    g_b = send(last((squp_b, sqdown_b, sqlo_b, sqhi_b)), swap)

    native = (rows * cols, LANES)
    m2, i2 = call(
        functools.partial(unpack_kernel, (cut[2], rows - cut[2]), ((0, 3), (mplanes, 1))),
        [SMEM, VMEM, VMEM], [(3, planes) + native, (planes,) + native], cost=2, inside=6 << 20,
    )(flip, out_a, out_b)
    (grad,) = call(
        functools.partial(unpack_kernel, (cut[3], rows - cut[3]), ((0, 3),)),
        [SMEM, VMEM, VMEM], [(3, planes) + native], cost=2, inside=6 << 20,
    )(flip, g_a, g_b)
    return untiled(m2, rows), untiled(i2, rows), untiled(grad, rows)


def solution(mesh):
    return jax.shard_map(
        shoot,
        mesh=mesh,
        in_specs=(
            P(None, ("groups", "gz"), "gy", None),
            P(("groups", "gz"), "gy", None),
            P(("groups", "gz"), "gy", None),
        ),
        out_specs=(
            P(None, ("groups", "gz"), "gy", None),
            P(("groups", "gz"), "gy", None),
            P(None, ("groups", "gz"), "gy", None),
        ),
        check_vma=False,
    )
```

```python
import functools
import math

import jax
import jax.numpy as jnp
from jax import lax
from jax.experimental import pallas as pl
from jax.experimental.pallas import tpu as pltpu
from jax.sharding import PartitionSpec as P

LANES = 128
SUB = 8

UNIT = 0.05
SCALE = UNIT * UNIT * UNIT
STEP_SIZE = 0.25
UNROLL = (4, 2, 1, 4)

AXES = ("gz", "gy")
VMEM = pl.BlockSpec(memory_space=pltpu.VMEM)
SMEM = pl.BlockSpec(memory_space=pltpu.SMEM)


def place(depth, half):
    return 4 * (depth // 2) + 2 * half + depth % 2


def swap_pairs(count):
    swapped = {1: 2, 2: 1}
    return [(i, 4 * (i // 4) + swapped.get(i % 4, i % 4)) for i in range(count)]


def beside_pairs(count, first):
    pairs = [
        (place(d, h), place(d + 1, h)) for h in range(2) for d in range(first, count // 2 - 1, 2)
    ]
    return pairs + [(b, a) for a, b in pairs]


def tiled(cells):
    lead, (rows, width) = cells.shape[:-2], cells.shape[-2:]
    cells = cells.reshape(lead + (rows // SUB, SUB, width // LANES, LANES))
    cells = jnp.swapaxes(cells, -2, -3)
    return cells.reshape(lead + (rows * width // LANES, LANES))


def untiled(cells, rows):
    lead, (total, lanes) = cells.shape[:-2], cells.shape[-2:]
    cols = total // rows
    cells = cells.reshape(lead + (rows // SUB, cols, SUB, LANES))
    cells = jnp.swapaxes(cells, -2, -3)
    return cells.reshape(lead + (rows, cols * LANES))


class Line:
    def __init__(self, cols):
        self.cols = cols
        lane = lax.broadcasted_iota(jnp.int32, (cols, LANES), 1)
        sub = lax.broadcasted_iota(jnp.int32, (cols, LANES), 0)
        self.first, self.last = sub == 0, sub == cols - 1
        self.at_start, self.near_start = lane == 0, lane < 2
        self.at_end, self.near_end = lane == LANES - 1, lane >= LANES - 2

    def beside(self, row):
        ahead = pltpu.roll(row, LANES - 1, 1)
        ahead = jnp.where(
            self.at_end, jnp.where(self.last, 0.0, pltpu.roll(ahead, self.cols - 1, 0)), ahead
        )
        behind = pltpu.roll(row, 1, 1)
        behind = jnp.where(
            self.at_start, jnp.where(self.first, 0.0, pltpu.roll(behind, 1, 0)), behind
        )
        return ahead, behind

    def smooth(self, row):
        ahead, behind = self.beside(row)
        mid = (ahead + behind) + (row + row)
        high = pltpu.roll(mid, LANES - 2, 1)
        high = jnp.where(
            self.near_end, jnp.where(self.last, ahead, pltpu.roll(high, self.cols - 1, 0)), high
        )
        low = pltpu.roll(mid, 2, 1)
        low = jnp.where(
            self.near_start, jnp.where(self.first, behind, pltpu.roll(low, 1, 0)), low
        )
        return 3.0 * mid + (low + high)


def smooth_rows(line, load, store, count, top):
    last = line.smooth(load(0))
    pairs = last if top else None
    sums = {-2: None, -1: last if top else None}
    for r in range(1, count):
        here = line.smooth(load(r))
        nxt = last + here
        sums[r - 1] = None if pairs is None else pairs + nxt
        last, pairs = here, nxt
        done = r - 3
        if done >= (0 if top else 3):
            out = 3.0 * sums[done] + sums[done + 2]
            store(done, out if sums[done - 2] is None else out + sums[done - 2])


def smooth_planes(planes, scale=SCALE):
    pairs = [a + b for a, b in zip(planes, planes[1:])]
    sums = [a + b for a, b in zip(pairs, pairs[1:])]
    out = [3.0 * mid + (low + high) for low, mid, high in zip(sums, sums[2:], sums[4:])]
    return out if scale == 1.0 else [scale * row for row in out]


def spot(row, cols):
    return (row // SUB) * SUB * cols + row % SUB


def mirrored(row, rows, cols, flip):
    a, b = spot(row, cols), spot(rows - 1 - row, cols)
    return a + flip * (b - a)


def pack_kernel(first, stop, rows, comps, with_image, flip_ref, m_ref, *refs):
    i_ref, t_ref, halo_ref, out_ref, tout_ref = {
        1: (None, None, None, *refs, None), 2: (refs[0], None, None, refs[-1], None)
    }.get(len(refs), refs)
    cols = out_ref.shape[-2]
    planes = m_ref.shape[1]
    flip = flip_ref[0]
    sign = (1 - 2 * flip).astype(jnp.float32)

    def copy(src, halo, dst, start, end, factor):
        for r in range(start, end):
            if r < rows:
                row = src[pl.ds(mirrored(r, rows, cols, flip), cols, stride=SUB), :]
            else:
                at = mirrored(r - rows, halo.shape[0] // cols, cols, flip)
                row = halo[pl.ds(at, cols, stride=SUB), :]
            dst[r - start] = row if factor is None else row * factor

    def halo_at(n, z):
        return None if halo_ref is None else halo_ref.at[n, z]

    def body(z, carry):
        for n, comp in enumerate(comps):
            copy(
                m_ref.at[comp, z], halo_at(comp, z), out_ref.at[n * planes + z], first, stop,
                sign if comp == 1 else None,
            )
        if with_image:
            at = len(comps) * planes + z
            copy(i_ref.at[z], halo_at(3, z), out_ref.at[at], first, stop, None)
        if t_ref is not None:
            copy(t_ref.at[z], halo_at(4, z), tout_ref.at[z], 0, tout_ref.shape[1], None)
        return carry

    lax.fori_loop(0, planes, body, 0)


def unpack_kernel(counts, parts, flip_ref, *refs):
    ins, outs = refs[: len(counts)], refs[len(counts) :]
    rows = sum(counts)
    flip = flip_ref[0]
    sign = (1 - 2 * flip).astype(jnp.float32)
    cols = ins[0].shape[-2]

    for out, (offset, components) in zip(outs, parts):
        planes = out.shape[-3]
        for comp in range(components):
            dst = out.at[comp] if len(out.shape) == 4 else out

            def body(z, carry, comp=comp, dst=dst, offset=offset, planes=planes):
                done = 0
                for ref, count in zip(ins, counts):
                    for r in range(count):
                        row = ref[offset + comp * planes + z, r]
                        at = mirrored(done + r, rows, cols, flip)
                        dst[z, pl.ds(at, cols, stride=SUB), :] = row * sign if comp == 1 else row
                    done += count
                return carry

            lax.fori_loop(0, planes, body, 0)


class Both:
    def __init__(self, copies):
        self.copies = copies

    def wait(self):
        for copy in self.copies:
            copy.wait()


class Fetcher:
    def __init__(self, sems, odd):
        self.sems, self.odd, self.used = sems, odd, 0

    def __call__(self, parts, buf, target, count):
        copies, row = [], 0
        for (even, odd), start, plane in parts:
            rows = even.shape[1] - start

            def copy_of(ref):
                return pltpu.make_async_copy(
                    ref.at[pl.ds(plane, count), pl.ds(start, rows)],
                    buf.at[pl.ds(target, count), pl.ds(row, rows)],
                    self.sems.at[self.used],
                )

            if even is odd:
                copy_of(even).start()
            else:
                pl.when(self.odd == 0)(lambda: copy_of(even).start())
                pl.when(self.odd == 1)(lambda: copy_of(odd).start())
            copies.append(copy_of(even))
            self.used += 1
            row += rows
        return Both(copies)


OVERLAP = 8


LOWER, UPPER = (2, 1), (1, 2)


def wait(copies):
    for copy in copies:
        copy.wait()


def velocity(line, edge_ref, blocks, image_copies, s_ref, v_ref, top):
    planes = v_ref.shape[1] - 2
    count = blocks[0][1].shape[1]
    zero = jnp.zeros(v_ref.shape[-2:], jnp.float32)

    for comp in range(3):
        for copies, _, _ in blocks:
            copies[comp].wait()

        def rows(r, carry, comp=comp):
            last, pairs = carry
            stack = [ref[offset + comp * planes + z, r] for _, ref, offset in blocks for z in range(planes)]
            here = smooth_planes(stack[planes - 4 : 2 * planes + 4], 1.0)
            nxt = [a + b for a, b in zip(last, here)]
            for z in range(planes + 2):
                s_ref[comp, z, r + 1] = pairs[z] + nxt[z]
            return here, nxt

        empty = [zero] * (planes + 2)
        lax.fori_loop(0, count, rows, (empty, empty), unroll=UNROLL[0])
        if top:
            for z in range(planes + 2):
                s_ref[comp, z, 0] = zero

    scales = [SCALE * edge_ref[0]] + [SCALE] * planes + [SCALE * edge_ref[1]]

    def finish(r, carry):
        for comp in range(3):
            for z in range(planes + 2):
                row = 3.0 * s_ref[comp, z, r + 2] + (s_ref[comp, z, r] + s_ref[comp, z, r + 4])
                v_ref[comp, z, r] = scales[z] * line.smooth(row)
        return carry

    lax.fori_loop(0 if top else 3, count - 3, finish, 0, unroll=UNROLL[1])
    wait(image_copies)


def change(speed, f, around):
    total = None
    for (rise, fall), (upper, lower) in zip(speed, around):
        up = rise * (f - lower if lower is not None else f)
        down = fall * (upper - f)
        total = up + down if total is None else total + (up + down)
    return total


def advance(line, v_ref, momentum, image, z, r, first):
    velo = [v_ref[c, z + 1, r] for c in range(3)]
    speed = [(jnp.maximum(v, 0.0), jnp.minimum(v, 0.0)) for v in velo]

    def around(load):
        mid = load(z, r)
        return mid, [
            line.beside(mid),
            (load(z, r + 1), None if first else load(z, r - 1)),
            (load(z + 1, r), load(z - 1, r)),
        ]

    new_image = None
    if image is not None:
        mid, sides = around(image)
        new_image = mid - STEP_SIZE * change(speed, mid, sides)
    if momentum is None:
        return None, new_image

    slopes = []
    for comp in range(3):
        ahead, behind = line.beside(velo[comp])
        slopes.append(
            (
                ahead - behind,
                v_ref[comp, z + 1, r + 1] - (0.0 if first else v_ref[comp, z + 1, r - 1]),
                v_ref[comp, z + 2, r] - v_ref[comp, z, r],
            )
        )
    divergence = slopes[0][0] + slopes[1][1] + slopes[2][2]
    fields = [around(load) for load in momentum]
    mids = [mid for mid, _ in fields]
    new = []
    for comp in range(3):
        mid, sides = fields[comp]
        stretch = mid * divergence
        for other in range(3):
            stretch = stretch + mids[other] * slopes[other][comp]
        moved = change(speed, mid, sides)
        new.append(mid - (STEP_SIZE * moved + (0.5 * STEP_SIZE) * stretch))
    return new, new_image


def over_rows(body, start, stop, top, unroll=1):
    if top and start == 0:
        body(0, True)
        start = 1

    def step(r, carry):
        body(r, False)
        return carry

    lax.fori_loop(start, stop, step, 0, unroll=unroll)


def momentum_at(own, lo, hi, planes):
    def at(comp):
        first = comp * planes

        def load(z, r):
            if z < 0:
                return lo[first + planes + z, r]
            if z >= planes:
                return hi[first + z - planes, r]
            return own[first + z, r]

        return load

    return [at(comp) for comp in range(3)]


def first_kernel(chunks, planes, edge_ref, odd_ref, *refs):
    top = chunks == 1
    each = chunks + 1
    ins, (near_ref, far_ref), scratch = refs[: 3 * each], refs[3 * each :][:2], refs[3 * each + 2 :]
    own, lo, hi, s_ref, v_ref, sems = scratch
    odd = odd_ref[0]
    fetch = Fetcher(sems, odd)
    mplanes = 3 * planes

    def sources(block, first_chunk, plane):
        which, at = first_chunk

        def both(n):
            return tuple(ins[part * each + n] for part in block)

        a = both(which)
        parts = [(a, 0 if top else a[0].shape[1] - OVERLAP, at)]
        return parts if top else parts + [(both(2), 0, plane)]

    blocks = [(LOWER, lo), ((0, 0), own), (UPPER, hi)]
    copies = [[], [], []]
    for comp in range(3):
        plane = comp * planes
        for n, (block, buf) in enumerate(blocks):
            first_chunk = (0, plane) if comp < 2 else (1, 0)
            copies[n].append(fetch(sources(block, first_chunk, plane), buf, plane, planes))
    image_copies = [
        fetch(sources(block, (1, planes), mplanes), buf, mplanes, buf.shape[0] - mplanes)
        for block, buf in blocks
    ]
    line = Line(own.shape[-2])

    def image(z, r):
        if z < 0:
            return lo[mplanes, r]
        if z >= planes:
            return hi[mplanes, r]
        return own[mplanes + z, r]

    velocity(
        line, edge_ref, [(c, buf, 0) for c, (_, buf) in zip(copies, blocks)], image_copies, s_ref, v_ref, top
    )
    momentum = momentum_at(own, lo, hi, planes)
    start = 0 if top else 4

    def body(r, first):
        images = []
        for z in range(planes):
            new, img = advance(line, v_ref, momentum, image, z, r, first)
            for c in range(3):
                near_ref[c * planes + z, r - start] = new[c]
                far_ref[c * planes + z, r - start] = new[c]
            images.append(img)
        for n in range(2):
            low, high = images[n], images[planes - 2 + n]
            near_ref[mplanes + n, r - start] = jnp.where(odd == 1, low, high)
            far_ref[mplanes + n, r - start] = jnp.where(odd == 1, high, low)

    over_rows(body, start, own.shape[1] - 4, top)


def second_kernel(chunks, planes, rows, edge_ref, odd_ref, *refs):
    top = chunks == 1
    start, stop, given = rows
    ins, refs = refs[: 4 * chunks], refs[4 * chunks :]
    out_ref, m2_ref, i2_ref, own, lo, hi, s_ref, v_ref, sems = refs
    fetch = Fetcher(sems, odd_ref[0])
    mplanes = 3 * planes

    def sources(block, plane):
        parts = []
        for n in range(chunks):
            pair = tuple(ins[part * chunks + n] for part in block)
            parts.append((pair, pair[0].shape[1] - OVERLAP if n + 1 < chunks else 0, plane))
        return parts

    blocks = [((3, 2), lo), ((0, 0), own), ((2, 3), hi)]
    copies = [[], [], []]
    for comp in range(3):
        plane = comp * planes
        for n, (block, buf) in enumerate(blocks):
            copies[n].append(fetch(sources(block, plane), buf, plane, planes))
    image_copies = [
        fetch(sources(block, mplanes), buf, target, 2)
        for block, buf, target in (
            ((3, 2), lo, mplanes), ((1, 0), own, mplanes), ((0, 1), own, mplanes + 2), ((2, 3), hi, mplanes),
        )
    ]
    line = Line(own.shape[-2])

    def image(z, r):
        if z < 0:
            return lo[mplanes + 2 + z, r]
        if z >= planes:
            return hi[mplanes + z - planes, r]
        return own[mplanes + z, r]

    velocity(
        line, edge_ref, [(c, buf, 0) for c, (_, buf) in zip(copies, blocks)], image_copies, s_ref, v_ref, top
    )
    momentum = momentum_at(own, lo, hi, planes)

    def image_row(zs, r, first=False):
        for z in zs:
            i2_ref[z + 1, r - start + 1] = advance(line, v_ref, None, image, z, r, first)[1]

    def step(keep, r, first):
        for z in range(planes):
            new, img = advance(line, v_ref, momentum, image, z, r, first)
            for c in range(3):
                m2_ref[c * planes + z, r - start] = new[c]
                if keep:
                    out_ref[c * planes + z, r - start] = new[c]
            i2_ref[z + 1, r - start + 1] = img
            if keep:
                out_ref[3 * planes + z, r - start] = img
        image_row((-1, planes), r, first)

    if top:
        for z in range(planes):
            i2_ref[z + 1, 0] = jnp.zeros_like(i2_ref[z + 1, 0])
    else:
        image_row(range(planes), start - 1)
    over_rows(functools.partial(step, True), start, start + given, top)
    if start + given < stop:
        over_rows(functools.partial(step, False), start + given, stop, top)
    image_row(range(planes), stop)


def force_kernel(top, planes, t_start, odd_ref, m2_ref, i2_ref, t_ref, *refs):
    if top:
        out_ref, near_ref, far_ref, tail_ref, q_ref = refs
        lead = 0
    else:
        before_ref, out_ref, near_ref, far_ref, q_ref = refs
        lead = before_ref.shape[1]
        for n in range(3 * planes):
            for r in range(lead):
                q_ref[n, r] = before_ref[n, r]
    line = Line(m2_ref.shape[-2])

    def force(r, carry):
        for z in range(planes):
            img = i2_ref[z + 1, r + 1]
            half = 0.5 * (img - t_ref[z, t_start + r])
            ahead, behind = line.beside(img)
            slopes = (
                ahead - behind,
                i2_ref[z + 1, r + 2] - i2_ref[z + 1, r],
                i2_ref[z + 2, r + 1] - i2_ref[z, r + 1],
            )
            for c in range(3):
                at = c * planes + z
                q_ref[at, r + lead] = m2_ref[at, r] - half * slopes[c]
        return carry

    lax.fori_loop(0, m2_ref.shape[1], force, 0, unroll=UNROLL[3])
    size = q_ref.shape[1]
    if top:
        for n in range(3 * planes):
            for r in range(6):
                tail_ref[n, r] = q_ref[n, size - 6 + r]

    def body(n, carry):
        def store(r, row):
            out_ref[n, r if top else r - 3] = row

        smooth_rows(line, lambda r: q_ref[n, r], store, size, top)
        return carry

    lax.fori_loop(0, 3 * planes, body, 0)
    odd = odd_ref[0]

    def side(r, carry):
        for c in range(3):
            for n in range(planes - 1):
                at = c * planes + n
                near_ref[c * (planes - 1) + n, r] = out_ref[at + 1 - odd, r]
                far_ref[c * (planes - 1) + n, r] = out_ref[at + odd, r]
        return carry

    lax.fori_loop(0, out_ref.shape[1], side, 0)


def last_kernel(planes, odd_ref, s_ref, near_ref, far_ref, out_ref):
    side = planes - 1
    odd = odd_ref[0] == 1

    def body(r, carry):
        for c in range(3):
            near = [near_ref[c * side + z, r] for z in range(3)]
            far = [far_ref[c * side + z, r] for z in range(3)]
            stack = [jnp.where(odd, a, b) for a, b in zip(near, far)]
            stack += [s_ref[c * planes + z, r] for z in range(planes)]
            stack += [jnp.where(odd, b, a) for a, b in zip(near, far)]
            for z, plane in enumerate(smooth_planes(stack)):
                out_ref[c * planes + z, r] = plane
        return carry

    lax.fori_loop(0, s_ref.shape[1], body, 0)


ANY = pl.BlockSpec(memory_space=pl.ANY)


def call(kernel, specs, outs, scratch=(), copies=0, cost=0.0, inside=1 << 20):
    sizes = [4 * math.prod(o) for o in outs] * 2 + [4 * math.prod(o) for o in scratch]
    return pl.pallas_call(
        kernel,
        in_specs=specs,
        out_specs=[VMEM] * len(outs),
        out_shape=[jax.ShapeDtypeStruct(o, jnp.float32) for o in outs],
        scratch_shapes=[pltpu.VMEM(s, jnp.float32) for s in scratch]
        + ([pltpu.SemaphoreType.DMA((copies,))] if copies else []),
        compiler_params=pltpu.CompilerParams(vmem_limit_bytes=sum(sizes) + inside + (1 << 20)),
        cost_estimate=pl.CostEstimate(flops=0, transcendentals=0, bytes_accessed=int(cost * 3.3e6)),
    )


def shoot(momentum, template, target):
    planes, rows, width = template.shape
    cols = width // LANES
    halves = lax.axis_size("gy")
    count = lax.axis_size("gz") * halves
    flat = lax.axis_index("gz") * halves + lax.axis_index("gy")
    depth = 2 * (flat // 4) + flat % 2
    edge = jnp.stack([depth > 0, depth < count // 2 - 1]).astype(jnp.float32)
    flip = lax.axis_index("gy").reshape(1)
    swap, near, far = swap_pairs(count), beside_pairs(count, 0), beside_pairs(count, 1)
    odd = lax.axis_index("gy") == 1
    tail = (cols, LANES)
    all_planes = 4 * planes
    mplanes = 3 * planes

    def send(cells, pairs):
        return lax.ppermute(cells, AXES, pairs)

    mom, img, tgt = tiled(momentum), tiled(template), tiled(target)
    edge_rows = 2 * SUB * cols

    def border(cells):
        return jnp.where(
            lax.axis_index("gy") == 0, cells[..., -edge_rows:, :], cells[..., :edge_rows, :]
        )

    reach = 4 + 4 + 3
    total = [rows + reach, rows + reach - 4, rows + reach - 8, rows]
    cut = [13 * rows // 16]
    cut += [cut[0] - 4, cut[0] - 8, cut[0] - 11]

    edges = jnp.concatenate([border(mom), border(img)[None], border(tgt)[None]])
    halo = lax.ppermute(edges, "gy", [(0, 1), (1, 0)])

    def pack(comps, with_image, start, stop, ins, outs):
        return call(
            functools.partial(pack_kernel, start, stop, rows, comps, with_image),
            [SMEM] + [VMEM] * len(ins),
            [(len(comps) * planes + (planes if with_image else 0), stop - start) + tail] + outs,
            cost=2, inside=10 << 20,
        )(flip, *ins)

    (a0,) = pack((0, 1), False, 0, cut[0], (mom,), [])
    a0 = send(a0, swap)
    (a1,) = pack((2,), True, 0, cut[0], (mom, img), [])
    a1 = send(a1, swap)
    b0, t0 = pack((0, 1, 2), True, cut[0], total[0], (mom, img, tgt, halo), [(planes, total[2]) + tail])
    b0 = send(b0, swap)
    t0 = send(t0, swap)

    def exchange(to_near, to_far):
        return send(to_near, near), send(to_far, far)

    def with_side(chunk):
        own, low, high = chunk[:-planes], chunk[-planes : 1 - planes], chunk[-1:]
        return (
            jnp.concatenate([own, jnp.where(odd, low, high)]),
            jnp.concatenate([own, jnp.where(odd, high, low)]),
        )

    z_a = (a0, *exchange(a0, a0))
    z_a2 = (a1, *exchange(*with_side(a1)))
    z_b = (b0, *exchange(*with_side(b0)))

    def first(chunks, parts, size):
        give = size - 4 - (0 if chunks == 1 else 4)
        return call(
            functools.partial(first_kernel, chunks, planes),
            [SMEM] * 2 + [ANY] * (3 * chunks + 3),
            [(mplanes + 2, give) + tail] * 2,
            [(all_planes, size) + tail] + [(mplanes + 1, size) + tail] * 2
            + [(3, planes + 2, size + 1) + tail, (3, planes + 2, size) + tail],
            copies=13 * chunks, cost=9,
        )(edge, flip, *parts)

    near_a, far_a = first(1, [part for pair in zip(z_a, z_a2) for part in pair], cut[0])
    from_near_a, from_far_a = exchange(near_a, far_a)
    near_b, far_b = first(
        2, [part for pair in zip(z_a, z_a2, z_b) for part in pair], total[0] - cut[0] + OVERLAP
    )
    from_near_b, from_far_b = exchange(near_b, far_b)

    def second(chunks, parts, size, given):
        start, stop = (0 if chunks == 1 else 4), size - 4
        return call(
            functools.partial(second_kernel, chunks, planes, (start, stop, given)),
            [SMEM] * 2 + [ANY] * (4 * chunks),
            [(all_planes, given) + tail, (mplanes, stop - start) + tail, (planes + 2, stop - start + 2) + tail],
            [(all_planes, size) + tail] + [(mplanes + 2, size) + tail] * 2
            + [(3, planes + 2, size + 1) + tail, (3, planes + 2, size) + tail],
            copies=13 * chunks, cost=9,
        )(edge, flip, *parts)

    def force(m2, i2, t_start, before, sq_rows):
        outs = [(mplanes, sq_rows) + tail] + [(3 * (planes - 1), sq_rows) + tail] * 2 + ([] if before else [(mplanes, 6) + tail])
        lead = 6 if before else 0
        return call(
            functools.partial(force_kernel, not before, planes, t_start),
            [SMEM] + [VMEM] * (3 + len(before)), outs, [(mplanes, lead + m2.shape[1]) + tail],
            cost=3, inside=8 << 20,
        )(flip, m2, i2, t0, *before)

    out_a, m2_a, i2_a = second(1, (near_a, far_a, from_near_a, from_far_a), cut[1], cut[2])
    out_a = send(out_a, swap)
    sq_a, sqnear_a, sqfar_a, q_tail = force(m2_a, i2_a, 0, (), cut[3])
    from_a = exchange(sqnear_a, sqfar_a)
    out_b, m2_b, i2_b = second(
        2, (near_a, near_b, far_a, far_b, from_near_a, from_near_b, from_far_a, from_far_b),
        total[1] - cut[1] + OVERLAP, rows - cut[2],
    )
    out_b = send(out_b, swap)
    sq_b, sqnear_b, sqfar_b = force(m2_b, i2_b, cut[2], (q_tail,), rows - cut[3])
    from_b = exchange(sqnear_b, sqfar_b)

    def last(parts):
        return call(
            functools.partial(last_kernel, planes), [SMEM] + [VMEM] * 3, [(mplanes, parts[0].shape[1]) + tail],
            cost=2, inside=6 << 20,
        )(flip, *parts)[0]

    g_a = send(last((sq_a, *from_a)), swap)
    g_b = send(last((sq_b, *from_b)), swap)

    native = (rows * cols, LANES)
    m2, i2 = call(
        functools.partial(unpack_kernel, (cut[2], rows - cut[2]), ((0, 3), (mplanes, 1))),
        [SMEM, VMEM, VMEM], [(3, planes) + native, (planes,) + native], cost=2, inside=6 << 20,
    )(flip, out_a, out_b)
    (grad,) = call(
        functools.partial(unpack_kernel, (cut[3], rows - cut[3]), ((0, 3),)),
        [SMEM, VMEM, VMEM], [(3, planes) + native], cost=2, inside=6 << 20,
    )(flip, g_a, g_b)
    return untiled(m2, rows), untiled(i2, rows), untiled(grad, rows)


def solution(mesh):
    return jax.shard_map(
        shoot,
        mesh=mesh,
        in_specs=(
            P(None, ("groups", "gz"), "gy", None),
            P(("groups", "gz"), "gy", None),
            P(("groups", "gz"), "gy", None),
        ),
        out_specs=(
            P(None, ("groups", "gz"), "gy", None),
            P(("groups", "gz"), "gy", None),
            P(None, ("groups", "gz"), "gy", None),
        ),
        check_vma=False,
    )
```

```python
import functools
import math

import jax
import jax.numpy as jnp
from jax import lax
from jax.experimental import pallas as pl
from jax.experimental.pallas import tpu as pltpu
from jax.sharding import PartitionSpec as P

LANES = 128
SUB = 8

UNIT = 0.05
SCALE = UNIT * UNIT * UNIT
STEP_SIZE = 0.25
UNROLL = (4, 2, 1, 4)

AXES = ("gz", "gy")
VMEM = pl.BlockSpec(memory_space=pltpu.VMEM)
SMEM = pl.BlockSpec(memory_space=pltpu.SMEM)


def place(depth, half):
    return 4 * (depth // 2) + 2 * half + depth % 2


def swap_pairs(count):
    swapped = {1: 2, 2: 1}
    return [(i, 4 * (i // 4) + swapped.get(i % 4, i % 4)) for i in range(count)]


def beside_pairs(count, first):
    pairs = [
        (place(d, h), place(d + 1, h)) for h in range(2) for d in range(first, count // 2 - 1, 2)
    ]
    return pairs + [(b, a) for a, b in pairs]


def tiled(cells):
    lead, (rows, width) = cells.shape[:-2], cells.shape[-2:]
    cells = cells.reshape(lead + (rows // SUB, SUB, width // LANES, LANES))
    cells = jnp.swapaxes(cells, -2, -3)
    return cells.reshape(lead + (rows * width // LANES, LANES))


def untiled(cells, rows):
    lead, (total, lanes) = cells.shape[:-2], cells.shape[-2:]
    cols = total // rows
    cells = cells.reshape(lead + (rows // SUB, cols, SUB, LANES))
    cells = jnp.swapaxes(cells, -2, -3)
    return cells.reshape(lead + (rows, cols * LANES))


class Line:
    def __init__(self, cols):
        self.cols = cols
        lane = lax.broadcasted_iota(jnp.int32, (cols, LANES), 1)
        sub = lax.broadcasted_iota(jnp.int32, (cols, LANES), 0)
        self.first, self.last = sub == 0, sub == cols - 1
        self.at_start, self.near_start = lane == 0, lane < 2
        self.at_end, self.near_end = lane == LANES - 1, lane >= LANES - 2

    def beside(self, row):
        ahead = pltpu.roll(row, LANES - 1, 1)
        ahead = jnp.where(
            self.at_end, jnp.where(self.last, 0.0, pltpu.roll(ahead, self.cols - 1, 0)), ahead
        )
        behind = pltpu.roll(row, 1, 1)
        behind = jnp.where(
            self.at_start, jnp.where(self.first, 0.0, pltpu.roll(behind, 1, 0)), behind
        )
        return ahead, behind

    def smooth(self, row):
        ahead, behind = self.beside(row)
        mid = (ahead + behind) + (row + row)
        high = pltpu.roll(mid, LANES - 2, 1)
        high = jnp.where(
            self.near_end, jnp.where(self.last, ahead, pltpu.roll(high, self.cols - 1, 0)), high
        )
        low = pltpu.roll(mid, 2, 1)
        low = jnp.where(
            self.near_start, jnp.where(self.first, behind, pltpu.roll(low, 1, 0)), low
        )
        return 3.0 * mid + (low + high)


def smooth_rows(line, load, store, count, top):
    last = line.smooth(load(0))
    pairs = last if top else None
    sums = {-2: None, -1: last if top else None}
    for r in range(1, count):
        here = line.smooth(load(r))
        nxt = last + here
        sums[r - 1] = None if pairs is None else pairs + nxt
        last, pairs = here, nxt
        done = r - 3
        if done >= (0 if top else 3):
            out = 3.0 * sums[done] + sums[done + 2]
            store(done, out if sums[done - 2] is None else out + sums[done - 2])


def smooth_planes(planes, scale=SCALE):
    pairs = [a + b for a, b in zip(planes, planes[1:])]
    sums = [a + b for a, b in zip(pairs, pairs[1:])]
    out = [3.0 * mid + (low + high) for low, mid, high in zip(sums, sums[2:], sums[4:])]
    return out if scale == 1.0 else [scale * row for row in out]


def spot(row, cols):
    return (row // SUB) * SUB * cols + row % SUB


def mirrored(row, rows, cols, flip):
    a, b = spot(row, cols), spot(rows - 1 - row, cols)
    return a + flip * (b - a)


def pack_kernel(first, stop, rows, comps, with_image, flip_ref, m_ref, *refs):
    i_ref, t_ref, halo_ref, out_ref, tout_ref = {
        1: (None, None, None, *refs, None), 2: (refs[0], None, None, refs[-1], None)
    }.get(len(refs), refs)
    cols = out_ref.shape[-2]
    planes = m_ref.shape[1]
    flip = flip_ref[0]
    sign = (1 - 2 * flip).astype(jnp.float32)

    def copy(src, halo, dst, start, end, factor):
        for r in range(start, end):
            if r < rows:
                row = src[pl.ds(mirrored(r, rows, cols, flip), cols, stride=SUB), :]
            else:
                at = mirrored(r - rows, halo.shape[0] // cols, cols, flip)
                row = halo[pl.ds(at, cols, stride=SUB), :]
            dst[r - start] = row if factor is None else row * factor

    def halo_at(n, z):
        return None if halo_ref is None else halo_ref.at[n, z]

    def body(z, carry):
        for n, comp in enumerate(comps):
            copy(
                m_ref.at[comp, z], halo_at(comp, z), out_ref.at[n * planes + z], first, stop,
                sign if comp == 1 else None,
            )
        if with_image:
            at = len(comps) * planes + z
            copy(i_ref.at[z], halo_at(3, z), out_ref.at[at], first, stop, None)
        if t_ref is not None:
            copy(t_ref.at[z], halo_at(4, z), tout_ref.at[z], 0, tout_ref.shape[1], None)
        return carry

    lax.fori_loop(0, planes, body, 0)


def unpack_kernel(counts, parts, flip_ref, *refs):
    ins, outs = refs[: len(counts)], refs[len(counts) :]
    rows = sum(counts)
    flip = flip_ref[0]
    sign = (1 - 2 * flip).astype(jnp.float32)
    cols = ins[0].shape[-2]

    for out, (offset, components) in zip(outs, parts):
        planes = out.shape[-3]
        for comp in range(components):
            dst = out.at[comp] if len(out.shape) == 4 else out

            def body(z, carry, comp=comp, dst=dst, offset=offset, planes=planes):
                done = 0
                for ref, count in zip(ins, counts):
                    for r in range(count):
                        row = ref[offset + comp * planes + z, r]
                        at = mirrored(done + r, rows, cols, flip)
                        dst[z, pl.ds(at, cols, stride=SUB), :] = row * sign if comp == 1 else row
                    done += count
                return carry

            lax.fori_loop(0, planes, body, 0)


class Both:
    def __init__(self, copies):
        self.copies = copies

    def wait(self):
        for copy in self.copies:
            copy.wait()


class Fetcher:
    def __init__(self, sems, odd):
        self.sems, self.odd, self.used = sems, odd, 0

    def __call__(self, parts, buf, target, count):
        copies, row = [], 0
        for (even, odd), start, plane in parts:
            rows = even.shape[1] - start

            def copy_of(ref):
                return pltpu.make_async_copy(
                    ref.at[pl.ds(plane, count), pl.ds(start, rows)],
                    buf.at[pl.ds(target, count), pl.ds(row, rows)],
                    self.sems.at[self.used],
                )

            if even is odd:
                copy_of(even).start()
            else:
                pl.when(self.odd == 0)(lambda: copy_of(even).start())
                pl.when(self.odd == 1)(lambda: copy_of(odd).start())
            copies.append(copy_of(even))
            self.used += 1
            row += rows
        return Both(copies)


OVERLAP = 8


LOWER, UPPER = (2, 1), (1, 2)


def wait(copies):
    for copy in copies:
        copy.wait()


def velocity(line, edge_ref, blocks, image_copies, s_ref, v_ref, top):
    planes = v_ref.shape[1] - 2
    count = blocks[0][1].shape[1]
    zero = jnp.zeros(v_ref.shape[-2:], jnp.float32)

    for comp in range(3):
        for copies, _, _ in blocks:
            copies[comp].wait()

        def rows(r, carry, comp=comp):
            last, pairs = carry
            stack = [ref[offset + comp * planes + z, r] for _, ref, offset in blocks for z in range(planes)]
            here = smooth_planes(stack[planes - 4 : 2 * planes + 4], 1.0)
            nxt = [a + b for a, b in zip(last, here)]
            for z in range(planes + 2):
                s_ref[comp, z, r + 1] = pairs[z] + nxt[z]
            return here, nxt

        empty = [zero] * (planes + 2)
        lax.fori_loop(0, count, rows, (empty, empty), unroll=UNROLL[0])
        if top:
            for z in range(planes + 2):
                s_ref[comp, z, 0] = zero

    scales = [SCALE * edge_ref[0]] + [SCALE] * planes + [SCALE * edge_ref[1]]

    def finish(r, carry):
        for comp in range(3):
            for z in range(planes + 2):
                row = 3.0 * s_ref[comp, z, r + 2] + (s_ref[comp, z, r] + s_ref[comp, z, r + 4])
                v_ref[comp, z, r] = scales[z] * line.smooth(row)
        return carry

    lax.fori_loop(0 if top else 3, count - 3, finish, 0, unroll=UNROLL[1])
    wait(image_copies)


def change(speed, f, around):
    total = None
    for (rise, fall), (upper, lower) in zip(speed, around):
        up = rise * (f - lower if lower is not None else f)
        down = fall * (upper - f)
        total = up + down if total is None else total + (up + down)
    return total


def advance(line, v_ref, momentum, image, z, r, first):
    velo = [v_ref[c, z + 1, r] for c in range(3)]
    speed = [(jnp.maximum(v, 0.0), jnp.minimum(v, 0.0)) for v in velo]

    def around(load):
        mid = load(z, r)
        return mid, [
            line.beside(mid),
            (load(z, r + 1), None if first else load(z, r - 1)),
            (load(z + 1, r), load(z - 1, r)),
        ]

    new_image = None
    if image is not None:
        mid, sides = around(image)
        new_image = mid - STEP_SIZE * change(speed, mid, sides)
    if momentum is None:
        return None, new_image

    slopes = []
    for comp in range(3):
        ahead, behind = line.beside(velo[comp])
        slopes.append(
            (
                ahead - behind,
                v_ref[comp, z + 1, r + 1] - (0.0 if first else v_ref[comp, z + 1, r - 1]),
                v_ref[comp, z + 2, r] - v_ref[comp, z, r],
            )
        )
    divergence = slopes[0][0] + slopes[1][1] + slopes[2][2]
    fields = [around(load) for load in momentum]
    mids = [mid for mid, _ in fields]
    new = []
    for comp in range(3):
        mid, sides = fields[comp]
        stretch = mid * divergence
        for other in range(3):
            stretch = stretch + mids[other] * slopes[other][comp]
        moved = change(speed, mid, sides)
        new.append(mid - (STEP_SIZE * moved + (0.5 * STEP_SIZE) * stretch))
    return new, new_image


def over_rows(body, start, stop, top, unroll=1):
    if top and start == 0:
        body(0, True)
        start = 1

    def step(r, carry):
        body(r, False)
        return carry

    lax.fori_loop(start, stop, step, 0, unroll=unroll)


def momentum_at(own, lo, hi, planes):
    def at(comp):
        first = comp * planes

        def load(z, r):
            if z < 0:
                return lo[first + planes + z, r]
            if z >= planes:
                return hi[first + z - planes, r]
            return own[first + z, r]

        return load

    return [at(comp) for comp in range(3)]


def first_kernel(chunks, planes, edge_ref, odd_ref, *refs):
    top = chunks == 1
    each = chunks + 1
    ins, (near_ref, far_ref), scratch = refs[: 3 * each], refs[3 * each :][:2], refs[3 * each + 2 :]
    own, lo, hi, s_ref, v_ref, sems = scratch
    odd = odd_ref[0]
    fetch = Fetcher(sems, odd)
    mplanes = 3 * planes

    def sources(block, first_chunk, plane):
        which, at = first_chunk

        def both(n):
            return tuple(ins[part * each + n] for part in block)

        a = both(which)
        parts = [(a, 0 if top else a[0].shape[1] - OVERLAP, at)]
        return parts if top else parts + [(both(2), 0, plane)]

    blocks = [(LOWER, lo), ((0, 0), own), (UPPER, hi)]
    copies = [[], [], []]
    for comp in range(3):
        plane = comp * planes
        for n, (block, buf) in enumerate(blocks):
            first_chunk = (0, plane) if comp < 2 else (1, 0)
            copies[n].append(fetch(sources(block, first_chunk, plane), buf, plane, planes))
    image_copies = [
        fetch(sources(block, (1, planes), mplanes), buf, mplanes, buf.shape[0] - mplanes)
        for block, buf in blocks
    ]
    line = Line(own.shape[-2])

    def image(z, r):
        if z < 0:
            return lo[mplanes, r]
        if z >= planes:
            return hi[mplanes, r]
        return own[mplanes + z, r]

    velocity(
        line, edge_ref, [(c, buf, 0) for c, (_, buf) in zip(copies, blocks)], image_copies, s_ref, v_ref, top
    )
    momentum = momentum_at(own, lo, hi, planes)
    start = 0 if top else 4

    def body(r, first):
        images = []
        for z in range(planes):
            new, img = advance(line, v_ref, momentum, image, z, r, first)
            for c in range(3):
                near_ref[c * planes + z, r - start] = new[c]
                far_ref[c * planes + z, r - start] = new[c]
            images.append(img)
        for n in range(2):
            low, high = images[n], images[planes - 2 + n]
            near_ref[mplanes + n, r - start] = jnp.where(odd == 1, low, high)
            far_ref[mplanes + n, r - start] = jnp.where(odd == 1, high, low)

    over_rows(body, start, own.shape[1] - 4, top)


def second_kernel(chunks, planes, rows, edge_ref, odd_ref, *refs):
    top = chunks == 1
    start, stop, given = rows
    ins, refs = refs[: 4 * chunks], refs[4 * chunks :]
    out_ref, m2_ref, i2_ref, own, lo, hi, s_ref, v_ref, sems = refs
    fetch = Fetcher(sems, odd_ref[0])
    mplanes = 3 * planes

    def sources(block, plane):
        parts = []
        for n in range(chunks):
            pair = tuple(ins[part * chunks + n] for part in block)
            parts.append((pair, pair[0].shape[1] - OVERLAP if n + 1 < chunks else 0, plane))
        return parts

    blocks = [((3, 2), lo), ((0, 0), own), ((2, 3), hi)]
    copies = [[], [], []]
    for comp in range(3):
        plane = comp * planes
        for n, (block, buf) in enumerate(blocks):
            copies[n].append(fetch(sources(block, plane), buf, plane, planes))
    image_copies = [
        fetch(sources(block, mplanes), buf, target, 2)
        for block, buf, target in (
            ((3, 2), lo, mplanes), ((1, 0), own, mplanes), ((0, 1), own, mplanes + 2), ((2, 3), hi, mplanes),
        )
    ]
    line = Line(own.shape[-2])

    def image(z, r):
        if z < 0:
            return lo[mplanes + 2 + z, r]
        if z >= planes:
            return hi[mplanes + z - planes, r]
        return own[mplanes + z, r]

    velocity(
        line, edge_ref, [(c, buf, 0) for c, (_, buf) in zip(copies, blocks)], image_copies, s_ref, v_ref, top
    )
    momentum = momentum_at(own, lo, hi, planes)

    def image_row(zs, r, first=False):
        for z in zs:
            i2_ref[z + 1, r - start + 1] = advance(line, v_ref, None, image, z, r, first)[1]

    def step(keep, r, first):
        for z in range(planes):
            new, img = advance(line, v_ref, momentum, image, z, r, first)
            for c in range(3):
                m2_ref[c * planes + z, r - start] = new[c]
                if keep:
                    out_ref[c * planes + z, r - start] = new[c]
            i2_ref[z + 1, r - start + 1] = img
            if keep:
                out_ref[3 * planes + z, r - start] = img
        image_row((-1, planes), r, first)

    if top:
        for z in range(planes):
            i2_ref[z + 1, 0] = jnp.zeros_like(i2_ref[z + 1, 0])
    else:
        image_row(range(planes), start - 1)
    over_rows(functools.partial(step, True), start, start + given, top)
    if start + given < stop:
        over_rows(functools.partial(step, False), start + given, stop, top)
    image_row(range(planes), stop)


def force_kernel(top, planes, t_start, odd_ref, m2_ref, i2_ref, t_ref, *refs):
    t_copy = pltpu.make_async_copy(
        t_ref.at[:, pl.ds(t_start, m2_ref.shape[1])], refs[-2], refs[-1].at[0]
    )
    t_copy.start()
    if top:
        out_ref, near_ref, far_ref, tail_ref, q_ref, t_buf, sem = refs
        lead = 0
    else:
        before_ref, out_ref, near_ref, far_ref, q_ref, t_buf, sem = refs
        lead = before_ref.shape[1]
        for n in range(3 * planes):
            for r in range(lead):
                q_ref[n, r] = before_ref[n, r]
    line = Line(m2_ref.shape[-2])

    def slopes(r, carry):
        for z in range(planes):
            ahead, behind = line.beside(i2_ref[z + 1, r + 1])
            q_ref[z, r + lead] = ahead - behind
            q_ref[planes + z, r + lead] = i2_ref[z + 1, r + 2] - i2_ref[z + 1, r]
            q_ref[2 * planes + z, r + lead] = i2_ref[z + 2, r + 1] - i2_ref[z, r + 1]
        return carry

    lax.fori_loop(0, m2_ref.shape[1], slopes, 0, unroll=UNROLL[3])
    t_copy.wait()

    def force(r, carry):
        for z in range(planes):
            half = 0.5 * (i2_ref[z + 1, r + 1] - t_buf[z, r])
            for c in range(3):
                at = c * planes + z
                q_ref[at, r + lead] = m2_ref[at, r] - half * q_ref[at, r + lead]
        return carry

    lax.fori_loop(0, m2_ref.shape[1], force, 0, unroll=UNROLL[3])
    size = q_ref.shape[1]
    if top:
        for n in range(3 * planes):
            for r in range(6):
                tail_ref[n, r] = q_ref[n, size - 6 + r]

    def body(n, carry):
        def store(r, row):
            out_ref[n, r if top else r - 3] = row

        smooth_rows(line, lambda r: q_ref[n, r], store, size, top)
        return carry

    lax.fori_loop(0, 3 * planes, body, 0)
    odd = odd_ref[0]

    def side(r, carry):
        for c in range(3):
            for n in range(planes - 1):
                at = c * planes + n
                near_ref[c * (planes - 1) + n, r] = out_ref[at + 1 - odd, r]
                far_ref[c * (planes - 1) + n, r] = out_ref[at + odd, r]
        return carry

    lax.fori_loop(0, out_ref.shape[1], side, 0)


def last_kernel(planes, odd_ref, s_ref, near_ref, far_ref, out_ref):
    side = planes - 1
    odd = odd_ref[0] == 1

    def body(r, carry):
        for c in range(3):
            near = [near_ref[c * side + z, r] for z in range(3)]
            far = [far_ref[c * side + z, r] for z in range(3)]
            stack = [jnp.where(odd, a, b) for a, b in zip(near, far)]
            stack += [s_ref[c * planes + z, r] for z in range(planes)]
            stack += [jnp.where(odd, b, a) for a, b in zip(near, far)]
            for z, plane in enumerate(smooth_planes(stack)):
                out_ref[c * planes + z, r] = plane
        return carry

    lax.fori_loop(0, s_ref.shape[1], body, 0)


ANY = pl.BlockSpec(memory_space=pl.ANY)


def call(kernel, specs, outs, scratch=(), copies=0, cost=0.0, inside=1 << 20):
    sizes = [4 * math.prod(o) for o in outs] * 2 + [4 * math.prod(o) for o in scratch]
    return pl.pallas_call(
        kernel,
        in_specs=specs,
        out_specs=[VMEM] * len(outs),
        out_shape=[jax.ShapeDtypeStruct(o, jnp.float32) for o in outs],
        scratch_shapes=[pltpu.VMEM(s, jnp.float32) for s in scratch]
        + ([pltpu.SemaphoreType.DMA((copies,))] if copies else []),
        compiler_params=pltpu.CompilerParams(vmem_limit_bytes=sum(sizes) + inside + (1 << 20)),
        cost_estimate=pl.CostEstimate(flops=0, transcendentals=0, bytes_accessed=int(cost * 3.3e6)),
    )


def shoot(momentum, template, target):
    planes, rows, width = template.shape
    cols = width // LANES
    halves = lax.axis_size("gy")
    count = lax.axis_size("gz") * halves
    flat = lax.axis_index("gz") * halves + lax.axis_index("gy")
    depth = 2 * (flat // 4) + flat % 2
    edge = jnp.stack([depth > 0, depth < count // 2 - 1]).astype(jnp.float32)
    flip = lax.axis_index("gy").reshape(1)
    swap, near, far = swap_pairs(count), beside_pairs(count, 0), beside_pairs(count, 1)
    odd = lax.axis_index("gy") == 1
    tail = (cols, LANES)
    all_planes = 4 * planes
    mplanes = 3 * planes

    def send(cells, pairs):
        return lax.ppermute(cells, AXES, pairs)

    mom, img, tgt = tiled(momentum), tiled(template), tiled(target)
    edge_rows = 2 * SUB * cols

    def border(cells):
        return jnp.where(
            lax.axis_index("gy") == 0, cells[..., -edge_rows:, :], cells[..., :edge_rows, :]
        )

    reach = 4 + 4 + 3
    total = [rows + reach, rows + reach - 4, rows + reach - 8, rows]
    cut = [3 * rows // 4]
    cut += [cut[0] - 4, cut[0] - 8, cut[0] - 11]

    edges = jnp.concatenate([border(mom), border(img)[None], border(tgt)[None]])
    halo = lax.ppermute(edges, "gy", [(0, 1), (1, 0)])

    def pack(comps, with_image, start, stop, ins, outs):
        return call(
            functools.partial(pack_kernel, start, stop, rows, comps, with_image),
            [SMEM] + [VMEM] * len(ins),
            [(len(comps) * planes + (planes if with_image else 0), stop - start) + tail] + outs,
            cost=2, inside=10 << 20,
        )(flip, *ins)

    (a0,) = pack((0, 1), False, 0, cut[0], (mom,), [])
    a0 = send(a0, swap)
    (a1,) = pack((2,), True, 0, cut[0], (mom, img), [])
    a1 = send(a1, swap)
    b0, t0 = pack((0, 1, 2), True, cut[0], total[0], (mom, img, tgt, halo), [(planes, total[2]) + tail])
    b0 = send(b0, swap)
    t0 = send(t0, swap)

    def exchange(to_near, to_far):
        return send(to_near, near), send(to_far, far)

    def with_side(chunk):
        own, low, high = chunk[:-planes], chunk[-planes : 1 - planes], chunk[-1:]
        return (
            jnp.concatenate([own, jnp.where(odd, low, high)]),
            jnp.concatenate([own, jnp.where(odd, high, low)]),
        )

    z_a = (a0, *exchange(a0, a0))
    z_a2 = (a1, *exchange(*with_side(a1)))
    z_b = (b0, *exchange(*with_side(b0)))

    def first(chunks, parts, size):
        give = size - 4 - (0 if chunks == 1 else 4)
        return call(
            functools.partial(first_kernel, chunks, planes),
            [SMEM] * 2 + [ANY] * (3 * chunks + 3),
            [(mplanes + 2, give) + tail] * 2,
            [(all_planes, size) + tail] + [(mplanes + 1, size) + tail] * 2
            + [(3, planes + 2, size + 1) + tail, (3, planes + 2, size) + tail],
            copies=13 * chunks, cost=9,
        )(edge, flip, *parts)

    near_a, far_a = first(1, [part for pair in zip(z_a, z_a2) for part in pair], cut[0])
    from_near_a, from_far_a = exchange(near_a, far_a)
    near_b, far_b = first(
        2, [part for pair in zip(z_a, z_a2, z_b) for part in pair], total[0] - cut[0] + OVERLAP
    )
    from_near_b, from_far_b = exchange(near_b, far_b)

    def second(chunks, parts, size, given):
        start, stop = (0 if chunks == 1 else 4), size - 4
        return call(
            functools.partial(second_kernel, chunks, planes, (start, stop, given)),
            [SMEM] * 2 + [ANY] * (4 * chunks),
            [(all_planes, given) + tail, (mplanes, stop - start) + tail, (planes + 2, stop - start + 2) + tail],
            [(all_planes, size) + tail] + [(mplanes + 2, size) + tail] * 2
            + [(3, planes + 2, size + 1) + tail, (3, planes + 2, size) + tail],
            copies=13 * chunks, cost=9,
        )(edge, flip, *parts)

    def force(m2, i2, t_start, before, sq_rows):
        outs = [(mplanes, sq_rows) + tail] + [(3 * (planes - 1), sq_rows) + tail] * 2 + ([] if before else [(mplanes, 6) + tail])
        lead = 6 if before else 0
        return call(
            functools.partial(force_kernel, not before, planes, t_start),
            [SMEM, VMEM, VMEM, ANY] + [VMEM] * len(before), outs,
            [(mplanes, lead + m2.shape[1]) + tail, (planes, m2.shape[1]) + tail],
            copies=1, cost=3, inside=8 << 20,
        )(flip, m2, i2, t0, *before)

    out_a, m2_a, i2_a = second(1, (near_a, far_a, from_near_a, from_far_a), cut[1], cut[2])
    out_a = send(out_a, swap)
    sq_a, sqnear_a, sqfar_a, q_tail = force(m2_a, i2_a, 0, (), cut[3])
    from_a = exchange(sqnear_a, sqfar_a)
    out_b, m2_b, i2_b = second(
        2, (near_a, near_b, far_a, far_b, from_near_a, from_near_b, from_far_a, from_far_b),
        total[1] - cut[1] + OVERLAP, rows - cut[2],
    )
    out_b = send(out_b, swap)
    sq_b, sqnear_b, sqfar_b = force(m2_b, i2_b, cut[2], (q_tail,), rows - cut[3])
    from_b = exchange(sqnear_b, sqfar_b)

    def last(parts):
        return call(
            functools.partial(last_kernel, planes), [SMEM] + [VMEM] * 3, [(mplanes, parts[0].shape[1]) + tail],
            cost=2, inside=6 << 20,
        )(flip, *parts)[0]

    g_a = send(last((sq_a, *from_a)), swap)
    g_b = send(last((sq_b, *from_b)), swap)

    native = (rows * cols, LANES)
    m2, i2 = call(
        functools.partial(unpack_kernel, (cut[2], rows - cut[2]), ((0, 3), (mplanes, 1))),
        [SMEM, VMEM, VMEM], [(3, planes) + native, (planes,) + native], cost=2, inside=6 << 20,
    )(flip, out_a, out_b)
    (grad,) = call(
        functools.partial(unpack_kernel, (cut[3], rows - cut[3]), ((0, 3),)),
        [SMEM, VMEM, VMEM], [(3, planes) + native], cost=2, inside=6 << 20,
    )(flip, g_a, g_b)
    return untiled(m2, rows), untiled(i2, rows), untiled(grad, rows)


def solution(mesh):
    return jax.shard_map(
        shoot,
        mesh=mesh,
        in_specs=(
            P(None, ("groups", "gz"), "gy", None),
            P(("groups", "gz"), "gy", None),
            P(("groups", "gz"), "gy", None),
        ),
        out_specs=(
            P(None, ("groups", "gz"), "gy", None),
            P(("groups", "gz"), "gy", None),
            P(None, ("groups", "gz"), "gy", None),
        ),
        check_vma=False,
    )
```

```python
import functools
import math

import jax
import jax.numpy as jnp
from jax import lax
from jax.experimental import pallas as pl
from jax.experimental.pallas import tpu as pltpu
from jax.sharding import PartitionSpec as P

LANES = 128
SUB = 8

UNIT = 0.05
SCALE = UNIT * UNIT * UNIT
STEP_SIZE = 0.25
UNROLL = (4, 2, 1, 4)

AXES = ("gz", "gy")
VMEM = pl.BlockSpec(memory_space=pltpu.VMEM)
SMEM = pl.BlockSpec(memory_space=pltpu.SMEM)


def place(depth, half):
    return 4 * (depth // 2) + 2 * half + depth % 2


def swap_pairs(count):
    swapped = {1: 2, 2: 1}
    return [(i, 4 * (i // 4) + swapped.get(i % 4, i % 4)) for i in range(count)]


def beside_pairs(count, first):
    pairs = [
        (place(d, h), place(d + 1, h)) for h in range(2) for d in range(first, count // 2 - 1, 2)
    ]
    return pairs + [(b, a) for a, b in pairs]


def tiled(cells):
    lead, (rows, width) = cells.shape[:-2], cells.shape[-2:]
    cells = cells.reshape(lead + (rows // SUB, SUB, width // LANES, LANES))
    cells = jnp.swapaxes(cells, -2, -3)
    return cells.reshape(lead + (rows * width // LANES, LANES))


def untiled(cells, rows):
    lead, (total, lanes) = cells.shape[:-2], cells.shape[-2:]
    cols = total // rows
    cells = cells.reshape(lead + (rows // SUB, cols, SUB, LANES))
    cells = jnp.swapaxes(cells, -2, -3)
    return cells.reshape(lead + (rows, cols * LANES))


class Line:
    def __init__(self, cols):
        self.cols = cols
        lane = lax.broadcasted_iota(jnp.int32, (cols, LANES), 1)
        sub = lax.broadcasted_iota(jnp.int32, (cols, LANES), 0)
        self.first, self.last = sub == 0, sub == cols - 1
        self.at_start, self.near_start = lane == 0, lane < 2
        self.at_end, self.near_end = lane == LANES - 1, lane >= LANES - 2

    def beside(self, row):
        ahead = pltpu.roll(row, LANES - 1, 1)
        ahead = jnp.where(
            self.at_end, jnp.where(self.last, 0.0, pltpu.roll(ahead, self.cols - 1, 0)), ahead
        )
        behind = pltpu.roll(row, 1, 1)
        behind = jnp.where(
            self.at_start, jnp.where(self.first, 0.0, pltpu.roll(behind, 1, 0)), behind
        )
        return ahead, behind

    def smooth(self, row):
        ahead, behind = self.beside(row)
        mid = (ahead + behind) + (row + row)
        high = pltpu.roll(mid, LANES - 2, 1)
        high = jnp.where(
            self.near_end, jnp.where(self.last, ahead, pltpu.roll(high, self.cols - 1, 0)), high
        )
        low = pltpu.roll(mid, 2, 1)
        low = jnp.where(
            self.near_start, jnp.where(self.first, behind, pltpu.roll(low, 1, 0)), low
        )
        return 3.0 * mid + (low + high)


def smooth_rows(line, load, store, count, top):
    last = line.smooth(load(0))
    pairs = last if top else None
    sums = {-2: None, -1: last if top else None}
    for r in range(1, count):
        here = line.smooth(load(r))
        nxt = last + here
        sums[r - 1] = None if pairs is None else pairs + nxt
        last, pairs = here, nxt
        done = r - 3
        if done >= (0 if top else 3):
            out = 3.0 * sums[done] + sums[done + 2]
            store(done, out if sums[done - 2] is None else out + sums[done - 2])


def smooth_planes(planes, scale=SCALE):
    pairs = [a + b for a, b in zip(planes, planes[1:])]
    sums = [a + b for a, b in zip(pairs, pairs[1:])]
    out = [3.0 * mid + (low + high) for low, mid, high in zip(sums, sums[2:], sums[4:])]
    return out if scale == 1.0 else [scale * row for row in out]


def spot(row, cols):
    return (row // SUB) * SUB * cols + row % SUB


def mirrored(row, rows, cols, flip):
    a, b = spot(row, cols), spot(rows - 1 - row, cols)
    return a + flip * (b - a)


def pack_kernel(first, stop, rows, comps, with_image, flip_ref, m_ref, *refs):
    i_ref, t_ref, halo_ref, out_ref, tout_ref = {
        1: (None, None, None, *refs, None), 2: (refs[0], None, None, refs[-1], None)
    }.get(len(refs), refs)
    cols = out_ref.shape[-2]
    planes = m_ref.shape[1]
    flip = flip_ref[0]
    sign = (1 - 2 * flip).astype(jnp.float32)

    def copy(src, halo, dst, start, end, factor):
        for r in range(start, end):
            if r < rows:
                row = src[pl.ds(mirrored(r, rows, cols, flip), cols, stride=SUB), :]
            else:
                at = mirrored(r - rows, halo.shape[0] // cols, cols, flip)
                row = halo[pl.ds(at, cols, stride=SUB), :]
            dst[r - start] = row if factor is None else row * factor

    def halo_at(n, z):
        return None if halo_ref is None else halo_ref.at[n, z]

    def body(z, carry):
        for n, comp in enumerate(comps):
            copy(
                m_ref.at[comp, z], halo_at(comp, z), out_ref.at[n * planes + z], first, stop,
                sign if comp == 1 else None,
            )
        if with_image:
            at = len(comps) * planes + z
            copy(i_ref.at[z], halo_at(3, z), out_ref.at[at], first, stop, None)
        if t_ref is not None:
            copy(t_ref.at[z], halo_at(4, z), tout_ref.at[z], 0, tout_ref.shape[1], None)
        return carry

    lax.fori_loop(0, planes, body, 0)


def pack_first_kernel(stop, rows, flip_ref, m_ref, out_ref, buf, sems):
    cols = out_ref.shape[-2]
    comps, planes, size = buf.shape[:3]
    flip = flip_ref[0]
    sign = (1 - 2 * flip).astype(jnp.float32)
    held = size // cols
    first = pl.multiple_of(flip * (rows - held) * cols, SUB * cols)
    copies = [
        pltpu.make_async_copy(m_ref.at[comp, :, pl.ds(first, size)], buf.at[comp], sems.at[comp])
        for comp in range(comps)
    ]
    for copy in copies:
        copy.start()
    for comp in range(comps):
        copies[comp].wait()

        def body(z, carry, comp=comp):
            for r in range(stop):
                row = buf[comp, z, pl.ds(mirrored(r, held, cols, flip), cols, stride=SUB), :]
                out_ref[comp * planes + z, r] = row * sign if comp == 1 else row
            return carry

        lax.fori_loop(0, planes, body, 0)


def unpack_kernel(counts, parts, flip_ref, *refs):
    ins, outs = refs[: len(counts)], refs[len(counts) :]
    rows = sum(counts)
    flip = flip_ref[0]
    sign = (1 - 2 * flip).astype(jnp.float32)
    cols = ins[0].shape[-2]

    for out, (offset, components) in zip(outs, parts):
        planes = out.shape[-3]
        for comp in range(components):
            dst = out.at[comp] if len(out.shape) == 4 else out

            def body(z, carry, comp=comp, dst=dst, offset=offset, planes=planes):
                done = 0
                for ref, count in zip(ins, counts):
                    for r in range(count):
                        row = ref[offset + comp * planes + z, r]
                        at = mirrored(done + r, rows, cols, flip)
                        dst[z, pl.ds(at, cols, stride=SUB), :] = row * sign if comp == 1 else row
                    done += count
                return carry

            lax.fori_loop(0, planes, body, 0)


class Both:
    def __init__(self, copies):
        self.copies = copies

    def wait(self):
        for copy in self.copies:
            copy.wait()


class Fetcher:
    def __init__(self, sems, odd):
        self.sems, self.odd, self.used = sems, odd, 0

    def __call__(self, parts, buf, target, count):
        copies, row = [], 0
        for (even, odd), start, plane in parts:
            rows = even.shape[1] - start

            def copy_of(ref):
                return pltpu.make_async_copy(
                    ref.at[pl.ds(plane, count), pl.ds(start, rows)],
                    buf.at[pl.ds(target, count), pl.ds(row, rows)],
                    self.sems.at[self.used],
                )

            if even is odd:
                copy_of(even).start()
            else:
                pl.when(self.odd == 0)(lambda: copy_of(even).start())
                pl.when(self.odd == 1)(lambda: copy_of(odd).start())
            copies.append(copy_of(even))
            self.used += 1
            row += rows
        return Both(copies)


OVERLAP = 8


LOWER, UPPER = (2, 1), (1, 2)


def wait(copies):
    for copy in copies:
        copy.wait()


def velocity(line, edge_ref, blocks, image_copies, s_ref, v_ref, top):
    planes = v_ref.shape[1] - 2
    count = blocks[0][1].shape[1]
    zero = jnp.zeros(v_ref.shape[-2:], jnp.float32)

    for comp in range(3):
        for copies, _, _ in blocks:
            copies[comp].wait()

        def rows(r, carry, comp=comp):
            last, pairs = carry
            stack = [ref[offset + comp * planes + z, r] for _, ref, offset in blocks for z in range(planes)]
            here = smooth_planes(stack[planes - 4 : 2 * planes + 4], 1.0)
            nxt = [a + b for a, b in zip(last, here)]
            for z in range(planes + 2):
                s_ref[comp, z, r + 1] = pairs[z] + nxt[z]
            return here, nxt

        empty = [zero] * (planes + 2)
        lax.fori_loop(0, count, rows, (empty, empty), unroll=UNROLL[0])
        if top:
            for z in range(planes + 2):
                s_ref[comp, z, 0] = zero

    scales = [SCALE * edge_ref[0]] + [SCALE] * planes + [SCALE * edge_ref[1]]

    def finish(r, carry):
        for comp in range(3):
            for z in range(planes + 2):
                row = 3.0 * s_ref[comp, z, r + 2] + (s_ref[comp, z, r] + s_ref[comp, z, r + 4])
                v_ref[comp, z, r] = scales[z] * line.smooth(row)
        return carry

    lax.fori_loop(0 if top else 3, count - 3, finish, 0, unroll=UNROLL[1])
    wait(image_copies)


def change(speed, f, around):
    total = None
    for (rise, fall), (upper, lower) in zip(speed, around):
        up = rise * (f - lower if lower is not None else f)
        down = fall * (upper - f)
        total = up + down if total is None else total + (up + down)
    return total


def advance(line, v_ref, momentum, image, z, r, first):
    velo = [v_ref[c, z + 1, r] for c in range(3)]
    speed = [(jnp.maximum(v, 0.0), jnp.minimum(v, 0.0)) for v in velo]

    def around(load):
        mid = load(z, r)
        return mid, [
            line.beside(mid),
            (load(z, r + 1), None if first else load(z, r - 1)),
            (load(z + 1, r), load(z - 1, r)),
        ]

    new_image = None
    if image is not None:
        mid, sides = around(image)
        new_image = mid - STEP_SIZE * change(speed, mid, sides)
    if momentum is None:
        return None, new_image

    slopes = []
    for comp in range(3):
        ahead, behind = line.beside(velo[comp])
        slopes.append(
            (
                ahead - behind,
                v_ref[comp, z + 1, r + 1] - (0.0 if first else v_ref[comp, z + 1, r - 1]),
                v_ref[comp, z + 2, r] - v_ref[comp, z, r],
            )
        )
    divergence = slopes[0][0] + slopes[1][1] + slopes[2][2]
    fields = [around(load) for load in momentum]
    mids = [mid for mid, _ in fields]
    new = []
    for comp in range(3):
        mid, sides = fields[comp]
        stretch = mid * divergence
        for other in range(3):
            stretch = stretch + mids[other] * slopes[other][comp]
        moved = change(speed, mid, sides)
        new.append(mid - (STEP_SIZE * moved + (0.5 * STEP_SIZE) * stretch))
    return new, new_image


def over_rows(body, start, stop, top, unroll=1):
    if top and start == 0:
        body(0, True)
        start = 1

    def step(r, carry):
        body(r, False)
        return carry

    lax.fori_loop(start, stop, step, 0, unroll=unroll)


def momentum_at(own, lo, hi, planes):
    def at(comp):
        first = comp * planes

        def load(z, r):
            if z < 0:
                return lo[first + planes + z, r]
            if z >= planes:
                return hi[first + z - planes, r]
            return own[first + z, r]

        return load

    return [at(comp) for comp in range(3)]


def first_kernel(chunks, planes, edge_ref, odd_ref, *refs):
    top = chunks == 1
    each = chunks + 1
    ins, (near_ref, far_ref), scratch = refs[: 3 * each], refs[3 * each :][:2], refs[3 * each + 2 :]
    own, lo, hi, s_ref, v_ref, sems = scratch
    odd = odd_ref[0]
    fetch = Fetcher(sems, odd)
    mplanes = 3 * planes

    def sources(block, first_chunk, plane):
        which, at = first_chunk

        def both(n):
            return tuple(ins[part * each + n] for part in block)

        a = both(which)
        parts = [(a, 0 if top else a[0].shape[1] - OVERLAP, at)]
        return parts if top else parts + [(both(2), 0, plane)]

    blocks = [(LOWER, lo), ((0, 0), own), (UPPER, hi)]
    copies = [[], [], []]
    for comp in range(3):
        plane = comp * planes
        for n, (block, buf) in enumerate(blocks):
            first_chunk = (0, plane) if comp < 2 else (1, 0)
            copies[n].append(fetch(sources(block, first_chunk, plane), buf, plane, planes))
    image_copies = [
        fetch(sources(block, (1, planes), mplanes), buf, mplanes, buf.shape[0] - mplanes)
        for block, buf in blocks
    ]
    line = Line(own.shape[-2])

    def image(z, r):
        if z < 0:
            return lo[mplanes, r]
        if z >= planes:
            return hi[mplanes, r]
        return own[mplanes + z, r]

    velocity(
        line, edge_ref, [(c, buf, 0) for c, (_, buf) in zip(copies, blocks)], image_copies, s_ref, v_ref, top
    )
    momentum = momentum_at(own, lo, hi, planes)
    start = 0 if top else 4

    def body(r, first):
        images = []
        for z in range(planes):
            new, img = advance(line, v_ref, momentum, image, z, r, first)
            for c in range(3):
                near_ref[c * planes + z, r - start] = new[c]
                far_ref[c * planes + z, r - start] = new[c]
            images.append(img)
        for n in range(2):
            low, high = images[n], images[planes - 2 + n]
            near_ref[mplanes + n, r - start] = jnp.where(odd == 1, low, high)
            far_ref[mplanes + n, r - start] = jnp.where(odd == 1, high, low)

    over_rows(body, start, own.shape[1] - 4, top)


def second_kernel(chunks, planes, rows, edge_ref, odd_ref, *refs):
    top = chunks == 1
    start, stop, given = rows
    ins, refs = refs[: 4 * chunks], refs[4 * chunks :]
    out_ref, m2_ref, i2_ref, own, lo, hi, s_ref, v_ref, sems = refs
    fetch = Fetcher(sems, odd_ref[0])
    mplanes = 3 * planes

    def sources(block, plane):
        parts = []
        for n in range(chunks):
            pair = tuple(ins[part * chunks + n] for part in block)
            parts.append((pair, pair[0].shape[1] - OVERLAP if n + 1 < chunks else 0, plane))
        return parts

    blocks = [((3, 2), lo), ((0, 0), own), ((2, 3), hi)]
    copies = [[], [], []]
    for comp in range(3):
        plane = comp * planes
        for n, (block, buf) in enumerate(blocks):
            copies[n].append(fetch(sources(block, plane), buf, plane, planes))
    image_copies = [
        fetch(sources(block, mplanes), buf, target, 2)
        for block, buf, target in (
            ((3, 2), lo, mplanes), ((1, 0), own, mplanes), ((0, 1), own, mplanes + 2), ((2, 3), hi, mplanes),
        )
    ]
    line = Line(own.shape[-2])

    def image(z, r):
        if z < 0:
            return lo[mplanes + 2 + z, r]
        if z >= planes:
            return hi[mplanes + z - planes, r]
        return own[mplanes + z, r]

    velocity(
        line, edge_ref, [(c, buf, 0) for c, (_, buf) in zip(copies, blocks)], image_copies, s_ref, v_ref, top
    )
    momentum = momentum_at(own, lo, hi, planes)

    def image_row(zs, r, first=False):
        for z in zs:
            i2_ref[z + 1, r - start + 1] = advance(line, v_ref, None, image, z, r, first)[1]

    def step(keep, r, first):
        for z in range(planes):
            new, img = advance(line, v_ref, momentum, image, z, r, first)
            for c in range(3):
                m2_ref[c * planes + z, r - start] = new[c]
                if keep:
                    out_ref[c * planes + z, r - start] = new[c]
            i2_ref[z + 1, r - start + 1] = img
            if keep:
                out_ref[3 * planes + z, r - start] = img
        image_row((-1, planes), r, first)

    if top:
        for z in range(planes):
            i2_ref[z + 1, 0] = jnp.zeros_like(i2_ref[z + 1, 0])
    else:
        image_row(range(planes), start - 1)
    over_rows(functools.partial(step, True), start, start + given, top)
    if start + given < stop:
        over_rows(functools.partial(step, False), start + given, stop, top)
    image_row(range(planes), stop)


def force_kernel(top, planes, t_start, odd_ref, m2_ref, i2_ref, t_ref, *refs):
    t_copy = pltpu.make_async_copy(
        t_ref.at[:, pl.ds(t_start, m2_ref.shape[1])], refs[-2], refs[-1].at[0]
    )
    t_copy.start()
    if top:
        out_ref, near_ref, far_ref, tail_ref, q_ref, t_buf, sem = refs
        lead = 0
    else:
        before_ref, out_ref, near_ref, far_ref, q_ref, t_buf, sem = refs
        lead = before_ref.shape[1]
        for n in range(3 * planes):
            for r in range(lead):
                q_ref[n, r] = before_ref[n, r]
    line = Line(m2_ref.shape[-2])

    def slopes(r, carry):
        for z in range(planes):
            ahead, behind = line.beside(i2_ref[z + 1, r + 1])
            q_ref[z, r + lead] = ahead - behind
            q_ref[planes + z, r + lead] = i2_ref[z + 1, r + 2] - i2_ref[z + 1, r]
            q_ref[2 * planes + z, r + lead] = i2_ref[z + 2, r + 1] - i2_ref[z, r + 1]
        return carry

    lax.fori_loop(0, m2_ref.shape[1], slopes, 0, unroll=UNROLL[3])
    t_copy.wait()

    def force(r, carry):
        for z in range(planes):
            half = 0.5 * (i2_ref[z + 1, r + 1] - t_buf[z, r])
            for c in range(3):
                at = c * planes + z
                q_ref[at, r + lead] = m2_ref[at, r] - half * q_ref[at, r + lead]
        return carry

    lax.fori_loop(0, m2_ref.shape[1], force, 0, unroll=UNROLL[3])
    size = q_ref.shape[1]
    if top:
        for n in range(3 * planes):
            for r in range(6):
                tail_ref[n, r] = q_ref[n, size - 6 + r]

    def body(n, carry):
        def store(r, row):
            out_ref[n, r if top else r - 3] = row

        smooth_rows(line, lambda r: q_ref[n, r], store, size, top)
        return carry

    lax.fori_loop(0, 3 * planes, body, 0)
    odd = odd_ref[0]

    def side(r, carry):
        for c in range(3):
            for n in range(planes - 1):
                at = c * planes + n
                near_ref[c * (planes - 1) + n, r] = out_ref[at + 1 - odd, r]
                far_ref[c * (planes - 1) + n, r] = out_ref[at + odd, r]
        return carry

    lax.fori_loop(0, out_ref.shape[1], side, 0)


def last_kernel(planes, odd_ref, s_ref, near_ref, far_ref, out_ref):
    side = planes - 1
    odd = odd_ref[0] == 1

    def body(r, carry):
        for c in range(3):
            near = [near_ref[c * side + z, r] for z in range(3)]
            far = [far_ref[c * side + z, r] for z in range(3)]
            stack = [jnp.where(odd, a, b) for a, b in zip(near, far)]
            stack += [s_ref[c * planes + z, r] for z in range(planes)]
            stack += [jnp.where(odd, b, a) for a, b in zip(near, far)]
            for z, plane in enumerate(smooth_planes(stack)):
                out_ref[c * planes + z, r] = plane
        return carry

    lax.fori_loop(0, s_ref.shape[1], body, 0)


ANY = pl.BlockSpec(memory_space=pl.ANY)


def call(kernel, specs, outs, scratch=(), copies=0, cost=0.0, inside=1 << 20):
    sizes = [4 * math.prod(o) for o in outs] * 2 + [4 * math.prod(o) for o in scratch]
    return pl.pallas_call(
        kernel,
        in_specs=specs,
        out_specs=[VMEM] * len(outs),
        out_shape=[jax.ShapeDtypeStruct(o, jnp.float32) for o in outs],
        scratch_shapes=[pltpu.VMEM(s, jnp.float32) for s in scratch]
        + ([pltpu.SemaphoreType.DMA((copies,))] if copies else []),
        compiler_params=pltpu.CompilerParams(vmem_limit_bytes=sum(sizes) + inside + (1 << 20)),
        cost_estimate=pl.CostEstimate(flops=0, transcendentals=0, bytes_accessed=int(cost * 3.3e6)),
    )


def shoot(momentum, template, target):
    planes, rows, width = template.shape
    cols = width // LANES
    halves = lax.axis_size("gy")
    count = lax.axis_size("gz") * halves
    flat = lax.axis_index("gz") * halves + lax.axis_index("gy")
    depth = 2 * (flat // 4) + flat % 2
    edge = jnp.stack([depth > 0, depth < count // 2 - 1]).astype(jnp.float32)
    flip = lax.axis_index("gy").reshape(1)
    swap, near, far = swap_pairs(count), beside_pairs(count, 0), beside_pairs(count, 1)
    odd = lax.axis_index("gy") == 1
    tail = (cols, LANES)
    all_planes = 4 * planes
    mplanes = 3 * planes

    def send(cells, pairs):
        return lax.ppermute(cells, AXES, pairs)

    mom, img, tgt = tiled(momentum), tiled(template), tiled(target)
    edge_rows = 2 * SUB * cols

    def border(cells):
        return jnp.where(
            lax.axis_index("gy") == 0, cells[..., -edge_rows:, :], cells[..., :edge_rows, :]
        )

    reach = 4 + 4 + 3
    total = [rows + reach, rows + reach - 4, rows + reach - 8, rows]
    cut = [13 * rows // 16]
    cut += [cut[0] - 4, cut[0] - 8, cut[0] - 11]

    edges = jnp.concatenate([border(mom), border(img)[None], border(tgt)[None]])
    halo = lax.ppermute(edges, "gy", [(0, 1), (1, 0)])

    def pack(comps, with_image, start, stop, ins, outs):
        return call(
            functools.partial(pack_kernel, start, stop, rows, comps, with_image),
            [SMEM] + [VMEM] * len(ins),
            [(len(comps) * planes + (planes if with_image else 0), stop - start) + tail] + outs,
            cost=2, inside=10 << 20,
        )(flip, *ins)

    held = -(-cut[0] // SUB) * SUB
    (a0,) = call(
        functools.partial(pack_first_kernel, cut[0], rows),
        [SMEM, ANY],
        [(2 * planes, cut[0]) + tail],
        [(2, planes, held * cols, LANES)],
        copies=2, cost=1, inside=56 << 20,
    )(flip, mom)
    a0 = send(a0, swap)
    (a1,) = pack((2,), True, 0, cut[0], (mom, img), [])
    a1 = send(a1, swap)
    b0, t0 = pack((0, 1, 2), True, cut[0], total[0], (mom, img, tgt, halo), [(planes, total[2]) + tail])
    b0 = send(b0, swap)
    t0 = send(t0, swap)

    def exchange(to_near, to_far):
        return send(to_near, near), send(to_far, far)

    def with_side(chunk):
        own, low, high = chunk[:-planes], chunk[-planes : 1 - planes], chunk[-1:]
        return (
            jnp.concatenate([own, jnp.where(odd, low, high)]),
            jnp.concatenate([own, jnp.where(odd, high, low)]),
        )

    z_a = (a0, *exchange(a0, a0))
    z_a2 = (a1, *exchange(*with_side(a1)))
    z_b = (b0, *exchange(*with_side(b0)))

    def first(chunks, parts, size):
        give = size - 4 - (0 if chunks == 1 else 4)
        return call(
            functools.partial(first_kernel, chunks, planes),
            [SMEM] * 2 + [ANY] * (3 * chunks + 3),
            [(mplanes + 2, give) + tail] * 2,
            [(all_planes, size) + tail] + [(mplanes + 1, size) + tail] * 2
            + [(3, planes + 2, size + 1) + tail, (3, planes + 2, size) + tail],
            copies=13 * chunks, cost=9,
        )(edge, flip, *parts)

    near_a, far_a = first(1, [part for pair in zip(z_a, z_a2) for part in pair], cut[0])
    from_near_a, from_far_a = exchange(near_a, far_a)
    near_b, far_b = first(
        2, [part for pair in zip(z_a, z_a2, z_b) for part in pair], total[0] - cut[0] + OVERLAP
    )
    from_near_b, from_far_b = exchange(near_b, far_b)

    def second(chunks, parts, size, given):
        start, stop = (0 if chunks == 1 else 4), size - 4
        return call(
            functools.partial(second_kernel, chunks, planes, (start, stop, given)),
            [SMEM] * 2 + [ANY] * (4 * chunks),
            [(all_planes, given) + tail, (mplanes, stop - start) + tail, (planes + 2, stop - start + 2) + tail],
            [(all_planes, size) + tail] + [(mplanes + 2, size) + tail] * 2
            + [(3, planes + 2, size + 1) + tail, (3, planes + 2, size) + tail],
            copies=13 * chunks, cost=9,
        )(edge, flip, *parts)

    def force(m2, i2, t_start, before, sq_rows):
        outs = [(mplanes, sq_rows) + tail] + [(3 * (planes - 1), sq_rows) + tail] * 2 + ([] if before else [(mplanes, 6) + tail])
        lead = 6 if before else 0
        return call(
            functools.partial(force_kernel, not before, planes, t_start),
            [SMEM, VMEM, VMEM, ANY] + [VMEM] * len(before), outs,
            [(mplanes, lead + m2.shape[1]) + tail, (planes, m2.shape[1]) + tail],
            copies=1, cost=3, inside=8 << 20,
        )(flip, m2, i2, t0, *before)

    out_a, m2_a, i2_a = second(1, (near_a, far_a, from_near_a, from_far_a), cut[1], cut[2])
    out_a = send(out_a, swap)
    sq_a, sqnear_a, sqfar_a, q_tail = force(m2_a, i2_a, 0, (), cut[3])
    from_a = exchange(sqnear_a, sqfar_a)
    out_b, m2_b, i2_b = second(
        2, (near_a, near_b, far_a, far_b, from_near_a, from_near_b, from_far_a, from_far_b),
        total[1] - cut[1] + OVERLAP, rows - cut[2],
    )
    out_b = send(out_b, swap)
    sq_b, sqnear_b, sqfar_b = force(m2_b, i2_b, cut[2], (q_tail,), rows - cut[3])
    from_b = exchange(sqnear_b, sqfar_b)

    def last(parts):
        return call(
            functools.partial(last_kernel, planes), [SMEM] + [VMEM] * 3, [(mplanes, parts[0].shape[1]) + tail],
            cost=2, inside=6 << 20,
        )(flip, *parts)[0]

    g_a = send(last((sq_a, *from_a)), swap)
    g_b = send(last((sq_b, *from_b)), swap)

    native = (rows * cols, LANES)
    m2, i2 = call(
        functools.partial(unpack_kernel, (cut[2], rows - cut[2]), ((0, 3), (mplanes, 1))),
        [SMEM, VMEM, VMEM], [(3, planes) + native, (planes,) + native], cost=2, inside=6 << 20,
    )(flip, out_a, out_b)
    (grad,) = call(
        functools.partial(unpack_kernel, (cut[3], rows - cut[3]), ((0, 3),)),
        [SMEM, VMEM, VMEM], [(3, planes) + native], cost=2, inside=6 << 20,
    )(flip, g_a, g_b)
    return untiled(m2, rows), untiled(i2, rows), untiled(grad, rows)


def solution(mesh):
    return jax.shard_map(
        shoot,
        mesh=mesh,
        in_specs=(
            P(None, ("groups", "gz"), "gy", None),
            P(("groups", "gz"), "gy", None),
            P(("groups", "gz"), "gy", None),
        ),
        out_specs=(
            P(None, ("groups", "gz"), "gy", None),
            P(("groups", "gz"), "gy", None),
            P(None, ("groups", "gz"), "gy", None),
        ),
        check_vma=False,
    )
```
